32 devices in a mesh: parts: 2 (over x), tm: 8 (over z, y), stn: 2 (over core).
Axes of the slice: x: 2, y: 2, z: 4, core: 2. Of those that a mesh axis runs over, the one named last changes fastest.
Arguments:
- voltages: bfloat16 [256, 2, 32, 2, 2048], P(('parts', 'stn'), None, 'tm'), parts along dimension 0, may hold values from -6 to 6
- filter_taps: float32 [16, 2048], replicated, may hold values from -1.5 to 1.5
- use_mask: int32 [512, 8], P('parts'), parts along dimension 0, may hold values 0 or 1
- block_index: int32 [512, 8], P('parts'), parts along dimension 0, may hold values from 0 to 127
- weight_blocks: bfloat16 [128, 512], P('tm'), may hold values from -0.5 to 0.5
Outputs:
- power: float32 [2048, 32, 512], P('stn', 'tm', 'parts'), parts along dimension 2
The draws below stay inside these ranges and needn't reach their ends.
There are 2 independent parts, one for each index of `parts`. The reference program is written for one: setup_inputs(seed, part) draws one part's arguments, and reference() takes and returns one part's arrays. A program takes and returns all parts, laid end to end along the dimension named above; an argument that names none is the same for every part. Nothing has to cross between parts.
All inputs are finite; a program needn't handle non-finite values.
Results may differ from the reference program's by a relative error of at most 0.008.
Values may be sent and summed in bfloat16 or wider, within the bound.
A program may use at most 192 MiB of HBM per device.

```python
import math
import jax
import jax.numpy as jnp
from jax import lax

C = 2048
P_SIZE = 64
Q = 32
BEAMS = 256
TAPS = 16
SB = 16
G = 16
S_DEV = 64
STATIONS = 128
FRAMES = 32
NB = 8
NWB = 128


def touch_ends(entries, own_key, low, largest):
    longest = entries.shape.index(max(entries.shape))
    spots = []
    for shift in (0, 1):
        where = [jax.random.randint(jax.random.fold_in(own_key, axis), (), 0, length) for axis, length in enumerate(entries.shape)]
        where[longest] = (where[longest] + shift) % entries.shape[longest]
        spots.append(tuple(where))
    return entries.at[spots[0]].set(low).at[spots[1]].set(largest)


def levels(own_key, dims, shards, smallest, top_value):
    level = 1.0
    for dim, shards_of in shards:
        heights = jax.random.uniform(jax.random.fold_in(jax.random.fold_in(own_key, 6), dim), (shards_of,), jnp.float32, smallest / len(shards), top_value / len(shards))
        level = level * jnp.repeat(jnp.exp(heights), dims[dim] // shards_of).reshape((-1,) + (1,) * (len(dims) - 1 - dim))
    return level


def bell_draw(rng, dims, deviation, most, pieces=(), kind=jnp.bfloat16):
    loudness = levels(rng, dims, pieces, -0.22, 0.18) if pieces else 1.0
    result = jax.random.normal(rng, dims, jnp.float32) * deviation * loudness
    return jnp.minimum(jnp.maximum(result, -most), most).astype(kind)


def setup_inputs(seed: int = 0, part: int = 0) -> dict:
    splits = jax.random.split(jax.random.key(seed), 6)
    part_keys = jax.random.split(jax.random.fold_in(splits[5], part), 6)
    voltages = bell_draw(part_keys[0], (STATIONS, 2, FRAMES, 2, C), 1.0, 6.0, ((0, 2), (2, 8)))
    filter_taps = bell_draw(splits[1], (TAPS, C), 0.25, 1.5, (), jnp.float32)
    use_mask = touch_ends((jax.random.randint(part_keys[2], (BEAMS, NB), 0, 2) < 1).astype(jnp.int32), jax.random.fold_in(part_keys[2], 1), 0, 1)
    block_index = touch_ends(jax.random.randint(part_keys[3], (BEAMS, NB), 0, NWB), jax.random.fold_in(part_keys[3], 1), 0, NWB - 1).astype(jnp.int32)
    weight_blocks = bell_draw(splits[4], (NWB, G * 2 * SB), (2 * S_DEV) ** -0.5, 0.5, ((0, 8),))
    return dict(voltages=voltages, filter_taps=filter_taps, use_mask=use_mask, block_index=block_index, weight_blocks=weight_blocks)


def transform_tables(first_size, second_size):
    full_size = first_size * second_size
    first_range = jnp.arange(first_size, dtype=jnp.int32)
    second_range = jnp.arange(second_size, dtype=jnp.int32)
    first_angle = (first_range[:, None] * first_range[None, :] % first_size).astype(jnp.float32) * (2.0 * math.pi / first_size)
    cosine_first = jnp.cos(first_angle)
    sine_first = jnp.sin(first_angle)
    section_one = jnp.stack([jnp.stack([cosine_first, -sine_first], axis=1), jnp.stack([sine_first, cosine_first], axis=1)], axis=0)
    second_angle = (second_range[:, None] * second_range[None, :] % second_size).astype(jnp.float32) * (2.0 * math.pi / second_size)
    cosine_second = jnp.cos(second_angle)
    sine_second = jnp.sin(second_angle)
    section_two = jnp.stack([jnp.stack([cosine_second, sine_second], axis=-1), jnp.stack([-sine_second, cosine_second], axis=-1)], axis=1)
    section_two = section_two.reshape(2 * second_size, 2 * second_size)
    twist_angle = (second_range[:, None] * first_range[None, :] % full_size).astype(jnp.float32) * (2.0 * math.pi / full_size)
    return (section_one.astype(jnp.bfloat16), jnp.cos(twist_angle), jnp.sin(twist_angle), section_two.astype(jnp.bfloat16))

def filter_frames(window, filter_taps, frame_count):
    history = filter_taps.shape[0] - 1
    shape_out = window.shape[:2] + (frame_count,) + window.shape[3:]
    summed = jnp.zeros(shape_out, jnp.float32)
    for tap_index in range(filter_taps.shape[0]):
        sliced = lax.slice_in_dim(window, history - tap_index, history - tap_index + frame_count, axis=2)
        summed = summed + filter_taps[tap_index] * sliced.astype(jnp.float32)
    return summed.astype(jnp.bfloat16)

def channelize(filtered, tables):
    section_one, twist_cos, twist_sin, section_two = tables
    first_size = section_one.shape[1]
    second_size = twist_cos.shape[0]
    station_count, frame_count = (filtered.shape[0], filtered.shape[2])
    reshaped = filtered.reshape(station_count, 2, frame_count, 2, first_size, second_size)
    first_section = jnp.einsum('spfrae,raob->spfeob', reshaped.astype(jnp.float32), section_one.astype(jnp.float32))
    real_part = first_section[:, :, :, :, 0, :]
    imag_part = first_section[:, :, :, :, 1, :]
    norm_factor = 1.0 / math.sqrt(first_size * second_size)
    twist_real = (real_part * twist_cos + imag_part * twist_sin) * norm_factor
    twist_imag = (imag_part * twist_cos - real_part * twist_sin) * norm_factor
    twiddled = jnp.stack([twist_real, twist_imag], axis=-2).astype(jnp.bfloat16)
    twiddled = twiddled.reshape(station_count, 2, frame_count, 2 * second_size, first_size)
    spectra = jnp.einsum('dk,spfkb->spfdb', section_two.astype(jnp.float32), twiddled.astype(jnp.float32))
    return spectra.astype(jnp.bfloat16).reshape(station_count, 2, frame_count, second_size, 2, first_size)

def beam_matrix(use_rows, picked):
    beam_count, block_count = use_rows.shape
    shaped = picked.reshape(beam_count, block_count, G, 2, SB) * use_rows.astype(jnp.bfloat16)[:, :, None, None, None]
    real_part = shaped[:, :, :, 0, :].transpose(2, 1, 3, 0).reshape(G, block_count * SB, beam_count)
    imag_part = shaped[:, :, :, 1, :].transpose(2, 1, 3, 0).reshape(G, block_count * SB, beam_count)
    upper_rows = jnp.stack([real_part, imag_part], axis=2)
    lower_rows = jnp.stack([-imag_part, real_part], axis=2)
    return jnp.stack([upper_rows, lower_rows], axis=1)

def form_beams(row_block, weights):
    row_count = row_block.shape[0]
    group_count = weights.shape[0]
    reshaped = row_block.reshape(group_count, -1, row_block.shape[2]).astype(jnp.float32)
    matrices = weights.reshape(group_count, row_block.shape[2], -1).astype(jnp.float32)
    product = jnp.einsum('gmk,gkn->gmn', reshaped, matrices)
    return product.reshape(row_count, -1)

def detect(summed):
    shaped = summed.reshape(summed.shape[0], 4, -1)
    return lax.optimization_barrier(jnp.sum(shaped * shaped, axis=1))

def reference(voltages, filter_taps, use_mask, block_index, weight_blocks):
    tables = transform_tables(P_SIZE, Q)
    history = TAPS - 1

    def per_station(station):
        window = jnp.pad(station[None], ((0, 0), (0, 0), (history, 0), (0, 0), (0, 0)))
        filtered = filter_frames(window, filter_taps, FRAMES)
        return channelize(filtered, tables)[0]
    spectra = lax.map(per_station, voltages)
    turned = spectra.transpose(2, 3, 5, 1, 4, 0).reshape(FRAMES, C, 2, 2, STATIONS)
    picked = weight_blocks[block_index]
    matrix = beam_matrix(use_mask, picked)
    member_count = STATIONS // S_DEV

    def per_frame(frame_rows):
        summed = jnp.zeros((C, 4 * BEAMS), jnp.float32)
        for member in range(member_count):
            low = member * S_DEV
            row_block = frame_rows[:, :, :, low:low + S_DEV].reshape(C, 2, 2 * S_DEV)
            weights = matrix[:, :, low:low + S_DEV]
            partial_value = form_beams(row_block, weights).astype(jnp.bfloat16)
            partial_value = lax.optimization_barrier(partial_value)
            summed = summed + partial_value.astype(jnp.float32)
        return detect(summed)
    detected = lax.map(per_frame, turned)
    return detected.transpose(1, 0, 2)
```

```python
import functools
import math

import jax
import jax.numpy as jnp
import numpy as np
from jax import lax
from jax.experimental import pallas as pl
from jax.experimental.pallas import tpu as pltpu
from jax.sharding import PartitionSpec as P

SB = 16
G = 16
LANES = 128
FIRST = 8
LAG = 2
MESH = pl.DeviceIdType.MESH


def transform_tables(channels):
    second = channels // FIRST
    parts = second // LANES
    a = np.arange(FIRST)
    l = np.arange(second)

    def waves(product, period):
        angle = (product % period).astype(np.float32) * np.float32(2.0 * math.pi / period)
        return np.cos(angle), np.sin(angle)

    cos, sin = waves(a[:, None] * a[None, :], FIRST)
    one = np.zeros((parts, 2, FIRST, 8, 8, FIRST, parts, 2), np.float32)
    for lh in range(parts):
        for s in range(8):
            one[lh, 0, :, s, s, :, lh, 0] = cos
            one[lh, 0, :, s, s, :, lh, 1] = sin
            one[lh, 1, :, s, s, :, lh, 0] = -sin
            one[lh, 1, :, s, s, :, lh, 1] = cos
    one = one.reshape(parts * 2 * FIRST * 8, 8 * FIRST * parts * 2)
    cos, sin = waves(l[:, None] * l[None, :], second)
    two = np.stack([np.stack([cos, -sin], axis=1), np.stack([sin, cos], axis=1)], axis=0)
    two = two.reshape(2, second, 2, 2, LANES).transpose(0, 1, 3, 2, 4).reshape(2 * second, 2 * second)
    cos, sin = waves(a[:, None] * l[None, :], channels)
    norm = np.float32(1.0 / math.sqrt(channels))
    cos, sin = (
        np.repeat((w * norm).reshape(FIRST, parts, LANES).swapaxes(0, 1), 8, axis=1) for w in (cos, sin))
    return jnp.asarray(one, jnp.bfloat16), jnp.asarray(two, jnp.bfloat16), jnp.asarray(cos), jnp.asarray(sin)


def kernel(size, v_ref, rows_ref, index_ref, mask_ref, taps_ref, one_ref, two_ref, cos_ref, sin_ref, out_ref,
           x, taps, held, tw, z, r, table, weights, turned, given, taken,
           local, send_w, recv_w, send_y, recv_y, send_l, recv_l, send_r, recv_r, send_z, recv_z, own_z, send_p, recv_p):
    me = lax.axis_index("tm")
    core = lax.axis_index("stn")
    col = me // 2
    y = lax.rem(me, 2)
    cols = size // 2
    frames = v_ref.shape[2]
    wide = 2 * frames
    depth = taps_ref.shape[0]
    base = depth - 1
    pols = v_ref.shape[1]
    share = v_ref.shape[0] // 2
    groups, _, beams2 = weights.shape
    beams = beams2 // 2
    lows = LANES // groups
    bf16 = jnp.bfloat16
    f32 = jnp.float32
    place = 2 * core + y

    barrier = pltpu.get_barrier_semaphore()
    for step in range(size):
        for side in range(2):
            if step or side:
                pl.semaphore_signal(
                    barrier, inc=1, device_id={"tm": lax.rem(me + step, size), "stn": lax.rem(core + side, 2)},
                    device_id_type=MESH)
    pl.semaphore_wait(barrier, 2 * size - 1)

    first_col = col == 0
    mid = (col > 0) & (col < cols - 1)
    has_left = col > 0
    to_right = col < cols - 2

    def weight_copy(step):
        return pltpu.make_async_remote_copy(
            src_ref=rows_ref, dst_ref=table.at[me], send_sem=send_w.at[step], recv_sem=recv_w.at[step],
            device_id={"tm": lax.rem(me + step, size)}, device_id_type=MESH)

    def mine(half, j):
        return v_ref.at[pl.ds(half * share, share), :, j]

    def swap_sent(n):
        return jnp.where(y == 0, n, wide - 1 - n)

    def swap_got(n):
        return jnp.where(y == 0, wide - 1 - n, n)

    def swap_copy(n):
        o = swap_sent(n)
        return pltpu.make_async_remote_copy(
            src_ref=mine(1 - y, lax.rem(o, frames)), dst_ref=x.at[base + o], send_sem=send_y.at[n], recv_sem=recv_y.at[n],
            device_id={"tm": 2 * col + 1 - y}, device_id_type=MESH)

    def left_copy(o, src):
        return pltpu.make_async_remote_copy(
            src_ref=src, dst_ref=x.at[base + wide + o], send_sem=send_l.at[o], recv_sem=recv_r.at[o],
            device_id={"tm": me - 2}, device_id_type=MESH)

    def right_copy(o, src):
        return pltpu.make_async_remote_copy(
            src_ref=src, dst_ref=x.at[base - wide + o], send_sem=send_r.at[o], recv_sem=recv_l.at[o],
            device_id={"tm": me + 2}, device_id_type=MESH)

    def own_src(o):
        return mine(y, o % frames)

    def got_src(o):
        return x.at[base + o]

    def power_copy(i):
        return pltpu.make_async_remote_copy(
            src_ref=given.at[i], dst_ref=taken.at[i], send_sem=send_p.at[i], recv_sem=recv_p.at[i],
            device_id={"tm": me + 2}, device_id_type=MESH)

    def own_copy(j):
        return pltpu.make_async_copy(mine(y, j), x.at[base + y * frames + j], local.at[j])

    for step in range(1, size):
        weight_copy(step).start()
    for n in range(frames):
        swap_copy(n).start()

    @pl.when(has_left & (y == 0))
    def _():
        for o in range(frames):
            left_copy(o, own_src(o)).start()

    @pl.when(has_left & (y == 1))
    def _():
        left_copy(frames, own_src(frames)).start()

    @pl.when(to_right & (y == 0))
    def _():
        right_copy(frames - 1, own_src(frames - 1)).start()

    @pl.when(to_right & (y == 1))
    def _():
        for o in range(wide - 1, frames - 1, -1):
            right_copy(o, own_src(o)).start()

    for j in range(frames):
        own_copy(j).start()
    keep = pltpu.make_async_copy(rows_ref, table.at[me], local.at[frames])
    keep.start()

    @pl.when(first_col)
    def _():
        def clear(n, carry):
            x[n] = jnp.zeros(x.shape[1:], x.dtype)
            return carry
        lax.fori_loop(0, base, clear, 0)

    for a in range(taps.shape[1] // 2):
        piece = taps_ref[:, a * LANES:(a + 1) * LANES]
        taps[:, 2 * a, :] = piece
        taps[:, 2 * a + 1, :] = piece

    for step in range(1, size):
        weight_copy(step).wait_recv()
    keep.wait()
    width = groups * 2 * SB
    entries = table[:, :, pl.ds(pl.multiple_of(core * width, width), width)].reshape(-1, width)
    entries = entries.astype(f32).T.astype(bf16)
    ids = lax.broadcasted_iota(jnp.int32, (entries.shape[1], beams), 0)
    stations = index_ref.shape[0] * SB
    for q in range(index_ref.shape[0]):
        onehot = jnp.where(ids == index_ref[q:q + 1, :], mask_ref[q:q + 1, :], 0).astype(f32).astype(bf16)
        picked = jnp.dot(entries, onehot, preferred_element_type=f32)
        for g in range(groups):
            low = 2 * g * SB
            re = picked[low:low + SB]
            im = picked[low + SB:low + 2 * SB]
            weights[g, q * SB:(q + 1) * SB, :beams] = re.astype(bf16)
            weights[g, q * SB:(q + 1) * SB, beams:] = im.astype(bf16)
            weights[g, stations + q * SB:stations + (q + 1) * SB, :beams] = (-im).astype(bf16)
            weights[g, stations + q * SB:stations + (q + 1) * SB, beams:] = re.astype(bf16)
    for j in range(frames):
        own_copy(j).wait()

    rounds = 2 * wide

    def offset(i):
        e = i - frames
        return jnp.where(e == wide - 1, wide - 1, jnp.where(lax.rem(e, 2) == 0, frames - 1 + e // 2, frames - 2 - e // 2))

    def busy(i):
        return (first_col & (i >= 0) & (i < rounds)) | (mid & (i >= frames) & (i < frames + wide))

    def plan(i):
        o = offset(i)
        slot = jnp.where(first_col, base + i, base + wide + o)
        owner = jnp.where(first_col, lax.rem(i // frames, 2), o // frames)
        bank = jnp.where(first_col, i // wide * frames + lax.rem(i, frames), lax.rem(o, frames))
        return slot, owner, bank

    def spectra_copy(i, h, p, owner, bank):
        return pltpu.make_async_remote_copy(
            src_ref=z.at[i, h, p], dst_ref=r.at[bank, p, :, :, pl.ds(place * share, share), :],
            send_sem=send_z.at[i, h, p], recv_sem=recv_z.at[i, place, p],
            device_id={"tm": 2 * col + owner, "stn": h}, device_id_type=MESH)

    def spectra_keep(i, h, p, bank):
        return pltpu.make_async_copy(
            z.at[i, h, p], r.at[bank, p, :, :, pl.ds(place * share, share), :], own_z.at[i, p])

    def spectra_wait(i, where, p, bank):
        return pltpu.make_async_remote_copy(
            src_ref=z.at[i, 0, p], dst_ref=r.at[bank, p, :, :, pl.ds(where * share, share), :],
            send_sem=send_z.at[i, 0, p], recv_sem=recv_z.at[i, where, p],
            device_id={"tm": 2 * col + 1 - y}, device_id_type=MESH)

    def forward(n):
        swap_copy(n).wait_recv()
        o = swap_got(n)

        @pl.when(to_right & (y == 0))
        def _():
            right_copy(o, got_src(o)).start()

        @pl.when(has_left & (y == 1))
        def _():
            left_copy(o, got_src(o)).start()

        @pl.when((n == frames - 1) & has_left & (y == 0))
        def _():
            for o in range(frames, wide):
                left_copy(o, got_src(o)).start()

        @pl.when((n == frames - 1) & has_left & (y == 1))
        def _():
            for o in range(frames + 1, wide):
                left_copy(o, own_src(o)).start()

        @pl.when((n == frames - 1) & to_right & (y == 0))
        def _():
            for o in range(frames - 2, 0, -1):
                right_copy(o, own_src(o)).start()

        @pl.when((n == frames - 1) & to_right & (y == 1))
        def _():
            for o in range(frames - 1, 0, -1):
                right_copy(o, got_src(o)).start()

    def wait_right(o):
        left_copy(o, got_src(0)).wait_recv()

    def wait_left(o):
        right_copy(o, got_src(0)).wait_recv()

    def arrive(i):
        @pl.when(first_col & (i >= wide))
        def _():
            wait_right(i - wide)

        @pl.when(mid & (i == frames))
        def _():
            for o in range(frames - 1):
                wait_right(o)
            for o in range(frames, wide):
                wait_left(o)

        o = offset(i)
        fresh = (lax.rem(i, 2) == 0) | (i == frames + wide - 1)

        @pl.when(mid & fresh)
        def _():
            wait_right(o)

        @pl.when(mid & jnp.logical_not(fresh))
        def _():
            wait_left(o + 1)

    halves = 2

    def channelize(i):
        slot, owner, bank = plan(i)

        def filter_rows(n, carry):
            quad = n // halves
            rows = pl.ds(pl.multiple_of(lax.rem(n, halves) * 16, 16), 16)
            sums = [None] * (4 * pols)
            for k in range(depth):
                tap = taps[k, rows, :]
                for m in range(4):
                    for p in range(pols):
                        term = tap * x[slot - k, quad * 4 + m, p, rows, :].astype(f32)
                        j = m * pols + p
                        sums[j] = term if k == 0 else sums[j] + term
            for m in range(4):
                for p in range(pols):
                    row = (lax.rem(quad, 2) * 4 + m) * 32 + lax.rem(n, halves) * 16
                    held[quad // 2, pl.ds(pl.multiple_of(row, 16), 16), p * LANES:(p + 1) * LANES] = (
                        sums[m * pols + p].astype(bf16))
            return carry
        lax.fori_loop(0, share // 4 * halves, filter_rows, 0)

        batches = share // 8
        block = FIRST * 8
        for b in range(batches):
            spread = jnp.dot(one_ref[...], held[b], preferred_element_type=f32)
            for lh in range(2):
                cos, sin = cos_ref[lh], sin_ref[lh]
                for p in range(pols):
                    re = spread[2 * lh * block:(2 * lh + 1) * block, p * LANES:(p + 1) * LANES]
                    im = spread[(2 * lh + 1) * block:(2 * lh + 2) * block, p * LANES:(p + 1) * LANES]
                    tw[p, b * block:(b + 1) * block, lh * LANES:(lh + 1) * LANES] = (re * cos + im * sin).astype(bf16)
                    tw[p, b * block:(b + 1) * block, (2 + lh) * LANES:(3 + lh) * LANES] = (
                        im * cos - re * sin).astype(bf16)
        for p in range(pols):
            for h in range(2):
                spectra = jnp.dot(
                    tw[p], two_ref[:, h * 2 * LANES:(h + 1) * 2 * LANES], preferred_element_type=f32)
                for k1 in range(FIRST):
                    rows = jnp.concatenate(
                        [spectra[b * block + k1 * 8:b * block + (k1 + 1) * 8] for b in range(batches)], axis=0).astype(bf16)
                    for part in range(2):
                        z[i, h, p, k1, part] = rows[:, part * LANES:(part + 1) * LANES]
                stay = (owner == y) & (core == h)

                @pl.when(stay)
                def _():
                    spectra_keep(i, h, p, bank).start()

                @pl.when(jnp.logical_not(stay))
                def _():
                    spectra_copy(i, h, p, owner, bank).start()

    def beamform(i):
        _, owner, bank = plan(i)
        for p in range(pols):
            for where in range(4):
                @pl.when(place == where)
                def _():
                    spectra_keep(i, core, p, bank).wait()

                @pl.when(place != where)
                def _():
                    spectra_wait(i, where, p, bank).wait_recv()

        def turn(k1, carry):
            for p in range(pols):
                for part in range(2):
                    tile = r[bank, p, k1, part].T
                    for g in range(groups):
                        turned[p, g, pl.ds(pl.multiple_of(k1 * lows, lows), lows), part * LANES:(part + 1) * LANES] = (
                            tile[g * lows:(g + 1) * lows])
            return carry
        lax.fori_loop(0, FIRST, turn, 0)

        stays = first_col & (i < wide)
        at = lax.rem(bank, frames)

        def group(g, carry):
            power = None
            for p in range(pols):
                beam = jnp.dot(turned[p, g], weights[g], preferred_element_type=f32)
                term = beam[:, :beams] * beam[:, :beams] + beam[:, beams:] * beam[:, beams:]
                power = term if p == 0 else power + term
            power = power.astype(bf16)
            rows = pl.ds(pl.multiple_of(g * LANES, LANES), LANES)

            @pl.when(stays)
            def _():
                taken[at, rows, :] = power

            @pl.when(jnp.logical_not(stays))
            def _():
                given[at, rows, :] = power
            return carry
        lax.fori_loop(0, groups, group, 0)

        @pl.when(jnp.logical_not(stays))
        def _():
            power_copy(at).start()

    def round_(i, carry):
        @pl.when(i < frames)
        def _():
            forward(i)

        @pl.when(busy(i))
        def _():
            arrive(i)
            channelize(i)

        late = i - LAG
        _, owner, _ = plan(late)

        @pl.when(busy(late) & (owner == y))
        def _():
            beamform(late)
        return carry
    lax.fori_loop(0, rounds + LAG, round_, 0)

    pieces = beams // LANES
    pitch = pieces * frames

    def finish(n, carry):
        down = (col > 1) & (y == 0)
        f = jnp.where(down, frames - 1 - n, n)

        @pl.when(has_left)
        def _():
            power_copy(f).wait_recv()

        def spread(g, carry):
            for k1 in range(FIRST):
                rows = taken[f, pl.ds(pl.multiple_of(g * LANES + k1 * lows, lows), lows), :].astype(f32)
                for half in range(lows // 8):
                    for piece in range(pieces):
                        row = g * (LANES * pitch) + (half * 8 * FIRST + k1) * pitch + piece * frames + f
                        out_ref[pl.ds(row, 8, stride=FIRST * pitch), :] = (
                            rows[half * 8:(half + 1) * 8, piece * LANES:(piece + 1) * LANES])
            return carry
        lax.fori_loop(0, groups, spread, 0)
        return carry
    lax.fori_loop(0, frames, finish, 0)

    for step in range(1, size):
        weight_copy(step).wait_send()
    for n in range(frames):
        swap_copy(n).wait_send()

    @pl.when(has_left)
    def _():
        for o in range(wide):
            left_copy(o, got_src(0)).wait_send()

    @pl.when(to_right)
    def _():
        for o in range(1, wide):
            right_copy(o, got_src(0)).wait_send()

    @pl.when(first_col | mid)
    def _():
        for n in range(frames):
            power_copy(n).wait_send()

    def drain(i, carry):
        @pl.when(busy(i))
        def _():
            _, owner, bank = plan(i)
            for h in range(2):
                @pl.when(jnp.logical_not((owner == y) & (core == h)))
                def _():
                    for p in range(pols):
                        spectra_copy(i, h, p, owner, bank).wait_send()
        return carry
    lax.fori_loop(0, rounds, drain, 0)


def fused(v, weight_rows, index, mask, taps, tables, size):
    stations, pols, frames, rows, _ = v.shape
    share = stations // 2
    groups = G // 2
    beams = index.shape[1]
    depth, channels = taps.shape
    wide = 2 * frames
    bf16 = jnp.bfloat16
    dma = pltpu.SemaphoreType.DMA
    vmem = pl.BlockSpec(memory_space=pltpu.VMEM)
    hbm = pl.BlockSpec(memory_space=pl.ANY)
    return pl.pallas_call(
        functools.partial(kernel, size),
        out_shape=jax.ShapeDtypeStruct((channels // 2 * frames * beams // LANES, LANES), jnp.float32),
        in_specs=[hbm] + [vmem] * 8,
        out_specs=vmem,
        scratch_shapes=[
            pltpu.VMEM((depth - 1 + 2 * wide, share, pols, rows, LANES), bf16),
            pltpu.VMEM((depth, rows, LANES), jnp.float32),
            pltpu.VMEM((share // 8, 8 * rows, pols * LANES), bf16),
            pltpu.VMEM((pols, FIRST * share, 4 * LANES), bf16),
            pltpu.VMEM((2 * wide, 2, pols, FIRST, 2, share, LANES), bf16),
            pltpu.VMEM((wide, pols, FIRST, 2, 4 * share, LANES), bf16),
            pltpu.VMEM((size,) + weight_rows.shape, bf16),
            pltpu.VMEM((groups, 8 * share, 2 * beams), bf16),
            pltpu.VMEM((pols, groups, LANES, 2 * LANES), bf16),
            pltpu.VMEM((frames, channels // 2, beams), bf16),
            pltpu.VMEM((frames, channels // 2, beams), bf16),
            dma((frames + 1,)), dma((size,)), dma((size,)), dma((frames,)), dma((frames,)),
            dma((wide,)), dma((wide,)), dma((wide,)), dma((wide,)),
            dma((2 * wide, 2, pols)), dma((2 * wide, 4, pols)), dma((2 * wide, pols)), dma((frames,)), dma((frames,)),
        ],
        compiler_params=pltpu.CompilerParams(collective_id=0, has_side_effects=True, vmem_limit_bytes=60 << 20),
        name="fused_beams",
    )(v, weight_rows, index, mask, taps, *tables)


def body(voltages, filter_taps, use_mask, block_index, weight_blocks):
    stations, pols, frames, _, channels = voltages.shape
    size = lax.axis_size("tm")
    v = voltages.reshape(stations, pols, frames, 2, channels // LANES, LANES).swapaxes(-3, -2)
    v = v.reshape(stations, pols, frames, 2 * channels // LANES, LANES)
    beams = block_index.shape[0]
    power = fused(v, weight_blocks, block_index.T, use_mask.T, filter_taps, transform_tables(channels), size)
    power = power.reshape(channels // 2, beams // LANES, frames, LANES)
    return power.swapaxes(1, 2).reshape(channels // 2, frames, beams)


def solution(mesh):
    in_specs = (
        P(("parts", "stn"), None, "tm", None, None),
        P(),
        P("parts", None),
        P("parts", None),
        P("tm", None),
    )
    out_specs = P("stn", "tm", "parts")
    return jax.shard_map(body, mesh=mesh, in_specs=in_specs, out_specs=out_specs, check_vma=False)
```

```python
import functools
import math

import jax
import jax.numpy as jnp
import numpy as np
from jax import lax
from jax.experimental import pallas as pl
from jax.experimental.pallas import tpu as pltpu
from jax.sharding import PartitionSpec as P

SB = 16
G = 16
LANES = 128
FIRST = 8
KEPT = 2
ROUNDS = 18
MESH = pl.DeviceIdType.MESH


def transform_tables(channels):
    second = channels // FIRST
    parts = second // LANES
    a = np.arange(FIRST)
    l = np.arange(second)

    def waves(product, period):
        angle = (product % period).astype(np.float32) * np.float32(2.0 * math.pi / period)
        return np.cos(angle), np.sin(angle)

    cos, sin = waves(a[:, None] * a[None, :], FIRST)
    one = np.zeros((parts, 2, FIRST, 8, 8, FIRST, parts, 2), np.float32)
    for lh in range(parts):
        for s in range(8):
            one[lh, 0, :, s, s, :, lh, 0] = cos
            one[lh, 0, :, s, s, :, lh, 1] = sin
            one[lh, 1, :, s, s, :, lh, 0] = -sin
            one[lh, 1, :, s, s, :, lh, 1] = cos
    one = one.reshape(parts * 2 * FIRST * 8, 8 * FIRST * parts * 2)
    cos, sin = waves(l[:, None] * l[None, :], second)
    two = np.stack([np.stack([cos, -sin], axis=1), np.stack([sin, cos], axis=1)], axis=0)
    two = two.reshape(2, second, 2, 2, LANES).transpose(0, 1, 3, 2, 4).reshape(2 * second, 2 * second)
    cos, sin = waves(a[:, None] * l[None, :], channels)
    norm = np.float32(1.0 / math.sqrt(channels))
    cos, sin = (
        np.repeat((w * norm).reshape(FIRST, parts, LANES).swapaxes(0, 1), 8, axis=1) for w in (cos, sin))
    return jnp.asarray(one, jnp.bfloat16), jnp.asarray(two, jnp.bfloat16), jnp.asarray(cos), jnp.asarray(sin)


def schedule(frames):
    wide = 2 * frames

    def orders(filters, early, beams, right, left):
        rows = []
        had = [0, 0]
        for j in range(ROUNDS):
            here = [d for k, d in filters if k == j]
            need = list(had)
            for d in here:
                need = [max(need[0], right(d)), max(need[1], left(d))]
            sent = [d for k, d in early if k == j]
            done = [d for k, d in beams if k == j]
            word = 0
            for d in (here + [-1])[:1] + (sent + [-1, -1])[:2] + (done + [-1])[:1]:
                word = word * 32 + d + 1
            rows.append((word, ((had[0] * 16 + need[0]) * 16 + had[1]) * 16 + need[1]))
            had = need
        return rows

    def right(d):
        return max(d - wide + 1, 0)

    def left(most):
        return lambda d: min(max(2 * wide - 1 - d, 0), most)

    def placed(first, order):
        return [(first + k, d) for k, d in enumerate(order)]

    head = placed(0, [0, 1, 2, 3, 4, 8, 12, 9, 13, 5, 6, 7])
    sent = [(0, 0)] + placed(4, [4, 8, 12, 9, 13, 5, 6, 7]) + placed(8, [1, 2, 3])
    shift = [11, 12, 10, 13, 9, 8, 14, 15]
    both = placed(4, shift + [2, 6, 3, 7])
    only = placed(4, shift)
    zero = lambda d: 0
    upper = [(8, 11), (10, 10), (11, 9), (14, 8)]
    lower = [(8, 12), (10, 13), (12, 14), (15, 15)]
    return [
        [orders(head, sent, [(6, 0), (8, 8), (10, 9), (12, 1), (13, 2), (14, 3)], right, zero),
         orders(head, sent, [(7, 4), (9, 12), (11, 13), (12, 5), (13, 6), (14, 7)], right, zero)],
        [orders(both, both, upper + [(16, 2), (17, 3)], right, left(wide)),
         orders(both, both, lower + [(16, 6), (17, 7)], right, left(wide))],
        [orders(only, only, upper, right, left(wide - 1)),
         orders(only, only, lower, right, left(wide - 1))],
    ]


def kernel(size, v_ref, rows_ref, index_ref, mask_ref, taps_ref, one_ref, two_ref, cos_ref, sin_ref, out_ref,
           x, taps, held, tw, z, r, table, weights, turned, given, taken,
           local, send_w, recv_w, send_y, recv_y, send_l, recv_l, send_r, recv_r, send_z, recv_z, own_z, send_p, recv_p):
    me = lax.axis_index("tm")
    core = lax.axis_index("stn")
    col = me // 2
    y = lax.rem(me, 2)
    cols = size // 2
    frames = v_ref.shape[2]
    wide = 2 * frames
    depth = taps_ref.shape[0]
    base = depth - 1
    pols = v_ref.shape[1]
    share = v_ref.shape[0] // 2
    groups, _, beams2 = weights.shape
    beams = beams2 // 2
    lows = LANES // groups
    bf16 = jnp.bfloat16
    f32 = jnp.float32
    place = 2 * core + y

    barrier = pltpu.get_barrier_semaphore()
    for step in range(size):
        for side in range(2):
            if step or side:
                pl.semaphore_signal(
                    barrier, inc=1, device_id={"tm": lax.rem(me + step, size), "stn": lax.rem(core + side, 2)},
                    device_id_type=MESH)
    pl.semaphore_wait(barrier, 2 * size - 1)

    first_col = col == 0
    second_col = col == 1
    mid = (col > 0) & (col < cols - 1)
    has_left = col > 0
    to_right = col < cols - 2

    def weight_copy(step):
        return pltpu.make_async_remote_copy(
            src_ref=rows_ref, dst_ref=table.at[me], send_sem=send_w.at[step], recv_sem=recv_w.at[step],
            device_id={"tm": lax.rem(me + step, size)}, device_id_type=MESH)

    def mine(half, j):
        return v_ref.at[pl.ds(half * share, share), :, j]

    def swap_sent(n):
        return jnp.where(y == 0, n, wide - 1 - n)

    def swap_got(n):
        return jnp.where(y == 0, wide - 1 - n, n)

    def swap_copy(n):
        o = swap_sent(n)
        return pltpu.make_async_remote_copy(
            src_ref=mine(1 - y, lax.rem(o, frames)), dst_ref=x.at[base + o], send_sem=send_y.at[n], recv_sem=recv_y.at[n],
            device_id={"tm": 2 * col + 1 - y}, device_id_type=MESH)

    def left_copy(o, src):
        return pltpu.make_async_remote_copy(
            src_ref=src, dst_ref=x.at[base + wide + o], send_sem=send_l.at[o], recv_sem=recv_r.at[o],
            device_id={"tm": me - 2}, device_id_type=MESH)

    def right_copy(o, src):
        return pltpu.make_async_remote_copy(
            src_ref=src, dst_ref=x.at[base - wide + o], send_sem=send_r.at[o], recv_sem=recv_l.at[o],
            device_id={"tm": me + 2}, device_id_type=MESH)

    def own_src(o):
        return mine(y, o % frames)

    def got_src(o):
        return x.at[base + o]

    def power_copy(i):
        return pltpu.make_async_remote_copy(
            src_ref=given.at[i], dst_ref=taken.at[i], send_sem=send_p.at[i], recv_sem=recv_p.at[i],
            device_id={"tm": me + 2}, device_id_type=MESH)

    def own_copy(j):
        return pltpu.make_async_copy(mine(y, j), x.at[base + y * frames + j], local.at[j])

    for step in range(1, size):
        weight_copy(step).start()
    for n in range(frames):
        swap_copy(n).start()

    @pl.when(has_left & (y == 0))
    def _():
        for o in range(frames):
            left_copy(o, own_src(o)).start()

    @pl.when(has_left & (y == 1))
    def _():
        left_copy(frames, own_src(frames)).start()

    @pl.when(to_right & (y == 0))
    def _():
        right_copy(frames - 1, own_src(frames - 1)).start()

    @pl.when(to_right & (y == 1))
    def _():
        for o in range(wide - 1, frames - 1, -1):
            right_copy(o, own_src(o)).start()

    for j in range(frames):
        own_copy(j).start()
    keep = pltpu.make_async_copy(rows_ref, table.at[me], local.at[frames])
    keep.start()

    def clear(n, carry):
        x[n] = jnp.zeros(x.shape[1:], x.dtype)
        return carry
    lax.fori_loop(0, jnp.where(first_col, base, jnp.where(second_col, base - wide, 0)), clear, 0)

    for a in range(taps.shape[1] // 2):
        piece = taps_ref[:, a * LANES:(a + 1) * LANES]
        taps[:, 2 * a, :] = piece
        taps[:, 2 * a + 1, :] = piece

    for step in range(1, size):
        weight_copy(step).wait_recv()
    keep.wait()
    width = groups * 2 * SB
    entries = table[:, :, pl.ds(pl.multiple_of(core * width, width), width)].reshape(-1, width)
    entries = entries.astype(f32).T.astype(bf16)
    ids = lax.broadcasted_iota(jnp.int32, (entries.shape[1], beams), 0)
    stations = index_ref.shape[0] * SB
    for q in range(index_ref.shape[0]):
        onehot = jnp.where(ids == index_ref[q:q + 1, :], mask_ref[q:q + 1, :], 0).astype(f32).astype(bf16)
        picked = jnp.dot(entries, onehot, preferred_element_type=f32)
        for g in range(groups):
            low = 2 * g * SB
            re = picked[low:low + SB]
            im = picked[low + SB:low + 2 * SB]
            weights[g, q * SB:(q + 1) * SB, :beams] = re.astype(bf16)
            weights[g, q * SB:(q + 1) * SB, beams:] = im.astype(bf16)
            weights[g, stations + q * SB:stations + (q + 1) * SB, :beams] = (-im).astype(bf16)
            weights[g, stations + q * SB:stations + (q + 1) * SB, beams:] = re.astype(bf16)
    for j in range(frames):
        own_copy(j).wait()

    plans = schedule(frames)

    def look(j):
        words = []
        for k in range(2):
            kinds = []
            for kind in plans:
                sides = []
                for rows in kind:
                    word = jnp.int32(0)
                    for step, row in enumerate(rows):
                        if row[k]:
                            word = jnp.where(j == step, row[k], word)
                    sides.append(word)
                kinds.append(jnp.where(y == 0, sides[0], sides[1]))
            words.append(jnp.where(first_col, kinds[0], jnp.where(second_col, kinds[1], jnp.where(mid, kinds[2], 0))))
        ops, waits = words
        ops = [lax.rem(ops // 32 ** n, 32) - 1 for n in (3, 2, 1, 0)]
        waits = [lax.rem(waits // 16 ** n, 16) for n in (3, 2, 1, 0)]
        return ops, waits

    def busy(d):
        stays = d < wide
        near = lax.rem(d, frames) < KEPT
        return (first_col & (stays | near)) | (second_col & jnp.logical_not(stays & near)) | (
            mid & jnp.logical_not(second_col | stays))

    def plan(d):
        owner = lax.rem(d // frames, 2)
        bank = d // wide * frames + lax.rem(d, frames)
        return owner, bank

    def spectra_copy(i, h, p, owner, bank):
        return pltpu.make_async_remote_copy(
            src_ref=z.at[i, h, p], dst_ref=r.at[bank, p, :, :, pl.ds(place * share, share), :],
            send_sem=send_z.at[i, h, p], recv_sem=recv_z.at[i, place, p],
            device_id={"tm": 2 * col + owner, "stn": h}, device_id_type=MESH)

    def spectra_keep(i, h, p, bank):
        return pltpu.make_async_copy(
            z.at[i, h, p], r.at[bank, p, :, :, pl.ds(place * share, share), :], own_z.at[i, p])

    def spectra_wait(i, where, p, bank):
        return pltpu.make_async_remote_copy(
            src_ref=z.at[i, 0, p], dst_ref=r.at[bank, p, :, :, pl.ds(where * share, share), :],
            send_sem=send_z.at[i, 0, p], recv_sem=recv_z.at[i, where, p],
            device_id={"tm": 2 * col + 1 - y}, device_id_type=MESH)

    def forward(n):
        swap_copy(n).wait_recv()
        o = swap_got(n)

        @pl.when(to_right & (y == 0))
        def _():
            right_copy(o, got_src(o)).start()

        @pl.when(has_left & (y == 1))
        def _():
            left_copy(o, got_src(o)).start()

        @pl.when((n == frames - 1) & has_left & (y == 0))
        def _():
            for o in range(frames, frames + KEPT):
                left_copy(o, got_src(o)).start()

            @pl.when(col > 1)
            def _():
                for o in range(frames + KEPT, wide):
                    left_copy(o, got_src(o)).start()

        @pl.when((n == frames - 1) & has_left & (y == 1))
        def _():
            for o in range(frames + 1, frames + KEPT):
                left_copy(o, own_src(o)).start()

            @pl.when(col > 1)
            def _():
                for o in range(frames + KEPT, wide):
                    left_copy(o, own_src(o)).start()

        @pl.when((n == frames - 1) & to_right & (y == 0))
        def _():
            for o in range(frames - 2, 0, -1):
                right_copy(o, own_src(o)).start()

            @pl.when(first_col)
            def _():
                right_copy(0, own_src(0)).start()

        @pl.when((n == frames - 1) & to_right & (y == 1))
        def _():
            for o in range(frames - 1, 0, -1):
                right_copy(o, got_src(o)).start()

            @pl.when(first_col)
            def _():
                right_copy(0, got_src(0)).start()

    def wait_right(o):
        left_copy(o, got_src(0)).wait_recv()

    def wait_left(o):
        right_copy(o, got_src(0)).wait_recv()

    halves = 2

    def channelize(i):
        slot = base + i

        def filter_rows(n, carry):
            quad = n // halves
            rows = pl.ds(pl.multiple_of(lax.rem(n, halves) * 16, 16), 16)
            sums = [None] * (4 * pols)
            for k in range(depth):
                tap = taps[k, rows, :]
                for m in range(4):
                    for p in range(pols):
                        term = tap * x[slot - k, quad * 4 + m, p, rows, :].astype(f32)
                        j = m * pols + p
                        sums[j] = term if k == 0 else sums[j] + term
            for m in range(4):
                for p in range(pols):
                    row = (lax.rem(quad, 2) * 4 + m) * 32 + lax.rem(n, halves) * 16
                    held[quad // 2, pl.ds(pl.multiple_of(row, 16), 16), p * LANES:(p + 1) * LANES] = (
                        sums[m * pols + p].astype(bf16))
            return carry
        lax.fori_loop(0, share // 4 * halves, filter_rows, 0)

        batches = share // 8
        block = FIRST * 8
        for b in range(batches):
            spread = jnp.dot(one_ref[...], held[b], preferred_element_type=f32)
            for lh in range(2):
                cos, sin = cos_ref[lh], sin_ref[lh]
                for p in range(pols):
                    re = spread[2 * lh * block:(2 * lh + 1) * block, p * LANES:(p + 1) * LANES]
                    im = spread[(2 * lh + 1) * block:(2 * lh + 2) * block, p * LANES:(p + 1) * LANES]
                    tw[p, b * block:(b + 1) * block, lh * LANES:(lh + 1) * LANES] = (re * cos + im * sin).astype(bf16)
                    tw[p, b * block:(b + 1) * block, (2 + lh) * LANES:(3 + lh) * LANES] = (
                        im * cos - re * sin).astype(bf16)
        for p in range(pols):
            for h in range(2):
                spectra = jnp.dot(
                    tw[p], two_ref[:, h * 2 * LANES:(h + 1) * 2 * LANES], preferred_element_type=f32)
                for k1 in range(FIRST):
                    rows = jnp.concatenate(
                        [spectra[b * block + k1 * 8:b * block + (k1 + 1) * 8] for b in range(batches)], axis=0).astype(bf16)
                    for part in range(2):
                        z[i, h, p, k1, part] = rows[:, part * LANES:(part + 1) * LANES]

    def share_out(i):
        owner, bank = plan(i)
        for p in range(pols):
            for h in range(2):
                stay = (owner == y) & (core == h)

                @pl.when(stay)
                def _():
                    spectra_keep(i, h, p, bank).start()

                @pl.when(jnp.logical_not(stay))
                def _():
                    spectra_copy(i, h, p, owner, bank).start()

    def beamform(i):
        _, bank = plan(i)
        for p in range(pols):
            for where in range(4):
                @pl.when(place == where)
                def _():
                    spectra_keep(i, core, p, bank).wait()

                @pl.when(place != where)
                def _():
                    spectra_wait(i, where, p, bank).wait_recv()

        def turn(k1, carry):
            for p in range(pols):
                for part in range(2):
                    tile = r[bank, p, k1, part].T
                    for g in range(groups):
                        turned[p, g, pl.ds(pl.multiple_of(k1 * lows, lows), lows), part * LANES:(part + 1) * LANES] = (
                            tile[g * lows:(g + 1) * lows])
            return carry
        lax.fori_loop(0, FIRST, turn, 0)

        stays = i < wide
        at = lax.rem(bank, frames)

        def group(g, carry):
            power = None
            for p in range(pols):
                beam = jnp.dot(turned[p, g], weights[g], preferred_element_type=f32)
                term = beam[:, :beams] * beam[:, :beams] + beam[:, beams:] * beam[:, beams:]
                power = term if p == 0 else power + term
            power = power.astype(bf16)
            rows = pl.ds(pl.multiple_of(g * LANES, LANES), LANES)

            @pl.when(stays)
            def _():
                taken[at, rows, :] = power

            @pl.when(jnp.logical_not(stays))
            def _():
                given[at, rows, :] = power
            return carry
        lax.fori_loop(0, groups, group, 0)

        @pl.when(jnp.logical_not(stays))
        def _():
            power_copy(at).start()

    def round_(j, carry):
        (made, sent, also, late), (right_from, right_to, left_from, left_to) = look(j)

        @pl.when(j < frames)
        def _():
            forward(j)

        @pl.when(made >= 0)
        def _():
            def from_right(o, carry):
                wait_right(o)
                return carry
            lax.fori_loop(right_from, right_to, from_right, 0)

            def from_left(n, carry):
                wait_left(wide - 1 - n)
                return carry
            lax.fori_loop(left_from, left_to, from_left, 0)
            channelize(made)

        @pl.when(sent >= 0)
        def _():
            share_out(sent)

        @pl.when(also >= 0)
        def _():
            share_out(also)

        @pl.when(late >= 0)
        def _():
            beamform(late)
        return carry
    lax.fori_loop(0, ROUNDS, round_, 0)

    pieces = beams // LANES
    pitch = pieces * frames

    def finish(n, carry):
        down = (col > 1) & (y == 0)
        f = jnp.where(down, frames - 1 - n, n)

        @pl.when(has_left & ((col > 1) | (f < KEPT)))
        def _():
            power_copy(f).wait_recv()

        def spread(g, carry):
            for k1 in range(FIRST):
                rows = taken[f, pl.ds(pl.multiple_of(g * LANES + k1 * lows, lows), lows), :].astype(f32)
                for half in range(lows // 8):
                    for piece in range(pieces):
                        row = g * (LANES * pitch) + (half * 8 * FIRST + k1) * pitch + piece * frames + f
                        out_ref[pl.ds(row, 8, stride=FIRST * pitch), :] = (
                            rows[half * 8:(half + 1) * 8, piece * LANES:(piece + 1) * LANES])
            return carry
        lax.fori_loop(0, groups, spread, 0)
        return carry
    lax.fori_loop(0, frames, finish, 0)

    for step in range(1, size):
        weight_copy(step).wait_send()
    for n in range(frames):
        swap_copy(n).wait_send()

    @pl.when(has_left)
    def _():
        for o in range(frames + KEPT):
            left_copy(o, got_src(0)).wait_send()

        @pl.when(col > 1)
        def _():
            for o in range(frames + KEPT, wide):
                left_copy(o, got_src(0)).wait_send()

    @pl.when(to_right)
    def _():
        for o in range(1, wide):
            right_copy(o, got_src(0)).wait_send()

        @pl.when(first_col)
        def _():
            right_copy(0, got_src(0)).wait_send()

    for n in range(frames):
        @pl.when(mid | (first_col & (n < KEPT)))
        def _():
            power_copy(n).wait_send()

    def drain(i, carry):
        @pl.when(busy(i))
        def _():
            owner, bank = plan(i)
            for h in range(2):
                @pl.when(jnp.logical_not((owner == y) & (core == h)))
                def _():
                    for p in range(pols):
                        spectra_copy(i, h, p, owner, bank).wait_send()
        return carry
    lax.fori_loop(0, 2 * wide, drain, 0)


def fused(v, weight_rows, index, mask, taps, tables, size):
    stations, pols, frames, rows, _ = v.shape
    share = stations // 2
    groups = G // 2
    beams = index.shape[1]
    depth, channels = taps.shape
    wide = 2 * frames
    bf16 = jnp.bfloat16
    dma = pltpu.SemaphoreType.DMA
    vmem = pl.BlockSpec(memory_space=pltpu.VMEM)
    hbm = pl.BlockSpec(memory_space=pl.ANY)
    return pl.pallas_call(
        functools.partial(kernel, size),
        out_shape=jax.ShapeDtypeStruct((channels // 2 * frames * beams // LANES, LANES), jnp.float32),
        in_specs=[hbm] + [vmem] * 8,
        out_specs=vmem,
        scratch_shapes=[
            pltpu.VMEM((depth - 1 + 2 * wide, share, pols, rows, LANES), bf16),
            pltpu.VMEM((depth, rows, LANES), jnp.float32),
            pltpu.VMEM((share // 8, 8 * rows, pols * LANES), bf16),
            pltpu.VMEM((pols, FIRST * share, 4 * LANES), bf16),
            pltpu.VMEM((2 * wide, 2, pols, FIRST, 2, share, LANES), bf16),
            pltpu.VMEM((wide, pols, FIRST, 2, 4 * share, LANES), bf16),
            pltpu.VMEM((size,) + weight_rows.shape, bf16),
            pltpu.VMEM((groups, 8 * share, 2 * beams), bf16),
            pltpu.VMEM((pols, groups, LANES, 2 * LANES), bf16),
            pltpu.VMEM((frames, channels // 2, beams), bf16),
            pltpu.VMEM((frames, channels // 2, beams), bf16),
            dma((frames + 1,)), dma((size,)), dma((size,)), dma((frames,)), dma((frames,)),
            dma((wide,)), dma((wide,)), dma((wide,)), dma((wide,)),
            dma((2 * wide, 2, pols)), dma((2 * wide, 4, pols)), dma((2 * wide, pols)), dma((frames,)), dma((frames,)),
        ],
        compiler_params=pltpu.CompilerParams(collective_id=0, has_side_effects=True, vmem_limit_bytes=60 << 20),
        name="fused_beams",
    )(v, weight_rows, index, mask, taps, *tables)


def body(voltages, filter_taps, use_mask, block_index, weight_blocks):
    stations, pols, frames, _, channels = voltages.shape
    size = lax.axis_size("tm")
    v = voltages.reshape(stations, pols, frames, 2, channels // LANES, LANES).swapaxes(-3, -2)
    v = v.reshape(stations, pols, frames, 2 * channels // LANES, LANES)
    beams = block_index.shape[0]
    power = fused(v, weight_blocks, block_index.T, use_mask.T, filter_taps, transform_tables(channels), size)
    power = power.reshape(channels // 2, beams // LANES, frames, LANES)
    return power.swapaxes(1, 2).reshape(channels // 2, frames, beams)


def solution(mesh):
    in_specs = (
        P(("parts", "stn"), None, "tm", None, None),
        P(),
        P("parts", None),
        P("parts", None),
        P("tm", None),
    )
    out_specs = P("stn", "tm", "parts")
    return jax.shard_map(body, mesh=mesh, in_specs=in_specs, out_specs=out_specs, check_vma=False)
```

```python
import functools
import math

import jax
import jax.numpy as jnp
import numpy as np
from jax import lax
from jax.experimental import pallas as pl
from jax.experimental.pallas import tpu as pltpu
from jax.sharding import PartitionSpec as P

SB = 16
G = 16
LANES = 128
FIRST = 8
KEPT = 3
ROUNDS = 18
MESH = pl.DeviceIdType.MESH


def transform_tables(channels):
    second = channels // FIRST
    parts = second // LANES
    a = np.arange(FIRST)
    l = np.arange(second)

    def waves(product, period):
        angle = (product % period).astype(np.float32) * np.float32(2.0 * math.pi / period)
        return np.cos(angle), np.sin(angle)

    cos, sin = waves(a[:, None] * a[None, :], FIRST)
    one = np.zeros((parts, 2, FIRST, 8, 8, FIRST, parts, 2), np.float32)
    for lh in range(parts):
        for s in range(8):
            one[lh, 0, :, s, s, :, lh, 0] = cos
            one[lh, 0, :, s, s, :, lh, 1] = sin
            one[lh, 1, :, s, s, :, lh, 0] = -sin
            one[lh, 1, :, s, s, :, lh, 1] = cos
    one = one.reshape(parts * 2 * FIRST * 8, 8 * FIRST * parts * 2)
    cos, sin = waves(l[:, None] * l[None, :], second)
    two = np.stack([np.stack([cos, -sin], axis=1), np.stack([sin, cos], axis=1)], axis=0)
    two = two.reshape(2, second, 2, 2, LANES).transpose(0, 1, 3, 2, 4).reshape(2 * second, 2 * second)
    cos, sin = waves(a[:, None] * l[None, :], channels)
    norm = np.float32(1.0 / math.sqrt(channels))
    cos, sin = (
        np.repeat((w * norm).reshape(FIRST, parts, LANES).swapaxes(0, 1), 8, axis=1) for w in (cos, sin))
    return jnp.asarray(one, jnp.bfloat16), jnp.asarray(two, jnp.bfloat16), jnp.asarray(cos), jnp.asarray(sin)


def schedule(frames):
    wide = 2 * frames

    def orders(filters, early, beams, right, left):
        rows = []
        had = [0, 0]
        for j in range(ROUNDS):
            here = [d for k, d in filters if k == j]
            need = list(had)
            for d in here:
                need = [max(need[0], right(d)), max(need[1], left(d))]
            sent = [d for k, d in early if k == j]
            done = [d for k, d in beams if k == j]
            word = 0
            for d in (here + [-1])[:1] + (sent + [-1, -1])[:2] + (done + [-1])[:1]:
                word = word * 32 + d + 1
            rows.append((word, ((had[0] * 16 + need[0]) * 16 + had[1]) * 16 + need[1]))
            had = need
        return rows

    def right(d):
        return max(d - wide + 1, 0)

    def left(most):
        return lambda d: min(max(2 * wide - 1 - d, 0), most)

    def placed(first, order):
        return [(first + k, d) for k, d in enumerate(order)]

    head = placed(0, [0, 1, 2, 3, 4, 8, 12, 9, 13, 10, 5, 14, 6, 7])
    sent = [(0, 0)] + placed(4, [4, 8, 12, 9, 13, 10, 1, 14, 6, 7]) + [(11, 5), (12, 2), (13, 3)]
    shift = [11, 12, 10, 13, 9, 8, 14, 15]
    both = placed(4, shift + [3, 7])
    only = placed(4, shift)
    zero = lambda d: 0
    upper = [(8, 11), (10, 10), (11, 9), (13, 8)]
    lower = [(8, 12), (10, 13), (12, 14), (14, 15)]
    return [
        [orders(head, sent, [(7, 0), (9, 8), (11, 9), (13, 10), (14, 1), (15, 2), (16, 3)], right, zero),
         orders(head, sent, [(8, 4), (10, 12), (12, 13), (14, 14), (15, 5), (16, 6), (17, 7)], right, zero)],
        [orders(both, both, upper + [(14, 3)], right, left(wide)),
         orders(both, both, lower + [(15, 7)], right, left(wide))],
        [orders(only, only, upper, right, left(wide - 1)),
         orders(only, only, lower, right, left(wide - 1))],
    ]


def kernel(size, v_ref, rows_ref, index_ref, mask_ref, taps_ref, one_ref, two_ref, cos_ref, sin_ref, out_ref,
           x, taps, held, tw, z, r, table, weights, turned, given, taken,
           local, send_w, recv_w, send_y, recv_y, send_l, recv_l, send_r, recv_r, send_z, recv_z, own_z, send_p, recv_p):
    me = lax.axis_index("tm")
    core = lax.axis_index("stn")
    col = me // 2
    y = lax.rem(me, 2)
    cols = size // 2
    frames = v_ref.shape[2]
    wide = 2 * frames
    depth = taps_ref.shape[0]
    base = depth - 1
    pols = v_ref.shape[1]
    share = v_ref.shape[0] // 2
    groups, _, beams2 = weights.shape
    beams = beams2 // 2
    lows = LANES // groups
    bf16 = jnp.bfloat16
    f32 = jnp.float32
    place = 2 * core + y

    barrier = pltpu.get_barrier_semaphore()
    for step in range(size):
        for side in range(2):
            if step or side:
                pl.semaphore_signal(
                    barrier, inc=1, device_id={"tm": lax.rem(me + step, size), "stn": lax.rem(core + side, 2)},
                    device_id_type=MESH)
    pl.semaphore_wait(barrier, 2 * size - 1)

    first_col = col == 0
    second_col = col == 1
    mid = (col > 0) & (col < cols - 1)
    has_left = col > 0
    to_right = col < cols - 2

    def weight_copy(step):
        return pltpu.make_async_remote_copy(
            src_ref=rows_ref, dst_ref=table.at[me], send_sem=send_w.at[step], recv_sem=recv_w.at[step],
            device_id={"tm": lax.rem(me + step, size)}, device_id_type=MESH)

    def mine(half, j):
        return v_ref.at[pl.ds(half * share, share), :, j]

    def swap_sent(n):
        return jnp.where(y == 0, n, wide - 1 - n)

    def swap_got(n):
        return jnp.where(y == 0, wide - 1 - n, n)

    def swap_copy(n):
        o = swap_sent(n)
        return pltpu.make_async_remote_copy(
            src_ref=mine(1 - y, lax.rem(o, frames)), dst_ref=x.at[base + o], send_sem=send_y.at[n], recv_sem=recv_y.at[n],
            device_id={"tm": 2 * col + 1 - y}, device_id_type=MESH)

    def left_copy(o, src):
        return pltpu.make_async_remote_copy(
            src_ref=src, dst_ref=x.at[base + wide + o], send_sem=send_l.at[o], recv_sem=recv_r.at[o],
            device_id={"tm": me - 2}, device_id_type=MESH)

    def right_copy(o, src):
        return pltpu.make_async_remote_copy(
            src_ref=src, dst_ref=x.at[base - wide + o], send_sem=send_r.at[o], recv_sem=recv_l.at[o],
            device_id={"tm": me + 2}, device_id_type=MESH)

    def own_src(o):
        return mine(y, o % frames)

    def got_src(o):
        return x.at[base + o]

    def power_copy(i):
        return pltpu.make_async_remote_copy(
            src_ref=given.at[i], dst_ref=taken.at[i], send_sem=send_p.at[i], recv_sem=recv_p.at[i],
            device_id={"tm": me + 2}, device_id_type=MESH)

    def own_copy(j):
        return pltpu.make_async_copy(mine(y, j), x.at[base + y * frames + j], local.at[j])

    for step in range(1, size):
        weight_copy(step).start()
    for n in range(frames):
        swap_copy(n).start()

    @pl.when(has_left & (y == 0))
    def _():
        for o in range(frames):
            left_copy(o, own_src(o)).start()

    @pl.when(has_left & (y == 1))
    def _():
        left_copy(frames, own_src(frames)).start()

    @pl.when(to_right & (y == 0))
    def _():
        right_copy(frames - 1, own_src(frames - 1)).start()

    @pl.when(to_right & (y == 1))
    def _():
        for o in range(wide - 1, frames - 1, -1):
            right_copy(o, own_src(o)).start()

    for j in range(frames):
        own_copy(j).start()
    keep = pltpu.make_async_copy(rows_ref, table.at[me], local.at[frames])
    keep.start()

    def clear(n, carry):
        x[n] = jnp.zeros(x.shape[1:], x.dtype)
        return carry
    lax.fori_loop(0, jnp.where(first_col, base, jnp.where(second_col, base - wide, 0)), clear, 0)

    for a in range(taps.shape[1] // 2):
        piece = taps_ref[:, a * LANES:(a + 1) * LANES]
        taps[:, 2 * a, :] = piece
        taps[:, 2 * a + 1, :] = piece

    for step in range(1, size):
        weight_copy(step).wait_recv()
    keep.wait()
    width = groups * 2 * SB
    entries = table[:, :, pl.ds(pl.multiple_of(core * width, width), width)].reshape(-1, width)
    entries = entries.astype(f32).T.astype(bf16)
    ids = lax.broadcasted_iota(jnp.int32, (entries.shape[1], beams), 0)
    stations = index_ref.shape[0] * SB
    for q in range(index_ref.shape[0]):
        onehot = jnp.where(ids == index_ref[q:q + 1, :], mask_ref[q:q + 1, :], 0).astype(f32).astype(bf16)
        picked = jnp.dot(entries, onehot, preferred_element_type=f32)
        for g in range(groups):
            low = 2 * g * SB
            re = picked[low:low + SB]
            im = picked[low + SB:low + 2 * SB]
            weights[g, q * SB:(q + 1) * SB, :beams] = re.astype(bf16)
            weights[g, q * SB:(q + 1) * SB, beams:] = im.astype(bf16)
            weights[g, stations + q * SB:stations + (q + 1) * SB, :beams] = (-im).astype(bf16)
            weights[g, stations + q * SB:stations + (q + 1) * SB, beams:] = re.astype(bf16)
    for j in range(frames):
        own_copy(j).wait()

    plans = schedule(frames)

    def look(j):
        words = []
        for k in range(2):
            kinds = []
            for kind in plans:
                sides = []
                for rows in kind:
                    word = jnp.int32(0)
                    for step, row in enumerate(rows):
                        if row[k]:
                            word = jnp.where(j == step, row[k], word)
                    sides.append(word)
                kinds.append(jnp.where(y == 0, sides[0], sides[1]))
            words.append(jnp.where(first_col, kinds[0], jnp.where(second_col, kinds[1], jnp.where(mid, kinds[2], 0))))
        ops, waits = words
        ops = [lax.rem(ops // 32 ** n, 32) - 1 for n in (3, 2, 1, 0)]
        waits = [lax.rem(waits // 16 ** n, 16) for n in (3, 2, 1, 0)]
        return ops, waits

    def busy(d):
        stays = d < wide
        near = lax.rem(d, frames) < KEPT
        return (first_col & (stays | near)) | (second_col & jnp.logical_not(stays & near)) | (
            mid & jnp.logical_not(second_col | stays))

    def plan(d):
        owner = lax.rem(d // frames, 2)
        bank = d // wide * frames + lax.rem(d, frames)
        return owner, bank

    def spectra_copy(i, h, p, owner, bank):
        return pltpu.make_async_remote_copy(
            src_ref=z.at[i, h, p], dst_ref=r.at[bank, p, :, :, pl.ds(place * share, share), :],
            send_sem=send_z.at[i, h, p], recv_sem=recv_z.at[i, place, p],
            device_id={"tm": 2 * col + owner, "stn": h}, device_id_type=MESH)

    def spectra_keep(i, h, p, bank):
        return pltpu.make_async_copy(
            z.at[i, h, p], r.at[bank, p, :, :, pl.ds(place * share, share), :], own_z.at[i, p])

    def spectra_wait(i, where, p, bank):
        return pltpu.make_async_remote_copy(
            src_ref=z.at[i, 0, p], dst_ref=r.at[bank, p, :, :, pl.ds(where * share, share), :],
            send_sem=send_z.at[i, 0, p], recv_sem=recv_z.at[i, where, p],
            device_id={"tm": 2 * col + 1 - y}, device_id_type=MESH)

    def forward(n):
        swap_copy(n).wait_recv()
        o = swap_got(n)

        @pl.when(to_right & (y == 0))
        def _():
            right_copy(o, got_src(o)).start()

        @pl.when(has_left & (y == 1))
        def _():
            left_copy(o, got_src(o)).start()

        @pl.when((n == frames - 1) & has_left & (y == 0))
        def _():
            for o in range(frames, frames + KEPT):
                left_copy(o, got_src(o)).start()

            @pl.when(col > 1)
            def _():
                for o in range(frames + KEPT, wide):
                    left_copy(o, got_src(o)).start()

        @pl.when((n == frames - 1) & has_left & (y == 1))
        def _():
            for o in range(frames + 1, frames + KEPT):
                left_copy(o, own_src(o)).start()

            @pl.when(col > 1)
            def _():
                for o in range(frames + KEPT, wide):
                    left_copy(o, own_src(o)).start()

        @pl.when((n == frames - 1) & to_right & (y == 0))
        def _():
            for o in range(frames - 2, 0, -1):
                right_copy(o, own_src(o)).start()

            @pl.when(first_col)
            def _():
                right_copy(0, own_src(0)).start()

        @pl.when((n == frames - 1) & to_right & (y == 1))
        def _():
            for o in range(frames - 1, 0, -1):
                right_copy(o, got_src(o)).start()

            @pl.when(first_col)
            def _():
                right_copy(0, got_src(0)).start()

    def wait_right(o):
        left_copy(o, got_src(0)).wait_recv()

    def wait_left(o):
        right_copy(o, got_src(0)).wait_recv()

    halves = 2

    def channelize(i):
        slot = base + i

        def filter_rows(n, carry):
            quad = n // halves
            rows = pl.ds(pl.multiple_of(lax.rem(n, halves) * 16, 16), 16)
            sums = [None] * (4 * pols)
            for k in range(depth):
                tap = taps[k, rows, :]
                for m in range(4):
                    for p in range(pols):
                        term = tap * x[slot - k, quad * 4 + m, p, rows, :].astype(f32)
                        j = m * pols + p
                        sums[j] = term if k == 0 else sums[j] + term
            for m in range(4):
                for p in range(pols):
                    row = (lax.rem(quad, 2) * 4 + m) * 32 + lax.rem(n, halves) * 16
                    held[quad // 2, pl.ds(pl.multiple_of(row, 16), 16), p * LANES:(p + 1) * LANES] = (
                        sums[m * pols + p].astype(bf16))
            return carry
        lax.fori_loop(0, share // 4 * halves, filter_rows, 0)

        batches = share // 8
        block = FIRST * 8
        for b in range(batches):
            spread = jnp.dot(one_ref[...], held[b], preferred_element_type=f32)
            for lh in range(2):
                cos, sin = cos_ref[lh], sin_ref[lh]
                for p in range(pols):
                    re = spread[2 * lh * block:(2 * lh + 1) * block, p * LANES:(p + 1) * LANES]
                    im = spread[(2 * lh + 1) * block:(2 * lh + 2) * block, p * LANES:(p + 1) * LANES]
                    tw[p, b * block:(b + 1) * block, lh * LANES:(lh + 1) * LANES] = (re * cos + im * sin).astype(bf16)
                    tw[p, b * block:(b + 1) * block, (2 + lh) * LANES:(3 + lh) * LANES] = (
                        im * cos - re * sin).astype(bf16)
        for p in range(pols):
            for h in range(2):
                spectra = jnp.dot(
                    tw[p], two_ref[:, h * 2 * LANES:(h + 1) * 2 * LANES], preferred_element_type=f32)
                for k1 in range(FIRST):
                    rows = jnp.concatenate(
                        [spectra[b * block + k1 * 8:b * block + (k1 + 1) * 8] for b in range(batches)], axis=0).astype(bf16)
                    for part in range(2):
                        z[i, h, p, k1, part] = rows[:, part * LANES:(part + 1) * LANES]

    def share_out(i):
        owner, bank = plan(i)
        for p in range(pols):
            for h in range(2):
                stay = (owner == y) & (core == h)

                @pl.when(stay)
                def _():
                    spectra_keep(i, h, p, bank).start()

                @pl.when(jnp.logical_not(stay))
                def _():
                    spectra_copy(i, h, p, owner, bank).start()

    def beamform(i):
        _, bank = plan(i)
        for p in range(pols):
            for where in range(4):
                @pl.when(place == where)
                def _():
                    spectra_keep(i, core, p, bank).wait()

                @pl.when(place != where)
                def _():
                    spectra_wait(i, where, p, bank).wait_recv()

        def turn(k1, carry):
            for p in range(pols):
                for part in range(2):
                    tile = r[bank, p, k1, part].T
                    for g in range(groups):
                        turned[p, g, pl.ds(pl.multiple_of(k1 * lows, lows), lows), part * LANES:(part + 1) * LANES] = (
                            tile[g * lows:(g + 1) * lows])
            return carry
        lax.fori_loop(0, FIRST, turn, 0)

        stays = i < wide
        at = lax.rem(bank, frames)

        def group(g, carry):
            power = None
            for p in range(pols):
                beam = jnp.dot(turned[p, g], weights[g], preferred_element_type=f32)
                term = beam[:, :beams] * beam[:, :beams] + beam[:, beams:] * beam[:, beams:]
                power = term if p == 0 else power + term
            power = power.astype(bf16)
            rows = pl.ds(pl.multiple_of(g * LANES, LANES), LANES)

            @pl.when(stays)
            def _():
                taken[at, rows, :] = power

            @pl.when(jnp.logical_not(stays))
            def _():
                given[at, rows, :] = power
            return carry
        lax.fori_loop(0, groups, group, 0)

        @pl.when(jnp.logical_not(stays))
        def _():
            power_copy(at).start()

    def round_(j, carry):
        (made, sent, also, late), (right_from, right_to, left_from, left_to) = look(j)

        @pl.when(j < frames)
        def _():
            forward(j)

        @pl.when(made >= 0)
        def _():
            def from_right(o, carry):
                wait_right(o)
                return carry
            lax.fori_loop(right_from, right_to, from_right, 0)

            def from_left(n, carry):
                wait_left(wide - 1 - n)
                return carry
            lax.fori_loop(left_from, left_to, from_left, 0)
            channelize(made)

        @pl.when(sent >= 0)
        def _():
            share_out(sent)

        @pl.when(also >= 0)
        def _():
            share_out(also)

        @pl.when(late >= 0)
        def _():
            beamform(late)
        return carry
    lax.fori_loop(0, ROUNDS, round_, 0)

    pieces = beams // LANES
    pitch = pieces * frames

    def finish(n, carry):
        down = (col > 1) & (y == 0)
        f = jnp.where(down, frames - 1 - n, n)

        @pl.when(has_left & ((col > 1) | (f < KEPT)))
        def _():
            power_copy(f).wait_recv()

        def spread(g, carry):
            for k1 in range(FIRST):
                rows = taken[f, pl.ds(pl.multiple_of(g * LANES + k1 * lows, lows), lows), :].astype(f32)
                for half in range(lows // 8):
                    for piece in range(pieces):
                        row = g * (LANES * pitch) + (half * 8 * FIRST + k1) * pitch + piece * frames + f
                        out_ref[pl.ds(row, 8, stride=FIRST * pitch), :] = (
                            rows[half * 8:(half + 1) * 8, piece * LANES:(piece + 1) * LANES])
            return carry
        lax.fori_loop(0, groups, spread, 0)
        return carry
    lax.fori_loop(0, frames, finish, 0)

    for step in range(1, size):
        weight_copy(step).wait_send()
    for n in range(frames):
        swap_copy(n).wait_send()

    @pl.when(has_left)
    def _():
        for o in range(frames + KEPT):
            left_copy(o, got_src(0)).wait_send()

        @pl.when(col > 1)
        def _():
            for o in range(frames + KEPT, wide):
                left_copy(o, got_src(0)).wait_send()

    @pl.when(to_right)
    def _():
        for o in range(1, wide):
            right_copy(o, got_src(0)).wait_send()

        @pl.when(first_col)
        def _():
            right_copy(0, got_src(0)).wait_send()

    for n in range(frames):
        @pl.when(mid | (first_col & (n < KEPT)))
        def _():
            power_copy(n).wait_send()

    def drain(i, carry):
        @pl.when(busy(i))
        def _():
            owner, bank = plan(i)
            for h in range(2):
                @pl.when(jnp.logical_not((owner == y) & (core == h)))
                def _():
                    for p in range(pols):
                        spectra_copy(i, h, p, owner, bank).wait_send()
        return carry
    lax.fori_loop(0, 2 * wide, drain, 0)


def fused(v, weight_rows, index, mask, taps, tables, size):
    stations, pols, frames, rows, _ = v.shape
    share = stations // 2
    groups = G // 2
    beams = index.shape[1]
    depth, channels = taps.shape
    wide = 2 * frames
    bf16 = jnp.bfloat16
    dma = pltpu.SemaphoreType.DMA
    vmem = pl.BlockSpec(memory_space=pltpu.VMEM)
    hbm = pl.BlockSpec(memory_space=pl.ANY)
    return pl.pallas_call(
        functools.partial(kernel, size),
        out_shape=jax.ShapeDtypeStruct((channels // 2 * frames * beams // LANES, LANES), jnp.float32),
        in_specs=[hbm] + [vmem] * 8,
        out_specs=vmem,
        scratch_shapes=[
            pltpu.VMEM((depth - 1 + 2 * wide, share, pols, rows, LANES), bf16),
            pltpu.VMEM((depth, rows, LANES), jnp.float32),
            pltpu.VMEM((share // 8, 8 * rows, pols * LANES), bf16),
            pltpu.VMEM((pols, FIRST * share, 4 * LANES), bf16),
            pltpu.VMEM((2 * wide, 2, pols, FIRST, 2, share, LANES), bf16),
            pltpu.VMEM((wide, pols, FIRST, 2, 4 * share, LANES), bf16),
            pltpu.VMEM((size,) + weight_rows.shape, bf16),
            pltpu.VMEM((groups, 8 * share, 2 * beams), bf16),
            pltpu.VMEM((pols, groups, LANES, 2 * LANES), bf16),
            pltpu.VMEM((frames, channels // 2, beams), bf16),
            pltpu.VMEM((frames, channels // 2, beams), bf16),
            dma((frames + 1,)), dma((size,)), dma((size,)), dma((frames,)), dma((frames,)),
            dma((wide,)), dma((wide,)), dma((wide,)), dma((wide,)),
            dma((2 * wide, 2, pols)), dma((2 * wide, 4, pols)), dma((2 * wide, pols)), dma((frames,)), dma((frames,)),
        ],
        compiler_params=pltpu.CompilerParams(collective_id=0, has_side_effects=True, vmem_limit_bytes=60 << 20),
        name="fused_beams",
    )(v, weight_rows, index, mask, taps, *tables)


def body(voltages, filter_taps, use_mask, block_index, weight_blocks):
    stations, pols, frames, _, channels = voltages.shape
    size = lax.axis_size("tm")
    v = voltages.reshape(stations, pols, frames, 2, channels // LANES, LANES).swapaxes(-3, -2)
    v = v.reshape(stations, pols, frames, 2 * channels // LANES, LANES)
    beams = block_index.shape[0]
    power = fused(v, weight_blocks, block_index.T, use_mask.T, filter_taps, transform_tables(channels), size)
    power = power.reshape(channels // 2, beams // LANES, frames, LANES)
    return power.swapaxes(1, 2).reshape(channels // 2, frames, beams)


def solution(mesh):
    in_specs = (
        P(("parts", "stn"), None, "tm", None, None),
        P(),
        P("parts", None),
        P("parts", None),
        P("tm", None),
    )
    out_specs = P("stn", "tm", "parts")
    return jax.shard_map(body, mesh=mesh, in_specs=in_specs, out_specs=out_specs, check_vma=False)
```

```python
import functools
import math

import jax
import jax.numpy as jnp
import numpy as np
from jax import lax
from jax.experimental import pallas as pl
from jax.experimental.pallas import tpu as pltpu
from jax.sharding import PartitionSpec as P

SB = 16
G = 16
LANES = 128
FIRST = 8
KEPT = 3
ROUNDS = 17
MESH = pl.DeviceIdType.MESH


def transform_tables(channels):
    second = channels // FIRST
    parts = second // LANES
    a = np.arange(FIRST)
    l = np.arange(second)

    def waves(product, period):
        angle = (product % period).astype(np.float32) * np.float32(2.0 * math.pi / period)
        return np.cos(angle), np.sin(angle)

    cos, sin = waves(a[:, None] * a[None, :], FIRST)
    one = np.zeros((parts, 2, FIRST, 8, 8, FIRST, parts, 2), np.float32)
    for lh in range(parts):
        for s in range(8):
            one[lh, 0, :, s, s, :, lh, 0] = cos
            one[lh, 0, :, s, s, :, lh, 1] = sin
            one[lh, 1, :, s, s, :, lh, 0] = -sin
            one[lh, 1, :, s, s, :, lh, 1] = cos
    one = one.reshape(parts * 2 * FIRST * 8, 8 * FIRST * parts * 2)
    cos, sin = waves(l[:, None] * l[None, :], second)
    two = np.stack([np.stack([cos, -sin], axis=1), np.stack([sin, cos], axis=1)], axis=0)
    two = two.reshape(2, second, 2, 2, LANES).transpose(0, 1, 3, 2, 4).reshape(2 * second, 2 * second)
    cos, sin = waves(a[:, None] * l[None, :], channels)
    norm = np.float32(1.0 / math.sqrt(channels))
    cos, sin = (
        np.repeat((w * norm).reshape(FIRST, parts, LANES).swapaxes(0, 1), 8, axis=1) for w in (cos, sin))
    return jnp.asarray(one, jnp.bfloat16), jnp.asarray(two, jnp.bfloat16), jnp.asarray(cos), jnp.asarray(sin)


def schedule(frames):
    wide = 2 * frames

    def orders(filters, early, beams, right, left):
        rows = []
        had = [0, 0]
        for j in range(ROUNDS):
            here = [d for k, d in filters if k == j]
            need = list(had)
            for d in here:
                need = [max(need[0], right(d)), max(need[1], left(d))]
            sent = [d for k, d in early if k == j]
            done = [d for k, d in beams if k == j]
            word = 0
            for d in (here + [-1])[:1] + (sent + [-1, -1])[:2] + (done + [-1])[:1]:
                word = word * 32 + d + 1
            rows.append((word, ((had[0] * 16 + need[0]) * 16 + had[1]) * 16 + need[1]))
            had = need
        return rows

    def right(d):
        return max(d - wide + 1, 0)

    def left(most):
        return lambda d: min(max(2 * wide - 1 - d, 0), most)

    def placed(first, order):
        return [(first + k, d) for k, d in enumerate(order)]

    upper_head = placed(0, [4, 5, 6, 7, 0, 8, 12, 9, 13, 10, 1, 14, 2, 3])
    lower_head = placed(0, [0, 1, 2, 3, 8, 9, 12, 10, 13, 4, 5, 14, 6, 7])
    upper_sent = [(0, 4), (1, 5)] + placed(4, [0, 8, 12, 9, 13, 10, 1, 14, 2, 3]) + [(11, 6), (12, 7)]
    lower_sent = [(0, 0)] + placed(4, [8, 9, 12, 10, 13, 4, 5, 14, 6, 7]) + placed(8, [1, 2, 3])
    upper_done = [(7, 0), (9, 8), (11, 9), (13, 10), (14, 1), (15, 2), (16, 3)]
    lower_done = [(10, 4), (11, 12), (12, 13), (13, 5), (14, 14), (15, 6), (16, 7)]
    shift = [11, 12, 10, 13, 9, 8, 14, 15]
    both = placed(4, shift + [3, 7])
    only = placed(4, shift)
    zero = lambda d: 0
    upper = [(8, 11), (10, 10), (11, 9), (13, 8)]
    lower = [(8, 12), (10, 13), (12, 14), (14, 15)]
    return [
        [orders(upper_head, upper_sent, upper_done, right, zero),
         orders(lower_head, lower_sent, lower_done, right, zero)],
        [orders(both, both, upper + [(14, 3)], right, left(wide)),
         orders(both, both, lower + [(15, 7)], right, left(wide))],
        [orders(only, only, upper, right, left(wide - 1)),
         orders(only, only, lower, right, left(wide - 1))],
    ]


def kernel(size, v_ref, rows_ref, index_ref, mask_ref, taps_ref, one_ref, two_ref, cos_ref, sin_ref, out_ref,
           x, taps, held, tw, z, r, table, weights, turned, given, taken,
           local, send_w, recv_w, send_y, recv_y, send_l, recv_l, send_r, recv_r, send_z, recv_z, own_z, send_p, recv_p):
    me = lax.axis_index("tm")
    core = lax.axis_index("stn")
    col = me // 2
    y = lax.rem(me, 2)
    cols = size // 2
    frames = v_ref.shape[2]
    wide = 2 * frames
    depth = taps_ref.shape[0]
    base = depth - 1
    pols = v_ref.shape[1]
    share = v_ref.shape[0] // 2
    groups, _, beams2 = weights.shape
    beams = beams2 // 2
    lows = LANES // groups
    bf16 = jnp.bfloat16
    f32 = jnp.float32
    place = 2 * core + y

    barrier = pltpu.get_barrier_semaphore()
    for step in range(size):
        for side in range(2):
            if step or side:
                pl.semaphore_signal(
                    barrier, inc=1, device_id={"tm": lax.rem(me + step, size), "stn": lax.rem(core + side, 2)},
                    device_id_type=MESH)
    pl.semaphore_wait(barrier, 2 * size - 1)

    first_col = col == 0
    second_col = col == 1
    mid = (col > 0) & (col < cols - 1)
    has_left = col > 0
    to_right = col < cols - 2

    def weight_copy(step):
        return pltpu.make_async_remote_copy(
            src_ref=rows_ref, dst_ref=table.at[me], send_sem=send_w.at[step], recv_sem=recv_w.at[step],
            device_id={"tm": lax.rem(me + step, size)}, device_id_type=MESH)

    def mine(half, j):
        return v_ref.at[pl.ds(half * share, share), :, j]

    def swap_sent(n):
        return y * frames + n

    def swap_got(n):
        return (1 - y) * frames + n

    def swap_copy(n):
        o = swap_sent(n)
        return pltpu.make_async_remote_copy(
            src_ref=mine(1 - y, lax.rem(o, frames)), dst_ref=x.at[base + o], send_sem=send_y.at[n], recv_sem=recv_y.at[n],
            device_id={"tm": 2 * col + 1 - y}, device_id_type=MESH)

    def left_copy(o, src):
        return pltpu.make_async_remote_copy(
            src_ref=src, dst_ref=x.at[base + wide + o], send_sem=send_l.at[o], recv_sem=recv_r.at[o],
            device_id={"tm": me - 2}, device_id_type=MESH)

    def right_copy(o, src):
        return pltpu.make_async_remote_copy(
            src_ref=src, dst_ref=x.at[base - wide + o], send_sem=send_r.at[o], recv_sem=recv_l.at[o],
            device_id={"tm": me + 2}, device_id_type=MESH)

    def own_src(o):
        return mine(y, o % frames)

    def got_src(o):
        return x.at[base + o]

    def power_copy(i):
        return pltpu.make_async_remote_copy(
            src_ref=given.at[i], dst_ref=taken.at[i], send_sem=send_p.at[i], recv_sem=recv_p.at[i],
            device_id={"tm": me + 2}, device_id_type=MESH)

    def own_copy(j):
        return pltpu.make_async_copy(mine(y, j), x.at[base + y * frames + j], local.at[j])

    for step in range(1, size):
        weight_copy(step).start()
    for n in range(frames):
        swap_copy(n).start()

    @pl.when(has_left & (y == 0))
    def _():
        for o in range(frames):
            left_copy(o, own_src(o)).start()

    @pl.when(has_left & (y == 1))
    def _():
        left_copy(frames, own_src(frames)).start()

    @pl.when(to_right & (y == 0))
    def _():
        right_copy(frames - 1, own_src(frames - 1)).start()

    @pl.when(to_right & (y == 1))
    def _():
        for o in range(wide - 1, frames - 1, -1):
            right_copy(o, own_src(o)).start()

    for j in range(frames):
        own_copy(j).start()
    keep = pltpu.make_async_copy(rows_ref, table.at[me], local.at[frames])
    keep.start()

    def clear(n, carry):
        x[n] = jnp.zeros(x.shape[1:], x.dtype)
        return carry
    lax.fori_loop(0, jnp.where(first_col, base, jnp.where(second_col, base - wide, 0)), clear, 0)

    for a in range(taps.shape[1] // 2):
        piece = taps_ref[:, a * LANES:(a + 1) * LANES]
        taps[:, 2 * a, :] = piece
        taps[:, 2 * a + 1, :] = piece

    for step in range(1, size):
        weight_copy(step).wait_recv()
    keep.wait()
    width = groups * 2 * SB
    entries = table[:, :, pl.ds(pl.multiple_of(core * width, width), width)].reshape(-1, width)
    entries = entries.astype(f32).T.astype(bf16)
    ids = lax.broadcasted_iota(jnp.int32, (entries.shape[1], beams), 0)
    stations = index_ref.shape[0] * SB
    for q in range(index_ref.shape[0]):
        onehot = jnp.where(ids == index_ref[q:q + 1, :], mask_ref[q:q + 1, :], 0).astype(f32).astype(bf16)
        picked = jnp.dot(entries, onehot, preferred_element_type=f32)
        for g in range(groups):
            low = 2 * g * SB
            re = picked[low:low + SB]
            im = picked[low + SB:low + 2 * SB]
            weights[g, q * SB:(q + 1) * SB, :beams] = re.astype(bf16)
            weights[g, q * SB:(q + 1) * SB, beams:] = im.astype(bf16)
            weights[g, stations + q * SB:stations + (q + 1) * SB, :beams] = (-im).astype(bf16)
            weights[g, stations + q * SB:stations + (q + 1) * SB, beams:] = re.astype(bf16)
    for j in range(frames):
        own_copy(j).wait()

    plans = schedule(frames)

    def look(j):
        words = []
        for k in range(2):
            kinds = []
            for kind in plans:
                sides = []
                for rows in kind:
                    word = jnp.int32(0)
                    for step, row in enumerate(rows):
                        if row[k]:
                            word = jnp.where(j == step, row[k], word)
                    sides.append(word)
                kinds.append(jnp.where(y == 0, sides[0], sides[1]))
            words.append(jnp.where(first_col, kinds[0], jnp.where(second_col, kinds[1], jnp.where(mid, kinds[2], 0))))
        ops, waits = words
        ops = [lax.rem(ops // 32 ** n, 32) - 1 for n in (3, 2, 1, 0)]
        waits = [lax.rem(waits // 16 ** n, 16) for n in (3, 2, 1, 0)]
        return ops, waits

    def busy(d):
        stays = d < wide
        near = lax.rem(d, frames) < KEPT
        return (first_col & (stays | near)) | (second_col & jnp.logical_not(stays & near)) | (
            mid & jnp.logical_not(second_col | stays))

    def plan(d):
        owner = lax.rem(d // frames, 2)
        bank = d // wide * frames + lax.rem(d, frames)
        return owner, bank

    def spectra_copy(i, h, p, owner, bank):
        return pltpu.make_async_remote_copy(
            src_ref=z.at[i, h, p], dst_ref=r.at[bank, p, :, :, pl.ds(place * share, share), :],
            send_sem=send_z.at[i, h, p], recv_sem=recv_z.at[i, place, p],
            device_id={"tm": 2 * col + owner, "stn": h}, device_id_type=MESH)

    def spectra_keep(i, h, p, bank):
        return pltpu.make_async_copy(
            z.at[i, h, p], r.at[bank, p, :, :, pl.ds(place * share, share), :], own_z.at[i, p])

    def spectra_wait(i, where, p, bank):
        return pltpu.make_async_remote_copy(
            src_ref=z.at[i, 0, p], dst_ref=r.at[bank, p, :, :, pl.ds(where * share, share), :],
            send_sem=send_z.at[i, 0, p], recv_sem=recv_z.at[i, where, p],
            device_id={"tm": 2 * col + 1 - y}, device_id_type=MESH)

    def forward(n):
        swap_copy(n).wait_recv()
        o = swap_got(n)

        @pl.when(to_right & (y == 0))
        def _():
            right_copy(o, got_src(o)).start()

        @pl.when(has_left & (y == 1))
        def _():
            left_copy(o, got_src(o)).start()

        @pl.when((n == frames - 1) & has_left & (y == 0))
        def _():
            for o in range(frames, frames + KEPT):
                left_copy(o, got_src(o)).start()

            @pl.when(col > 1)
            def _():
                for o in range(frames + KEPT, wide):
                    left_copy(o, got_src(o)).start()

        @pl.when((n == frames - 1) & has_left & (y == 1))
        def _():
            for o in range(frames + 1, frames + KEPT):
                left_copy(o, own_src(o)).start()

            @pl.when(col > 1)
            def _():
                for o in range(frames + KEPT, wide):
                    left_copy(o, own_src(o)).start()

        @pl.when((n == frames - 1) & to_right & (y == 0))
        def _():
            for o in range(frames - 2, 0, -1):
                right_copy(o, own_src(o)).start()

            @pl.when(first_col)
            def _():
                right_copy(0, own_src(0)).start()

        @pl.when((n == frames - 1) & to_right & (y == 1))
        def _():
            for o in range(frames - 1, 0, -1):
                right_copy(o, got_src(o)).start()

            @pl.when(first_col)
            def _():
                right_copy(0, got_src(0)).start()

    def wait_right(o):
        left_copy(o, got_src(0)).wait_recv()

    def wait_left(o):
        right_copy(o, got_src(0)).wait_recv()

    halves = 2

    def channelize(i):
        slot = base + i

        def filter_rows(n, carry):
            quad = n // halves
            rows = pl.ds(pl.multiple_of(lax.rem(n, halves) * 16, 16), 16)
            sums = [None] * (4 * pols)
            for k in range(depth):
                tap = taps[k, rows, :]
                for m in range(4):
                    for p in range(pols):
                        term = tap * x[slot - k, quad * 4 + m, p, rows, :].astype(f32)
                        j = m * pols + p
                        sums[j] = term if k == 0 else sums[j] + term
            for m in range(4):
                for p in range(pols):
                    row = (lax.rem(quad, 2) * 4 + m) * 32 + lax.rem(n, halves) * 16
                    held[quad // 2, pl.ds(pl.multiple_of(row, 16), 16), p * LANES:(p + 1) * LANES] = (
                        sums[m * pols + p].astype(bf16))
            return carry
        lax.fori_loop(0, share // 4 * halves, filter_rows, 0)

        batches = share // 8
        block = FIRST * 8
        for b in range(batches):
            spread = jnp.dot(one_ref[...], held[b], preferred_element_type=f32)
            for lh in range(2):
                cos, sin = cos_ref[lh], sin_ref[lh]
                for p in range(pols):
                    re = spread[2 * lh * block:(2 * lh + 1) * block, p * LANES:(p + 1) * LANES]
                    im = spread[(2 * lh + 1) * block:(2 * lh + 2) * block, p * LANES:(p + 1) * LANES]
                    tw[p, b * block:(b + 1) * block, lh * LANES:(lh + 1) * LANES] = (re * cos + im * sin).astype(bf16)
                    tw[p, b * block:(b + 1) * block, (2 + lh) * LANES:(3 + lh) * LANES] = (
                        im * cos - re * sin).astype(bf16)
        for p in range(pols):
            for h in range(2):
                spectra = jnp.dot(
                    tw[p], two_ref[:, h * 2 * LANES:(h + 1) * 2 * LANES], preferred_element_type=f32)
                for k1 in range(FIRST):
                    rows = jnp.concatenate(
                        [spectra[b * block + k1 * 8:b * block + (k1 + 1) * 8] for b in range(batches)], axis=0).astype(bf16)
                    for part in range(2):
                        z[i, h, p, k1, part] = rows[:, part * LANES:(part + 1) * LANES]

    def share_out(i):
        owner, bank = plan(i)
        for p in range(pols):
            for h in range(2):
                stay = (owner == y) & (core == h)

                @pl.when(stay)
                def _():
                    spectra_keep(i, h, p, bank).start()

                @pl.when(jnp.logical_not(stay))
                def _():
                    spectra_copy(i, h, p, owner, bank).start()

    def beamform(i):
        _, bank = plan(i)
        for p in range(pols):
            for where in range(4):
                @pl.when(place == where)
                def _():
                    spectra_keep(i, core, p, bank).wait()

                @pl.when(place != where)
                def _():
                    spectra_wait(i, where, p, bank).wait_recv()

        def turn(k1, carry):
            for p in range(pols):
                for part in range(2):
                    tile = r[bank, p, k1, part].T
                    for g in range(groups):
                        turned[p, g, pl.ds(pl.multiple_of(k1 * lows, lows), lows), part * LANES:(part + 1) * LANES] = (
                            tile[g * lows:(g + 1) * lows])
            return carry
        lax.fori_loop(0, FIRST, turn, 0)

        stays = i < wide
        at = lax.rem(bank, frames)

        def group(g, carry):
            power = None
            for p in range(pols):
                beam = jnp.dot(turned[p, g], weights[g], preferred_element_type=f32)
                term = beam[:, :beams] * beam[:, :beams] + beam[:, beams:] * beam[:, beams:]
                power = term if p == 0 else power + term
            power = power.astype(bf16)
            rows = pl.ds(pl.multiple_of(g * LANES, LANES), LANES)

            @pl.when(stays)
            def _():
                taken[at, rows, :] = power

            @pl.when(jnp.logical_not(stays))
            def _():
                given[at, rows, :] = power
            return carry
        lax.fori_loop(0, groups, group, 0)

        @pl.when(jnp.logical_not(stays))
        def _():
            power_copy(at).start()

    def round_(j, carry):
        (made, sent, also, late), (right_from, right_to, left_from, left_to) = look(j)

        @pl.when(j < frames)
        def _():
            forward(j)

        @pl.when(made >= 0)
        def _():
            def from_right(o, carry):
                wait_right(o)
                return carry
            lax.fori_loop(right_from, right_to, from_right, 0)

            def from_left(n, carry):
                wait_left(wide - 1 - n)
                return carry
            lax.fori_loop(left_from, left_to, from_left, 0)
            channelize(made)

        @pl.when(sent >= 0)
        def _():
            share_out(sent)

        @pl.when(also >= 0)
        def _():
            share_out(also)

        @pl.when(late >= 0)
        def _():
            beamform(late)
        return carry
    lax.fori_loop(0, ROUNDS, round_, 0)

    pieces = beams // LANES
    pitch = pieces * frames

    def finish(n, carry):
        down = (col > 1) & (y == 0)
        f = jnp.where(down, frames - 1 - n, n)

        @pl.when(has_left & ((col > 1) | (f < KEPT)))
        def _():
            power_copy(f).wait_recv()

        def spread(g, carry):
            for k1 in range(FIRST):
                rows = taken[f, pl.ds(pl.multiple_of(g * LANES + k1 * lows, lows), lows), :].astype(f32)
                for half in range(lows // 8):
                    for piece in range(pieces):
                        row = g * (LANES * pitch) + (half * 8 * FIRST + k1) * pitch + piece * frames + f
                        out_ref[pl.ds(row, 8, stride=FIRST * pitch), :] = (
                            rows[half * 8:(half + 1) * 8, piece * LANES:(piece + 1) * LANES])
            return carry
        lax.fori_loop(0, groups, spread, 0)
        return carry
    lax.fori_loop(0, frames, finish, 0)

    for step in range(1, size):
        weight_copy(step).wait_send()
    for n in range(frames):
        swap_copy(n).wait_send()

    @pl.when(has_left)
    def _():
        for o in range(frames + KEPT):
            left_copy(o, got_src(0)).wait_send()

        @pl.when(col > 1)
        def _():
            for o in range(frames + KEPT, wide):
                left_copy(o, got_src(0)).wait_send()

    @pl.when(to_right)
    def _():
        for o in range(1, wide):
            right_copy(o, got_src(0)).wait_send()

        @pl.when(first_col)
        def _():
            right_copy(0, got_src(0)).wait_send()

    for n in range(frames):
        @pl.when(mid | (first_col & (n < KEPT)))
        def _():
            power_copy(n).wait_send()

    def drain(i, carry):
        @pl.when(busy(i))
        def _():
            owner, bank = plan(i)
            for h in range(2):
                @pl.when(jnp.logical_not((owner == y) & (core == h)))
                def _():
                    for p in range(pols):
                        spectra_copy(i, h, p, owner, bank).wait_send()
        return carry
    lax.fori_loop(0, 2 * wide, drain, 0)


def fused(v, weight_rows, index, mask, taps, tables, size):
    stations, pols, frames, rows, _ = v.shape
    share = stations // 2
    groups = G // 2
    beams = index.shape[1]
    depth, channels = taps.shape
    wide = 2 * frames
    bf16 = jnp.bfloat16
    dma = pltpu.SemaphoreType.DMA
    vmem = pl.BlockSpec(memory_space=pltpu.VMEM)
    hbm = pl.BlockSpec(memory_space=pl.ANY)
    return pl.pallas_call(
        functools.partial(kernel, size),
        out_shape=jax.ShapeDtypeStruct((channels // 2 * frames * beams // LANES, LANES), jnp.float32),
        in_specs=[hbm] + [vmem] * 8,
        out_specs=vmem,
        scratch_shapes=[
            pltpu.VMEM((depth - 1 + 2 * wide, share, pols, rows, LANES), bf16),
            pltpu.VMEM((depth, rows, LANES), jnp.float32),
            pltpu.VMEM((share // 8, 8 * rows, pols * LANES), bf16),
            pltpu.VMEM((pols, FIRST * share, 4 * LANES), bf16),
            pltpu.VMEM((2 * wide, 2, pols, FIRST, 2, share, LANES), bf16),
            pltpu.VMEM((wide, pols, FIRST, 2, 4 * share, LANES), bf16),
            pltpu.VMEM((size,) + weight_rows.shape, bf16),
            pltpu.VMEM((groups, 8 * share, 2 * beams), bf16),
            pltpu.VMEM((pols, groups, LANES, 2 * LANES), bf16),
            pltpu.VMEM((frames, channels // 2, beams), bf16),
            pltpu.VMEM((frames, channels // 2, beams), bf16),
            dma((frames + 1,)), dma((size,)), dma((size,)), dma((frames,)), dma((frames,)),
            dma((wide,)), dma((wide,)), dma((wide,)), dma((wide,)),
            dma((2 * wide, 2, pols)), dma((2 * wide, 4, pols)), dma((2 * wide, pols)), dma((frames,)), dma((frames,)),
        ],
        compiler_params=pltpu.CompilerParams(collective_id=0, has_side_effects=True, vmem_limit_bytes=60 << 20),
        name="fused_beams",
    )(v, weight_rows, index, mask, taps, *tables)


def body(voltages, filter_taps, use_mask, block_index, weight_blocks):
    stations, pols, frames, _, channels = voltages.shape
    size = lax.axis_size("tm")
    v = voltages.reshape(stations, pols, frames, 2, channels // LANES, LANES).swapaxes(-3, -2)
    v = v.reshape(stations, pols, frames, 2 * channels // LANES, LANES)
    beams = block_index.shape[0]
    power = fused(v, weight_blocks, block_index.T, use_mask.T, filter_taps, transform_tables(channels), size)
    power = power.reshape(channels // 2, beams // LANES, frames, LANES)
    return power.swapaxes(1, 2).reshape(channels // 2, frames, beams)


def solution(mesh):
    in_specs = (
        P(("parts", "stn"), None, "tm", None, None),
        P(),
        P("parts", None),
        P("parts", None),
        P("tm", None),
    )
    out_specs = P("stn", "tm", "parts")
    return jax.shard_map(body, mesh=mesh, in_specs=in_specs, out_specs=out_specs, check_vma=False)
```

```python
import functools
import math

import jax
import jax.numpy as jnp
import numpy as np
from jax import lax
from jax.experimental import pallas as pl
from jax.experimental.pallas import tpu as pltpu
from jax.sharding import PartitionSpec as P

SB = 16
G = 16
LANES = 128
FIRST = 8
KEPT = 3
ROUNDS = 17
MESH = pl.DeviceIdType.MESH


def transform_tables(channels):
    second = channels // FIRST
    parts = second // LANES
    a = np.arange(FIRST)
    l = np.arange(second)

    def waves(product, period):
        angle = (product % period).astype(np.float32) * np.float32(2.0 * math.pi / period)
        return np.cos(angle), np.sin(angle)

    cos, sin = waves(a[:, None] * a[None, :], FIRST)
    one = np.zeros((parts, 2, FIRST, 8, 8, FIRST, parts, 2), np.float32)
    for lh in range(parts):
        for s in range(8):
            one[lh, 0, :, s, s, :, lh, 0] = cos
            one[lh, 0, :, s, s, :, lh, 1] = sin
            one[lh, 1, :, s, s, :, lh, 0] = -sin
            one[lh, 1, :, s, s, :, lh, 1] = cos
    one = one.reshape(parts * 2 * FIRST * 8, 8 * FIRST * parts * 2)
    cos, sin = waves(l[:, None] * l[None, :], second)
    two = np.stack([np.stack([cos, -sin], axis=1), np.stack([sin, cos], axis=1)], axis=0)
    two = two.reshape(2, second, 2, 2, LANES).transpose(0, 1, 3, 2, 4).reshape(2 * second, 2 * second)
    cos, sin = waves(a[:, None] * l[None, :], channels)
    norm = np.float32(1.0 / math.sqrt(channels))
    cos, sin = (
        np.repeat((w * norm).reshape(FIRST, parts, LANES).swapaxes(0, 1), 8, axis=1) for w in (cos, sin))
    return jnp.asarray(one, jnp.bfloat16), jnp.asarray(two, jnp.bfloat16), jnp.asarray(cos), jnp.asarray(sin)


def schedule(frames):
    wide = 2 * frames

    def orders(filters, early, beams, right, left):
        rows = []
        had = [0, 0]
        for j in range(ROUNDS):
            here = [d for k, d in filters if k == j]
            need = list(had)
            for d in here:
                need = [max(need[0], right(d)), max(need[1], left(d))]
            sent = [d for k, d in early if k == j]
            done = [d for k, d in beams if k == j]
            word = 0
            for d in (here + [-1])[:1] + (sent + [-1, -1])[:2] + (done + [-1])[:1]:
                word = word * 32 + d + 1
            rows.append((word, ((had[0] * 16 + need[0]) * 16 + had[1]) * 16 + need[1]))
            had = need
        return rows

    def right(d):
        return max(d - wide + 1, 0)

    def left(most):
        return lambda d: min(max(2 * wide - 1 - d, 0), most)

    def placed(first, order):
        return [(first + k, d) for k, d in enumerate(order)]

    upper_head = placed(0, [4, 5, 6, 7, 0, 8, 12, 9, 13, 10, 1, 14, 2, 3])
    lower_head = placed(0, [0, 1, 2, 3, 8, 9, 12, 10, 13, 4, 5, 14, 6, 7])
    upper_sent = [(0, 4), (1, 5)] + placed(4, [0, 8, 12, 9, 13, 10, 1, 14, 2, 3]) + [(11, 6), (12, 7)]
    lower_sent = [(0, 0)] + placed(4, [8, 9, 12, 10, 13, 4, 5, 14, 6, 7]) + placed(8, [1, 2, 3])
    upper_done = [(7, 0), (9, 8), (11, 9), (13, 10), (14, 1), (15, 2), (16, 3)]
    lower_done = [(10, 4), (11, 12), (12, 13), (13, 5), (14, 14), (15, 6), (16, 7)]
    shift = [11, 12, 10, 13, 9, 8, 14, 15]
    both = placed(4, shift + [3, 7])
    only = placed(4, shift)
    zero = lambda d: 0
    upper = [(8, 11), (10, 10), (11, 9), (13, 8)]
    lower = [(8, 12), (10, 13), (12, 14), (14, 15)]
    return [
        [orders(upper_head, upper_sent, upper_done, right, zero),
         orders(lower_head, lower_sent, lower_done, right, zero)],
        [orders(both, both, upper + [(14, 3)], right, left(wide)),
         orders(both, both, lower + [(15, 7)], right, left(wide))],
        [orders(only, only, upper, right, left(wide - 1)),
         orders(only, only, lower, right, left(wide - 1))],
    ]


def kernel(size, v_ref, rows_ref, index_ref, mask_ref, taps_ref, one_ref, two_ref, cos_ref, sin_ref, out_ref,
           x, taps, held, tw, z, r, table, weights, turned, given,
           local, send_w, recv_w, send_y, recv_y, send_l, recv_l, send_r, recv_r, send_z, recv_z, own_z, send_p, recv_p, own_p):
    me = lax.axis_index("tm")
    core = lax.axis_index("stn")
    col = me // 2
    y = lax.rem(me, 2)
    cols = size // 2
    frames = v_ref.shape[2]
    wide = 2 * frames
    depth = taps_ref.shape[0]
    base = depth - 1
    pols = v_ref.shape[1]
    share = v_ref.shape[0] // 2
    groups, _, beams2 = weights.shape
    beams = beams2 // 2
    lows = LANES // groups
    bf16 = jnp.bfloat16
    f32 = jnp.float32
    place = 2 * core + y

    barrier = pltpu.get_barrier_semaphore()
    for step in range(size):
        for side in range(2):
            if step or side:
                pl.semaphore_signal(
                    barrier, inc=1, device_id={"tm": lax.rem(me + step, size), "stn": lax.rem(core + side, 2)},
                    device_id_type=MESH)
    pl.semaphore_wait(barrier, 2 * size - 1)

    first_col = col == 0
    second_col = col == 1
    mid = (col > 0) & (col < cols - 1)
    has_left = col > 0
    to_right = col < cols - 2

    def weight_copy(step):
        return pltpu.make_async_remote_copy(
            src_ref=rows_ref, dst_ref=table.at[me], send_sem=send_w.at[step], recv_sem=recv_w.at[step],
            device_id={"tm": lax.rem(me + step, size)}, device_id_type=MESH)

    def mine(half, j):
        return v_ref.at[pl.ds(half * share, share), :, j]

    def swap_sent(n):
        return y * frames + n

    def swap_got(n):
        return (1 - y) * frames + n

    def swap_copy(n):
        o = swap_sent(n)
        return pltpu.make_async_remote_copy(
            src_ref=mine(1 - y, lax.rem(o, frames)), dst_ref=x.at[base + o], send_sem=send_y.at[n], recv_sem=recv_y.at[n],
            device_id={"tm": 2 * col + 1 - y}, device_id_type=MESH)

    def left_copy(o, src):
        return pltpu.make_async_remote_copy(
            src_ref=src, dst_ref=x.at[base + wide + o], send_sem=send_l.at[o], recv_sem=recv_r.at[o],
            device_id={"tm": me - 2}, device_id_type=MESH)

    def right_copy(o, src):
        return pltpu.make_async_remote_copy(
            src_ref=src, dst_ref=x.at[base - wide + o], send_sem=send_r.at[o], recv_sem=recv_l.at[o],
            device_id={"tm": me + 2}, device_id_type=MESH)

    def own_src(o):
        return mine(y, o % frames)

    def got_src(o):
        return x.at[base + o]

    def power_copy(i):
        return pltpu.make_async_remote_copy(
            src_ref=given.at[frames + i], dst_ref=out_ref.at[i], send_sem=send_p.at[i], recv_sem=recv_p.at[i],
            device_id={"tm": me + 2}, device_id_type=MESH)

    def power_keep(i):
        return pltpu.make_async_copy(given.at[i], out_ref.at[i], own_p.at[i])

    def own_copy(j):
        return pltpu.make_async_copy(mine(y, j), x.at[base + y * frames + j], local.at[j])

    for step in range(1, size):
        weight_copy(step).start()
    for n in range(frames):
        swap_copy(n).start()

    @pl.when(has_left & (y == 0))
    def _():
        for o in range(frames):
            left_copy(o, own_src(o)).start()

    @pl.when(has_left & (y == 1))
    def _():
        left_copy(frames, own_src(frames)).start()

    @pl.when(to_right & (y == 0))
    def _():
        right_copy(frames - 1, own_src(frames - 1)).start()

    @pl.when(to_right & (y == 1))
    def _():
        for o in range(wide - 1, frames - 1, -1):
            right_copy(o, own_src(o)).start()

    for j in range(frames):
        own_copy(j).start()
    keep = pltpu.make_async_copy(rows_ref, table.at[me], local.at[frames])
    keep.start()

    def clear(n, carry):
        x[n] = jnp.zeros(x.shape[1:], x.dtype)
        return carry
    lax.fori_loop(0, jnp.where(first_col, base, jnp.where(second_col, base - wide, 0)), clear, 0)

    for a in range(taps.shape[1] // 2):
        piece = taps_ref[:, a * LANES:(a + 1) * LANES]
        taps[:, 2 * a, :] = piece
        taps[:, 2 * a + 1, :] = piece

    for step in range(1, size):
        weight_copy(step).wait_recv()
    keep.wait()
    width = groups * 2 * SB
    entries = table[:, :, pl.ds(pl.multiple_of(core * width, width), width)].reshape(-1, width)
    entries = entries.astype(f32).T.astype(bf16)
    ids = lax.broadcasted_iota(jnp.int32, (entries.shape[1], beams), 0)
    stations = index_ref.shape[0] * SB
    for q in range(index_ref.shape[0]):
        onehot = jnp.where(ids == index_ref[q:q + 1, :], mask_ref[q:q + 1, :], 0).astype(f32).astype(bf16)
        picked = jnp.dot(entries, onehot, preferred_element_type=f32)
        for g in range(groups):
            low = 2 * g * SB
            re = picked[low:low + SB]
            im = picked[low + SB:low + 2 * SB]
            weights[g, q * SB:(q + 1) * SB, :beams] = re.astype(bf16)
            weights[g, q * SB:(q + 1) * SB, beams:] = im.astype(bf16)
            weights[g, stations + q * SB:stations + (q + 1) * SB, :beams] = (-im).astype(bf16)
            weights[g, stations + q * SB:stations + (q + 1) * SB, beams:] = re.astype(bf16)
    for j in range(frames):
        own_copy(j).wait()

    plans = schedule(frames)

    def look(j):
        words = []
        for k in range(2):
            kinds = []
            for kind in plans:
                sides = []
                for rows in kind:
                    word = jnp.int32(0)
                    for step, row in enumerate(rows):
                        if row[k]:
                            word = jnp.where(j == step, row[k], word)
                    sides.append(word)
                kinds.append(jnp.where(y == 0, sides[0], sides[1]))
            words.append(jnp.where(first_col, kinds[0], jnp.where(second_col, kinds[1], jnp.where(mid, kinds[2], 0))))
        ops, waits = words
        ops = [lax.rem(ops // 32 ** n, 32) - 1 for n in (3, 2, 1, 0)]
        waits = [lax.rem(waits // 16 ** n, 16) for n in (3, 2, 1, 0)]
        return ops, waits

    def busy(d):
        stays = d < wide
        near = lax.rem(d, frames) < KEPT
        return (first_col & (stays | near)) | (second_col & jnp.logical_not(stays & near)) | (
            mid & jnp.logical_not(second_col | stays))

    def plan(d):
        owner = lax.rem(d // frames, 2)
        bank = d // wide * frames + lax.rem(d, frames)
        return owner, bank

    def spectra_copy(i, h, p, owner, bank):
        return pltpu.make_async_remote_copy(
            src_ref=z.at[i, h, p], dst_ref=r.at[bank, p, :, :, pl.ds(place * share, share), :],
            send_sem=send_z.at[i, h, p], recv_sem=recv_z.at[i, place, p],
            device_id={"tm": 2 * col + owner, "stn": h}, device_id_type=MESH)

    def spectra_keep(i, h, p, bank):
        return pltpu.make_async_copy(
            z.at[i, h, p], r.at[bank, p, :, :, pl.ds(place * share, share), :], own_z.at[i, p])

    def spectra_wait(i, where, p, bank):
        return pltpu.make_async_remote_copy(
            src_ref=z.at[i, 0, p], dst_ref=r.at[bank, p, :, :, pl.ds(where * share, share), :],
            send_sem=send_z.at[i, 0, p], recv_sem=recv_z.at[i, where, p],
            device_id={"tm": 2 * col + 1 - y}, device_id_type=MESH)

    def forward(n):
        swap_copy(n).wait_recv()
        o = swap_got(n)

        @pl.when(to_right & (y == 0))
        def _():
            right_copy(o, got_src(o)).start()

        @pl.when(has_left & (y == 1))
        def _():
            left_copy(o, got_src(o)).start()

        @pl.when((n == frames - 1) & has_left & (y == 0))
        def _():
            for o in range(frames, frames + KEPT):
                left_copy(o, got_src(o)).start()

            @pl.when(col > 1)
            def _():
                for o in range(frames + KEPT, wide):
                    left_copy(o, got_src(o)).start()

        @pl.when((n == frames - 1) & has_left & (y == 1))
        def _():
            for o in range(frames + 1, frames + KEPT):
                left_copy(o, own_src(o)).start()

            @pl.when(col > 1)
            def _():
                for o in range(frames + KEPT, wide):
                    left_copy(o, own_src(o)).start()

        @pl.when((n == frames - 1) & to_right & (y == 0))
        def _():
            for o in range(frames - 2, 0, -1):
                right_copy(o, own_src(o)).start()

            @pl.when(first_col)
            def _():
                right_copy(0, own_src(0)).start()

        @pl.when((n == frames - 1) & to_right & (y == 1))
        def _():
            for o in range(frames - 1, 0, -1):
                right_copy(o, got_src(o)).start()

            @pl.when(first_col)
            def _():
                right_copy(0, got_src(0)).start()

    def wait_right(o):
        left_copy(o, got_src(0)).wait_recv()

    def wait_left(o):
        right_copy(o, got_src(0)).wait_recv()

    halves = 2

    def channelize(i):
        slot = base + i

        def filter_rows(n, carry):
            quad = n // halves
            rows = pl.ds(pl.multiple_of(lax.rem(n, halves) * 16, 16), 16)
            sums = [None] * (4 * pols)
            for k in range(depth):
                tap = taps[k, rows, :]
                for m in range(4):
                    for p in range(pols):
                        term = tap * x[slot - k, quad * 4 + m, p, rows, :].astype(f32)
                        j = m * pols + p
                        sums[j] = term if k == 0 else sums[j] + term
            for m in range(4):
                for p in range(pols):
                    row = (lax.rem(quad, 2) * 4 + m) * 32 + lax.rem(n, halves) * 16
                    held[quad // 2, pl.ds(pl.multiple_of(row, 16), 16), p * LANES:(p + 1) * LANES] = (
                        sums[m * pols + p].astype(bf16))
            return carry
        lax.fori_loop(0, share // 4 * halves, filter_rows, 0)

        batches = share // 8
        block = FIRST * 8
        for b in range(batches):
            spread = jnp.dot(one_ref[...], held[b], preferred_element_type=f32)
            for lh in range(2):
                cos, sin = cos_ref[lh], sin_ref[lh]
                for p in range(pols):
                    re = spread[2 * lh * block:(2 * lh + 1) * block, p * LANES:(p + 1) * LANES]
                    im = spread[(2 * lh + 1) * block:(2 * lh + 2) * block, p * LANES:(p + 1) * LANES]
                    tw[p, b * block:(b + 1) * block, lh * LANES:(lh + 1) * LANES] = (re * cos + im * sin).astype(bf16)
                    tw[p, b * block:(b + 1) * block, (2 + lh) * LANES:(3 + lh) * LANES] = (
                        im * cos - re * sin).astype(bf16)
        for p in range(pols):
            for h in range(2):
                spectra = jnp.dot(
                    tw[p], two_ref[:, h * 2 * LANES:(h + 1) * 2 * LANES], preferred_element_type=f32)
                for k1 in range(FIRST):
                    rows = jnp.concatenate(
                        [spectra[b * block + k1 * 8:b * block + (k1 + 1) * 8] for b in range(batches)], axis=0).astype(bf16)
                    for part in range(2):
                        z[i, h, p, k1, part] = rows[:, part * LANES:(part + 1) * LANES]

    def share_out(i):
        owner, bank = plan(i)
        for p in range(pols):
            for h in range(2):
                stay = (owner == y) & (core == h)

                @pl.when(stay)
                def _():
                    spectra_keep(i, h, p, bank).start()

                @pl.when(jnp.logical_not(stay))
                def _():
                    spectra_copy(i, h, p, owner, bank).start()

    def beamform(i):
        _, bank = plan(i)
        for p in range(pols):
            for where in range(4):
                @pl.when(place == where)
                def _():
                    spectra_keep(i, core, p, bank).wait()

                @pl.when(place != where)
                def _():
                    spectra_wait(i, where, p, bank).wait_recv()

        def turn(k1, carry):
            for p in range(pols):
                for part in range(2):
                    tile = r[bank, p, k1, part].T
                    for g in range(groups):
                        turned[p, g, pl.ds(pl.multiple_of(k1 * lows, lows), lows), part * LANES:(part + 1) * LANES] = (
                            tile[g * lows:(g + 1) * lows])
            return carry
        lax.fori_loop(0, FIRST, turn, 0)

        stays = i < wide
        at = lax.rem(bank, frames)

        def group(g, carry):
            power = None
            for p in range(pols):
                beam = jnp.dot(turned[p, g], weights[g], preferred_element_type=f32)
                term = beam[:, :beams] * beam[:, :beams] + beam[:, beams:] * beam[:, beams:]
                power = term if p == 0 else power + term
            given[bank, pl.ds(pl.multiple_of(g * LANES, LANES), LANES), :] = power.astype(bf16)
            return carry
        lax.fori_loop(0, groups, group, 0)

        @pl.when(stays)
        def _():
            power_keep(at).start()

        @pl.when(jnp.logical_not(stays))
        def _():
            power_copy(at).start()

    def round_(j, carry):
        (made, sent, also, late), (right_from, right_to, left_from, left_to) = look(j)

        @pl.when(j < frames)
        def _():
            forward(j)

        @pl.when(made >= 0)
        def _():
            def from_right(o, carry):
                wait_right(o)
                return carry
            lax.fori_loop(right_from, right_to, from_right, 0)

            def from_left(n, carry):
                wait_left(wide - 1 - n)
                return carry
            lax.fori_loop(left_from, left_to, from_left, 0)
            channelize(made)

        @pl.when(sent >= 0)
        def _():
            share_out(sent)

        @pl.when(also >= 0)
        def _():
            share_out(also)

        @pl.when(late >= 0)
        def _():
            beamform(late)
        return carry
    lax.fori_loop(0, ROUNDS, round_, 0)

    for n in range(frames):
        @pl.when(has_left & ((col > 1) | (n < KEPT)))
        def _():
            power_copy(n).wait_recv()

        @pl.when(first_col | (second_col & (n >= KEPT)))
        def _():
            power_keep(n).wait()

    for step in range(1, size):
        weight_copy(step).wait_send()
    for n in range(frames):
        swap_copy(n).wait_send()

    @pl.when(has_left)
    def _():
        for o in range(frames + KEPT):
            left_copy(o, got_src(0)).wait_send()

        @pl.when(col > 1)
        def _():
            for o in range(frames + KEPT, wide):
                left_copy(o, got_src(0)).wait_send()

    @pl.when(to_right)
    def _():
        for o in range(1, wide):
            right_copy(o, got_src(0)).wait_send()

        @pl.when(first_col)
        def _():
            right_copy(0, got_src(0)).wait_send()

    for n in range(frames):
        @pl.when(mid | (first_col & (n < KEPT)))
        def _():
            power_copy(n).wait_send()

    def drain(i, carry):
        @pl.when(busy(i))
        def _():
            owner, bank = plan(i)
            for h in range(2):
                @pl.when(jnp.logical_not((owner == y) & (core == h)))
                def _():
                    for p in range(pols):
                        spectra_copy(i, h, p, owner, bank).wait_send()
        return carry
    lax.fori_loop(0, 2 * wide, drain, 0)


def fused(v, weight_rows, index, mask, taps, tables, size):
    stations, pols, frames, rows, _ = v.shape
    share = stations // 2
    groups = G // 2
    beams = index.shape[1]
    depth, channels = taps.shape
    wide = 2 * frames
    bf16 = jnp.bfloat16
    dma = pltpu.SemaphoreType.DMA
    vmem = pl.BlockSpec(memory_space=pltpu.VMEM)
    hbm = pl.BlockSpec(memory_space=pl.ANY)
    return pl.pallas_call(
        functools.partial(kernel, size),
        out_shape=jax.ShapeDtypeStruct((frames, channels // 2, beams), bf16),
        in_specs=[hbm] + [vmem] * 8,
        out_specs=hbm,
        scratch_shapes=[
            pltpu.VMEM((depth - 1 + 2 * wide, share, pols, rows, LANES), bf16),
            pltpu.VMEM((depth, rows, LANES), jnp.float32),
            pltpu.VMEM((share // 8, 8 * rows, pols * LANES), bf16),
            pltpu.VMEM((pols, FIRST * share, 4 * LANES), bf16),
            pltpu.VMEM((2 * wide, 2, pols, FIRST, 2, share, LANES), bf16),
            pltpu.VMEM((wide, pols, FIRST, 2, 4 * share, LANES), bf16),
            pltpu.VMEM((size,) + weight_rows.shape, bf16),
            pltpu.VMEM((groups, 8 * share, 2 * beams), bf16),
            pltpu.VMEM((pols, groups, LANES, 2 * LANES), bf16),
            pltpu.VMEM((wide, channels // 2, beams), bf16),
            dma((frames + 1,)), dma((size,)), dma((size,)), dma((frames,)), dma((frames,)),
            dma((wide,)), dma((wide,)), dma((wide,)), dma((wide,)),
            dma((2 * wide, 2, pols)), dma((2 * wide, 4, pols)), dma((2 * wide, pols)), dma((frames,)), dma((frames,)), dma((frames,)),
        ],
        compiler_params=pltpu.CompilerParams(collective_id=0, has_side_effects=True, vmem_limit_bytes=60 << 20),
        name="fused_beams",
    )(v, weight_rows, index, mask, taps, *tables)


def spread_kernel(power_ref, out_ref):
    frames, rows, beams = power_ref.shape
    lows = LANES // (G // 2)
    pieces = beams // LANES
    pitch = pieces * frames
    for part in range(rows // LANES):
        for f in range(frames):
            for k1 in range(FIRST):
                tile = power_ref[f, part * LANES + k1 * lows:part * LANES + (k1 + 1) * lows, :].astype(jnp.float32)
                for half in range(lows // 8):
                    for piece in range(pieces):
                        row = part * LANES * pitch + (half * 8 * FIRST + k1) * pitch + piece * frames + f
                        out_ref[pl.ds(row, 8, stride=FIRST * pitch), :] = (
                            tile[half * 8:(half + 1) * 8, piece * LANES:(piece + 1) * LANES])


def spread(power):
    frames, rows, beams = power.shape
    step = 2 * LANES
    high = step * frames * beams // LANES
    return pl.pallas_call(
        spread_kernel,
        grid=(rows // step,),
        out_shape=jax.ShapeDtypeStruct((rows * frames * beams // LANES, LANES), jnp.float32),
        in_specs=[pl.BlockSpec((frames, step, beams), lambda n: (0, n, 0))],
        out_specs=pl.BlockSpec((high, LANES), lambda n: (n, 0)),
        name="spread_power",
    )(power)


def body(voltages, filter_taps, use_mask, block_index, weight_blocks):
    stations, pols, frames, _, channels = voltages.shape
    size = lax.axis_size("tm")
    v = voltages.reshape(stations, pols, frames, 2, channels // LANES, LANES).swapaxes(-3, -2)
    v = v.reshape(stations, pols, frames, 2 * channels // LANES, LANES)
    beams = block_index.shape[0]
    power = fused(v, weight_blocks, block_index.T, use_mask.T, filter_taps, transform_tables(channels), size)
    power = spread(power).reshape(channels // 2, beams // LANES, frames, LANES)
    return power.swapaxes(1, 2).reshape(channels // 2, frames, beams)


def solution(mesh):
    in_specs = (
        P(("parts", "stn"), None, "tm", None, None),
        P(),
        P("parts", None),
        P("parts", None),
        P("tm", None),
    )
    out_specs = P("stn", "tm", "parts")
    return jax.shard_map(body, mesh=mesh, in_specs=in_specs, out_specs=out_specs, check_vma=False)
```

```python
import functools
import math

import jax
import jax.numpy as jnp
import numpy as np
from jax import lax
from jax.experimental import pallas as pl
from jax.experimental.pallas import tpu as pltpu
from jax.sharding import PartitionSpec as P

SB = 16
G = 16
LANES = 128
FIRST = 8
KEPT = 3
ROUNDS = 17
MESH = pl.DeviceIdType.MESH


def transform_tables(channels):
    second = channels // FIRST
    parts = second // LANES
    a = np.arange(FIRST)
    l = np.arange(second)

    def waves(product, period):
        angle = (product % period).astype(np.float32) * np.float32(2.0 * math.pi / period)
        return np.cos(angle), np.sin(angle)

    cos, sin = waves(a[:, None] * a[None, :], FIRST)
    one = np.zeros((parts, 2, FIRST, 8, 8, FIRST, parts, 2), np.float32)
    for lh in range(parts):
        for s in range(8):
            one[lh, 0, :, s, s, :, lh, 0] = cos
            one[lh, 0, :, s, s, :, lh, 1] = sin
            one[lh, 1, :, s, s, :, lh, 0] = -sin
            one[lh, 1, :, s, s, :, lh, 1] = cos
    one = one.reshape(parts * 2 * FIRST * 8, 8 * FIRST * parts * 2)
    cos, sin = waves(l[:, None] * l[None, :], second)
    two = np.stack([np.stack([cos, -sin], axis=1), np.stack([sin, cos], axis=1)], axis=0)
    two = two.reshape(2, second, 2, 2, LANES).transpose(0, 1, 3, 2, 4).reshape(2 * second, 2 * second)
    cos, sin = waves(a[:, None] * l[None, :], channels)
    norm = np.float32(1.0 / math.sqrt(channels))
    cos, sin = (
        np.repeat((w * norm).reshape(FIRST, parts, LANES).swapaxes(0, 1), 8, axis=1) for w in (cos, sin))
    return jnp.asarray(one, jnp.bfloat16), jnp.asarray(two, jnp.bfloat16), jnp.asarray(cos), jnp.asarray(sin)


def schedule(frames):
    wide = 2 * frames

    def orders(filters, early, beams, right, left):
        rows = []
        had = [0, 0]
        for j in range(ROUNDS):
            here = [d for k, d in filters if k == j]
            need = list(had)
            for d in here:
                need = [max(need[0], right(d)), max(need[1], left(d))]
            sent = [d for k, d in early if k == j]
            done = [d for k, d in beams if k == j]
            word = 0
            for d in (here + [-1])[:1] + (sent + [-1, -1])[:2] + (done + [-1])[:1]:
                word = word * 32 + d + 1
            rows.append((word, ((had[0] * 16 + need[0]) * 16 + had[1]) * 16 + need[1]))
            had = need
        return rows

    def right(d):
        return max(d - wide + 1, 0)

    def left(most):
        return lambda d: min(max(2 * wide - 1 - d, 0), most)

    def placed(first, order):
        return [(first + k, d) for k, d in enumerate(order)]

    upper_head = placed(0, [4, 5, 6, 7, 0, 8, 12, 9, 13, 10, 1, 14, 2, 3])
    lower_head = placed(0, [0, 1, 2, 3, 8, 9, 12, 10, 13, 4, 5, 14, 6, 7])
    upper_sent = [(0, 4), (1, 5)] + placed(4, [0, 8, 12, 9, 13, 10, 1, 14, 2, 3]) + [(11, 6), (12, 7)]
    lower_sent = [(0, 0)] + placed(4, [8, 9, 12, 10, 13, 4, 5, 14, 6, 7]) + placed(8, [1, 2, 3])
    upper_done = [(7, 0), (9, 8), (11, 9), (13, 10), (14, 1), (15, 2), (16, 3)]
    lower_done = [(10, 4), (11, 12), (12, 13), (13, 5), (14, 14), (15, 6), (16, 7)]
    shift = [11, 12, 10, 13, 9, 8, 14, 15]
    both = placed(4, shift + [3, 7])
    only = placed(4, shift)
    zero = lambda d: 0
    upper = [(8, 11), (10, 10), (11, 9), (13, 8)]
    lower = [(8, 12), (10, 13), (12, 14), (14, 15)]
    return [
        [orders(upper_head, upper_sent, upper_done, right, zero),
         orders(lower_head, lower_sent, lower_done, right, zero)],
        [orders(both, both, upper + [(14, 3)], right, left(wide)),
         orders(both, both, lower + [(15, 7)], right, left(wide))],
        [orders(only, only, upper, right, left(wide - 1)),
         orders(only, only, lower, right, left(wide - 1))],
    ]


def kernel(size, v_ref, rows_ref, index_ref, mask_ref, taps_ref, one_ref, two_ref, cos_ref, sin_ref, out_ref,
           x, taps, held, tw, z, r, table, weights, turned, given,
           local, send_w, recv_w, send_wl, recv_wl, send_wr, recv_wr, send_y, recv_y, send_l, recv_l, send_r, recv_r, send_z, recv_z, own_z, send_p, recv_p, own_p):
    me = lax.axis_index("tm")
    core = lax.axis_index("stn")
    col = me // 2
    y = lax.rem(me, 2)
    cols = size // 2
    frames = v_ref.shape[2]
    wide = 2 * frames
    depth = taps_ref.shape[0]
    base = depth - 1
    pols = v_ref.shape[1]
    share = v_ref.shape[0] // 2
    groups, _, beams2 = weights.shape
    beams = beams2 // 2
    lows = LANES // groups
    bf16 = jnp.bfloat16
    f32 = jnp.float32
    place = 2 * core + y

    first_col = col == 0
    second_col = col == 1
    mid = (col > 0) & (col < cols - 1)
    has_left = col > 0
    has_right = col < cols - 1
    to_right = col < cols - 2

    barrier = pltpu.get_barrier_semaphore()

    def greet(**where):
        pl.semaphore_signal(barrier, inc=1, device_id=where, device_id_type=MESH)

    greet(stn=1 - core)
    for side in range(2):
        greet(tm=2 * col + 1 - y, stn=side)

    @pl.when(has_left)
    def _():
        greet(tm=me - 2)

    @pl.when(has_right)
    def _():
        greet(tm=me + 2)
    pl.semaphore_wait(barrier, 3 + has_left.astype(jnp.int32) + has_right.astype(jnp.int32))

    def rows_copy():
        return pltpu.make_async_remote_copy(
            src_ref=rows_ref, dst_ref=table.at[me], send_sem=send_w.at[0], recv_sem=recv_w.at[0],
            device_id={"tm": 2 * col + 1 - y}, device_id_type=MESH)

    def rows_left(k):
        block = table.at[pl.ds(2 * (col + k), 2)]
        return pltpu.make_async_remote_copy(
            src_ref=block, dst_ref=block, send_sem=send_wl.at[k], recv_sem=recv_wl.at[k],
            device_id={"tm": me - 2}, device_id_type=MESH)

    def rows_right(k):
        block = table.at[pl.ds(2 * (col - k), 2)]
        return pltpu.make_async_remote_copy(
            src_ref=block, dst_ref=block, send_sem=send_wr.at[k], recv_sem=recv_wr.at[k],
            device_id={"tm": me + 2}, device_id_type=MESH)

    def rows_got(k, from_left):
        block = table.at[pl.ds(2 * (col - 1 - k if from_left else col + 1 + k), 2)]
        return pltpu.make_async_remote_copy(
            src_ref=block, dst_ref=block, send_sem=(send_wr if from_left else send_wl).at[k],
            recv_sem=(recv_wr if from_left else recv_wl).at[k], device_id={"tm": 2 * col + 1 - y}, device_id_type=MESH)

    def mine(half, j):
        return v_ref.at[pl.ds(half * share, share), :, j]

    def swap_sent(n):
        return y * frames + n

    def swap_got(n):
        return (1 - y) * frames + n

    def swap_copy(n):
        o = swap_sent(n)
        return pltpu.make_async_remote_copy(
            src_ref=mine(1 - y, lax.rem(o, frames)), dst_ref=x.at[base + o], send_sem=send_y.at[n], recv_sem=recv_y.at[n],
            device_id={"tm": 2 * col + 1 - y}, device_id_type=MESH)

    def left_copy(o, src):
        return pltpu.make_async_remote_copy(
            src_ref=src, dst_ref=x.at[base + wide + o], send_sem=send_l.at[o], recv_sem=recv_r.at[o],
            device_id={"tm": me - 2}, device_id_type=MESH)

    def right_copy(o, src):
        return pltpu.make_async_remote_copy(
            src_ref=src, dst_ref=x.at[base - wide + o], send_sem=send_r.at[o], recv_sem=recv_l.at[o],
            device_id={"tm": me + 2}, device_id_type=MESH)

    def own_src(o):
        return mine(y, o % frames)

    def got_src(o):
        return x.at[base + o]

    def power_copy(i):
        return pltpu.make_async_remote_copy(
            src_ref=given.at[frames + i], dst_ref=out_ref.at[i], send_sem=send_p.at[i], recv_sem=recv_p.at[i],
            device_id={"tm": me + 2}, device_id_type=MESH)

    def power_keep(i):
        return pltpu.make_async_copy(given.at[i], out_ref.at[i], own_p.at[i])

    def own_copy(j):
        return pltpu.make_async_copy(mine(y, j), x.at[base + y * frames + j], local.at[j])

    rows_copy().start()
    for n in range(frames):
        swap_copy(n).start()

    @pl.when(has_left & (y == 0))
    def _():
        for o in range(2):
            left_copy(o, own_src(o)).start()

    @pl.when(has_left & (y == 1))
    def _():
        left_copy(frames, own_src(frames)).start()

    @pl.when(to_right & (y == 0))
    def _():
        right_copy(frames - 1, own_src(frames - 1)).start()

    @pl.when(to_right & (y == 1))
    def _():
        for o in range(wide - 1, wide - 3, -1):
            right_copy(o, own_src(o)).start()

    for j in range(frames):
        own_copy(j).start()
    keep = pltpu.make_async_copy(rows_ref, table.at[me], local.at[frames])
    keep.start()

    def clear(n, carry):
        x[n] = jnp.zeros(x.shape[1:], x.dtype)
        return carry
    lax.fori_loop(0, jnp.where(first_col, base, jnp.where(second_col, base - wide, 0)), clear, 0)

    for a in range(taps.shape[1] // 2):
        piece = taps_ref[:, a * LANES:(a + 1) * LANES]
        taps[:, 2 * a, :] = piece
        taps[:, 2 * a + 1, :] = piece

    for j in range(frames):
        own_copy(j).wait()

    plans = schedule(frames)

    def look(j):
        words = []
        for k in range(2):
            kinds = []
            for kind in plans:
                sides = []
                for rows in kind:
                    word = jnp.int32(0)
                    for step, row in enumerate(rows):
                        if row[k]:
                            word = jnp.where(j == step, row[k], word)
                    sides.append(word)
                kinds.append(jnp.where(y == 0, sides[0], sides[1]))
            words.append(jnp.where(first_col, kinds[0], jnp.where(second_col, kinds[1], jnp.where(mid, kinds[2], 0))))
        ops, waits = words
        ops = [lax.rem(ops // 32 ** n, 32) - 1 for n in (3, 2, 1, 0)]
        waits = [lax.rem(waits // 16 ** n, 16) for n in (3, 2, 1, 0)]
        return ops, waits

    def busy(d):
        stays = d < wide
        near = lax.rem(d, frames) < KEPT
        return (first_col & (stays | near)) | (second_col & jnp.logical_not(stays & near)) | (
            mid & jnp.logical_not(second_col | stays))

    def plan(d):
        owner = lax.rem(d // frames, 2)
        bank = d // wide * frames + lax.rem(d, frames)
        return owner, bank

    def spectra_copy(i, h, p, owner, bank):
        return pltpu.make_async_remote_copy(
            src_ref=z.at[i, h, p], dst_ref=r.at[bank, p, :, :, pl.ds(place * share, share), :],
            send_sem=send_z.at[i, h, p], recv_sem=recv_z.at[i, place, p],
            device_id={"tm": 2 * col + owner, "stn": h}, device_id_type=MESH)

    def spectra_keep(i, h, p, bank):
        return pltpu.make_async_copy(
            z.at[i, h, p], r.at[bank, p, :, :, pl.ds(place * share, share), :], own_z.at[i, p])

    def spectra_wait(i, where, p, bank):
        return pltpu.make_async_remote_copy(
            src_ref=z.at[i, 0, p], dst_ref=r.at[bank, p, :, :, pl.ds(where * share, share), :],
            send_sem=send_z.at[i, 0, p], recv_sem=recv_z.at[i, where, p],
            device_id={"tm": 2 * col + 1 - y}, device_id_type=MESH)

    def pick_weights():
        width = groups * 2 * SB
        entries = table[:, :, pl.ds(pl.multiple_of(core * width, width), width)].reshape(-1, width)
        entries = entries.astype(f32).T.astype(bf16)
        ids = lax.broadcasted_iota(jnp.int32, (entries.shape[1], beams), 0)
        stations = index_ref.shape[0] * SB
        for q in range(index_ref.shape[0]):
            onehot = jnp.where(ids == index_ref[q:q + 1, :], mask_ref[q:q + 1, :], 0).astype(f32).astype(bf16)
            picked = jnp.dot(entries, onehot, preferred_element_type=f32)
            for g in range(groups):
                low = 2 * g * SB
                re = picked[low:low + SB]
                im = picked[low + SB:low + 2 * SB]
                weights[g, q * SB:(q + 1) * SB, :beams] = re.astype(bf16)
                weights[g, q * SB:(q + 1) * SB, beams:] = im.astype(bf16)
                weights[g, stations + q * SB:stations + (q + 1) * SB, :beams] = (-im).astype(bf16)
                weights[g, stations + q * SB:stations + (q + 1) * SB, beams:] = re.astype(bf16)

    def pass_rows(j):
        @pl.when(j == 0)
        def _():
            keep.wait()
            rows_copy().wait_recv()

        @pl.when((j > 0) & (col - j >= 0))
        def _():
            rows_got(j - 1, True).wait_recv()

        @pl.when((j > 0) & (col + j < cols))
        def _():
            rows_got(j - 1, False).wait_recv()

        @pl.when((j < cols - 1) & has_left & (col + j < cols))
        def _():
            rows_left(j).start()

        @pl.when((j < cols - 1) & has_right & (col - j >= 0))
        def _():
            rows_right(j).start()

    def forward(n):
        o = swap_got(n)

        @pl.when((n < frames - 2) & has_left & (y == 0))
        def _():
            left_copy(n + 2, mine(y, n + 2)).start()

        @pl.when((n < frames - 2) & to_right & (y == 1))
        def _():
            right_copy(wide - 3 - n, mine(y, frames - 3 - n)).start()

        @pl.when(to_right & (y == 0))
        def _():
            right_copy(o, got_src(o)).start()

        @pl.when(has_left & (y == 1))
        def _():
            left_copy(o, got_src(o)).start()

        @pl.when((n == frames - 1) & has_left & (y == 0))
        def _():
            for o in range(frames, frames + KEPT):
                left_copy(o, got_src(o)).start()

            @pl.when(col > 1)
            def _():
                for o in range(frames + KEPT, wide):
                    left_copy(o, got_src(o)).start()

        @pl.when((n == frames - 1) & has_left & (y == 1))
        def _():
            for o in range(frames + 1, frames + KEPT):
                left_copy(o, own_src(o)).start()

            @pl.when(col > 1)
            def _():
                for o in range(frames + KEPT, wide):
                    left_copy(o, own_src(o)).start()

        @pl.when((n == frames - 1) & to_right & (y == 0))
        def _():
            for o in range(frames - 2, 0, -1):
                right_copy(o, own_src(o)).start()

            @pl.when(first_col)
            def _():
                right_copy(0, own_src(0)).start()

        @pl.when((n == frames - 1) & to_right & (y == 1))
        def _():
            for o in range(frames - 1, 0, -1):
                right_copy(o, got_src(o)).start()

            @pl.when(first_col)
            def _():
                right_copy(0, got_src(0)).start()

    def wait_right(o):
        left_copy(o, got_src(0)).wait_recv()

    def wait_left(o):
        right_copy(o, got_src(0)).wait_recv()

    halves = 2

    def channelize(i):
        slot = base + i

        def filter_rows(n, carry):
            quad = n // halves
            rows = pl.ds(pl.multiple_of(lax.rem(n, halves) * 16, 16), 16)
            sums = [None] * (4 * pols)
            for k in range(depth):
                tap = taps[k, rows, :]
                for m in range(4):
                    for p in range(pols):
                        term = tap * x[slot - k, quad * 4 + m, p, rows, :].astype(f32)
                        j = m * pols + p
                        sums[j] = term if k == 0 else sums[j] + term
            for m in range(4):
                for p in range(pols):
                    row = (lax.rem(quad, 2) * 4 + m) * 32 + lax.rem(n, halves) * 16
                    held[quad // 2, pl.ds(pl.multiple_of(row, 16), 16), p * LANES:(p + 1) * LANES] = (
                        sums[m * pols + p].astype(bf16))
            return carry
        lax.fori_loop(0, share // 4 * halves, filter_rows, 0)

        batches = share // 8
        block = FIRST * 8
        for b in range(batches):
            spread = jnp.dot(one_ref[...], held[b], preferred_element_type=f32)
            for lh in range(2):
                cos, sin = cos_ref[lh], sin_ref[lh]
                for p in range(pols):
                    re = spread[2 * lh * block:(2 * lh + 1) * block, p * LANES:(p + 1) * LANES]
                    im = spread[(2 * lh + 1) * block:(2 * lh + 2) * block, p * LANES:(p + 1) * LANES]
                    tw[p, b * block:(b + 1) * block, lh * LANES:(lh + 1) * LANES] = (re * cos + im * sin).astype(bf16)
                    tw[p, b * block:(b + 1) * block, (2 + lh) * LANES:(3 + lh) * LANES] = (
                        im * cos - re * sin).astype(bf16)
        for p in range(pols):
            for h in range(2):
                spectra = jnp.dot(
                    tw[p], two_ref[:, h * 2 * LANES:(h + 1) * 2 * LANES], preferred_element_type=f32)
                for k1 in range(FIRST):
                    rows = jnp.concatenate(
                        [spectra[b * block + k1 * 8:b * block + (k1 + 1) * 8] for b in range(batches)], axis=0).astype(bf16)
                    for part in range(2):
                        z[i, h, p, k1, part] = rows[:, part * LANES:(part + 1) * LANES]

    def share_out(i):
        owner, bank = plan(i)
        for p in range(pols):
            for h in range(2):
                stay = (owner == y) & (core == h)

                @pl.when(stay)
                def _():
                    spectra_keep(i, h, p, bank).start()

                @pl.when(jnp.logical_not(stay))
                def _():
                    spectra_copy(i, h, p, owner, bank).start()

    def beamform(i):
        _, bank = plan(i)
        for p in range(pols):
            for where in range(4):
                @pl.when(place == where)
                def _():
                    spectra_keep(i, core, p, bank).wait()

                @pl.when(place != where)
                def _():
                    spectra_wait(i, where, p, bank).wait_recv()

        def turn(k1, carry):
            for p in range(pols):
                for part in range(2):
                    tile = r[bank, p, k1, part].T
                    for g in range(groups):
                        turned[p, g, pl.ds(pl.multiple_of(k1 * lows, lows), lows), part * LANES:(part + 1) * LANES] = (
                            tile[g * lows:(g + 1) * lows])
            return carry
        lax.fori_loop(0, FIRST, turn, 0)

        stays = i < wide
        at = lax.rem(bank, frames)

        def group(g, carry):
            power = None
            for p in range(pols):
                beam = jnp.dot(turned[p, g], weights[g], preferred_element_type=f32)
                term = beam[:, :beams] * beam[:, :beams] + beam[:, beams:] * beam[:, beams:]
                power = term if p == 0 else power + term
            given[bank, pl.ds(pl.multiple_of(g * LANES, LANES), LANES), :] = power.astype(bf16)
            return carry
        lax.fori_loop(0, groups, group, 0)

        @pl.when(stays)
        def _():
            power_keep(at).start()

        @pl.when(jnp.logical_not(stays))
        def _():
            power_copy(at).start()

    def round_(j, carry):
        (made, sent, also, late), (right_from, right_to, left_from, left_to) = look(j)

        @pl.when(j < frames)
        def _():
            swap_copy(j).wait_recv()

        @pl.when(j < cols)
        def _():
            pass_rows(j)

        @pl.when(j < frames)
        def _():
            forward(j)

        @pl.when(j == cols - 1)
        def _():
            pick_weights()

        @pl.when(made >= 0)
        def _():
            def from_right(o, carry):
                wait_right(o)
                return carry
            lax.fori_loop(right_from, right_to, from_right, 0)

            def from_left(n, carry):
                wait_left(wide - 1 - n)
                return carry
            lax.fori_loop(left_from, left_to, from_left, 0)
            channelize(made)

        @pl.when(sent >= 0)
        def _():
            share_out(sent)

        @pl.when(also >= 0)
        def _():
            share_out(also)

        @pl.when(late >= 0)
        def _():
            beamform(late)
        return carry
    lax.fori_loop(0, ROUNDS, round_, 0)

    for n in range(frames):
        @pl.when(has_left & ((col > 1) | (n < KEPT)))
        def _():
            power_copy(n).wait_recv()

        @pl.when(first_col | (second_col & (n >= KEPT)))
        def _():
            power_keep(n).wait()

    rows_copy().wait_send()
    for k in range(cols - 1):
        @pl.when(has_left & (col + k < cols))
        def _():
            rows_left(k).wait_send()

        @pl.when(has_right & (col - k >= 0))
        def _():
            rows_right(k).wait_send()
    for n in range(frames):
        swap_copy(n).wait_send()

    @pl.when(has_left)
    def _():
        for o in range(frames + KEPT):
            left_copy(o, got_src(0)).wait_send()

        @pl.when(col > 1)
        def _():
            for o in range(frames + KEPT, wide):
                left_copy(o, got_src(0)).wait_send()

    @pl.when(to_right)
    def _():
        for o in range(1, wide):
            right_copy(o, got_src(0)).wait_send()

        @pl.when(first_col)
        def _():
            right_copy(0, got_src(0)).wait_send()

    for n in range(frames):
        @pl.when(mid | (first_col & (n < KEPT)))
        def _():
            power_copy(n).wait_send()

    def drain(i, carry):
        @pl.when(busy(i))
        def _():
            owner, bank = plan(i)
            for h in range(2):
                @pl.when(jnp.logical_not((owner == y) & (core == h)))
                def _():
                    for p in range(pols):
                        spectra_copy(i, h, p, owner, bank).wait_send()
        return carry
    lax.fori_loop(0, 2 * wide, drain, 0)


def fused(v, weight_rows, index, mask, taps, tables, size):
    stations, pols, frames, rows, _ = v.shape
    share = stations // 2
    groups = G // 2
    beams = index.shape[1]
    depth, channels = taps.shape
    wide = 2 * frames
    bf16 = jnp.bfloat16
    dma = pltpu.SemaphoreType.DMA
    vmem = pl.BlockSpec(memory_space=pltpu.VMEM)
    hbm = pl.BlockSpec(memory_space=pl.ANY)
    return pl.pallas_call(
        functools.partial(kernel, size),
        out_shape=jax.ShapeDtypeStruct((frames, channels // 2, beams), bf16),
        in_specs=[hbm] + [vmem] * 8,
        out_specs=hbm,
        scratch_shapes=[
            pltpu.VMEM((depth - 1 + 2 * wide, share, pols, rows, LANES), bf16),
            pltpu.VMEM((depth, rows, LANES), jnp.float32),
            pltpu.VMEM((share // 8, 8 * rows, pols * LANES), bf16),
            pltpu.VMEM((pols, FIRST * share, 4 * LANES), bf16),
            pltpu.VMEM((2 * wide, 2, pols, FIRST, 2, share, LANES), bf16),
            pltpu.VMEM((wide, pols, FIRST, 2, 4 * share, LANES), bf16),
            pltpu.VMEM((size,) + weight_rows.shape, bf16),
            pltpu.VMEM((groups, 8 * share, 2 * beams), bf16),
            pltpu.VMEM((pols, groups, LANES, 2 * LANES), bf16),
            pltpu.VMEM((wide, channels // 2, beams), bf16),
            dma((frames + 1,)), dma((1,)), dma((1,)), dma((size // 2,)), dma((size // 2,)), dma((size // 2,)), dma((size // 2,)),
            dma((frames,)), dma((frames,)),
            dma((wide,)), dma((wide,)), dma((wide,)), dma((wide,)),
            dma((2 * wide, 2, pols)), dma((2 * wide, 4, pols)), dma((2 * wide, pols)), dma((frames,)), dma((frames,)), dma((frames,)),
        ],
        compiler_params=pltpu.CompilerParams(collective_id=0, has_side_effects=True, vmem_limit_bytes=60 << 20),
        name="fused_beams",
    )(v, weight_rows, index, mask, taps, *tables)


def spread_kernel(power_ref, out_ref):
    frames, rows, beams = power_ref.shape
    lows = LANES // (G // 2)
    pieces = beams // LANES
    pitch = pieces * frames
    for part in range(rows // LANES):
        for k1 in range(FIRST):
            low = part * LANES + k1 * lows
            tiles = [power_ref[f, low:low + lows, :].astype(jnp.float32) for f in range(frames)]
            for half in range(lows // 8):
                block = jnp.stack(
                    [tiles[f][half * 8:(half + 1) * 8, piece * LANES:(piece + 1) * LANES]
                     for piece in range(pieces) for f in range(frames)], axis=0)
                block = jnp.swapaxes(block, 0, 1)
                for m in range(8):
                    row = (part * LANES + (half * 8 + m) * FIRST + k1) * pitch
                    out_ref[row:row + pitch, :] = block[m]


def spread(power):
    frames, rows, beams = power.shape
    step = rows // 2
    high = step * frames * beams // LANES
    return pl.pallas_call(
        spread_kernel,
        grid=(rows // step,),
        out_shape=jax.ShapeDtypeStruct((rows * frames * beams // LANES, LANES), jnp.float32),
        in_specs=[pl.BlockSpec((frames, step, beams), lambda n: (0, n, 0))],
        out_specs=pl.BlockSpec((high, LANES), lambda n: (n, 0)),
        compiler_params=pltpu.CompilerParams(vmem_limit_bytes=32 << 20),
        name="spread_power",
    )(power)


def body(voltages, filter_taps, use_mask, block_index, weight_blocks):
    stations, pols, frames, _, channels = voltages.shape
    size = lax.axis_size("tm")
    v = voltages.reshape(stations, pols, frames, 2, channels // LANES, LANES).swapaxes(-3, -2)
    v = v.reshape(stations, pols, frames, 2 * channels // LANES, LANES)
    beams = block_index.shape[0]
    power = fused(v, weight_blocks, block_index.T, use_mask.T, filter_taps, transform_tables(channels), size)
    power = spread(power).reshape(channels // 2, beams // LANES, frames, LANES)
    return power.swapaxes(1, 2).reshape(channels // 2, frames, beams)


def solution(mesh):
    in_specs = (
        P(("parts", "stn"), None, "tm", None, None),
        P(),
        P("parts", None),
        P("parts", None),
        P("tm", None),
    )
    out_specs = P("stn", "tm", "parts")
    return jax.shard_map(body, mesh=mesh, in_specs=in_specs, out_specs=out_specs, check_vma=False)
```

```python
import functools
import math

import jax
import jax.numpy as jnp
import numpy as np
from jax import lax
from jax.experimental import pallas as pl
from jax.experimental.pallas import tpu as pltpu
from jax.sharding import PartitionSpec as P

SB = 16
G = 16
LANES = 128
FIRST = 8
KEPT = 3
ROUNDS = 17
MESH = pl.DeviceIdType.MESH


def transform_tables(channels):
    second = channels // FIRST
    parts = second // LANES
    a = np.arange(FIRST)
    l = np.arange(second)

    def waves(product, period):
        angle = (product % period).astype(np.float32) * np.float32(2.0 * math.pi / period)
        return np.cos(angle), np.sin(angle)

    cos, sin = waves(a[:, None] * a[None, :], FIRST)
    one = np.zeros((parts, 2, FIRST, 8, 8, FIRST, parts, 2), np.float32)
    for lh in range(parts):
        for s in range(8):
            one[lh, 0, :, s, s, :, lh, 0] = cos
            one[lh, 0, :, s, s, :, lh, 1] = sin
            one[lh, 1, :, s, s, :, lh, 0] = -sin
            one[lh, 1, :, s, s, :, lh, 1] = cos
    one = one.reshape(parts * 2 * FIRST * 8, 8 * FIRST * parts * 2)
    cos, sin = waves(l[:, None] * l[None, :], second)
    two = np.stack([np.stack([cos, -sin], axis=1), np.stack([sin, cos], axis=1)], axis=0)
    two = two.reshape(2, second, 2, 2, LANES).transpose(0, 1, 3, 2, 4).reshape(2 * second, 2 * second)
    cos, sin = waves(a[:, None] * l[None, :], channels)
    norm = np.float32(1.0 / math.sqrt(channels))
    cos, sin = (
        np.repeat((w * norm).reshape(FIRST, parts, LANES).swapaxes(0, 1), 8, axis=1) for w in (cos, sin))
    return jnp.asarray(one, jnp.bfloat16), jnp.asarray(two, jnp.bfloat16), jnp.asarray(cos), jnp.asarray(sin)


def schedule(frames):
    wide = 2 * frames

    def orders(filters, early, beams, right, left):
        rows = []
        had = [0, 0]
        for j in range(ROUNDS):
            here = [d for k, d in filters if k == j]
            need = list(had)
            for d in here:
                need = [max(need[0], right(d)), max(need[1], left(d))]
            sent = [d for k, d in early if k == j]
            done = [d for k, d in beams if k == j]
            word = 0
            for d in (here + [-1])[:1] + (sent + [-1, -1])[:2] + (done + [-1])[:1]:
                word = word * 32 + d + 1
            rows.append((word, ((had[0] * 16 + need[0]) * 16 + had[1]) * 16 + need[1]))
            had = need
        return rows

    def right(d):
        return max(d - wide + 1, 0)

    def left(most):
        return lambda d: min(max(2 * wide - 1 - d, 0), most)

    def placed(first, order):
        return [(first + k, d) for k, d in enumerate(order)]

    upper_head = placed(0, [4, 5, 6, 7, 0, 8, 12, 9, 13, 10, 1, 14, 2, 3])
    lower_head = placed(0, [0, 1, 2, 3, 8, 9, 12, 10, 13, 4, 5, 14, 6, 7])
    upper_sent = [(0, 4), (1, 5)] + placed(4, [0, 8, 12, 9, 13, 10, 1, 14, 2, 3]) + [(11, 6), (12, 7)]
    lower_sent = [(0, 0)] + placed(4, [8, 9, 12, 10, 13, 4, 5, 14, 6, 7]) + placed(8, [1, 2, 3])
    upper_done = [(7, 0), (9, 8), (11, 9), (13, 10), (14, 1), (15, 2), (16, 3)]
    lower_done = [(10, 4), (11, 12), (12, 13), (13, 5), (14, 14), (15, 6), (16, 7)]
    upper_shift = [12, 11, 10, 13, 9, 14, 8, 15]
    lower_shift = [11, 12, 10, 13, 9, 8, 14, 15]
    upper_both, lower_both = placed(4, upper_shift + [7, 3]), placed(4, lower_shift + [3, 7])
    upper_only, lower_only = placed(4, upper_shift), placed(4, lower_shift)
    zero = lambda d: 0
    upper = [(7, 11), (9, 10), (11, 9), (13, 8)]
    lower = [(7, 12), (9, 13), (11, 14), (13, 15)]
    return [
        [orders(upper_head, upper_sent, upper_done, right, zero),
         orders(lower_head, lower_sent, lower_done, right, zero)],
        [orders(upper_both, upper_both, upper + [(14, 3)], right, left(wide)),
         orders(lower_both, lower_both, lower + [(14, 7)], right, left(wide))],
        [orders(upper_only, upper_only, upper, right, left(wide - 1)),
         orders(lower_only, lower_only, lower, right, left(wide - 1))],
    ]


def kernel(size, v_ref, rows_ref, index_ref, mask_ref, taps_ref, one_ref, two_ref, cos_ref, sin_ref, out_ref,
           x, taps, held, tw, z, r, table, weights, turned, given,
           local, send_w, recv_w, send_wl, recv_wl, send_wr, recv_wr, send_y, recv_y, send_l, recv_l, send_r, recv_r, send_z, recv_z, own_z, send_p, recv_p, own_p):
    me = lax.axis_index("tm")
    core = lax.axis_index("stn")
    col = me // 2
    y = lax.rem(me, 2)
    cols = size // 2
    frames = v_ref.shape[2]
    wide = 2 * frames
    depth = taps_ref.shape[0]
    base = depth - 1
    pols = v_ref.shape[1]
    share = v_ref.shape[0] // 2
    groups, _, beams2 = weights.shape
    beams = beams2 // 2
    lows = LANES // groups
    bf16 = jnp.bfloat16
    f32 = jnp.float32
    place = 2 * core + y

    first_col = col == 0
    second_col = col == 1
    mid = (col > 0) & (col < cols - 1)
    has_left = col > 0
    has_right = col < cols - 1
    to_right = col < cols - 2

    barrier = pltpu.get_barrier_semaphore()

    def greet(**where):
        pl.semaphore_signal(barrier, inc=1, device_id=where, device_id_type=MESH)

    greet(stn=1 - core)
    for side in range(2):
        greet(tm=2 * col + 1 - y, stn=side)

    @pl.when(has_left)
    def _():
        greet(tm=me - 2)

    @pl.when(has_right)
    def _():
        greet(tm=me + 2)
    pl.semaphore_wait(barrier, 3 + has_left.astype(jnp.int32) + has_right.astype(jnp.int32))

    def rows_copy():
        return pltpu.make_async_remote_copy(
            src_ref=rows_ref, dst_ref=table.at[me], send_sem=send_w.at[0], recv_sem=recv_w.at[0],
            device_id={"tm": 2 * col + 1 - y}, device_id_type=MESH)

    def rows_left(k):
        block = table.at[pl.ds(2 * (col + k), 2)]
        return pltpu.make_async_remote_copy(
            src_ref=block, dst_ref=block, send_sem=send_wl.at[k], recv_sem=recv_wl.at[k],
            device_id={"tm": me - 2}, device_id_type=MESH)

    def rows_right(k):
        block = table.at[pl.ds(2 * (col - k), 2)]
        return pltpu.make_async_remote_copy(
            src_ref=block, dst_ref=block, send_sem=send_wr.at[k], recv_sem=recv_wr.at[k],
            device_id={"tm": me + 2}, device_id_type=MESH)

    def rows_got(k, from_left):
        block = table.at[pl.ds(2 * (col - 1 - k if from_left else col + 1 + k), 2)]
        return pltpu.make_async_remote_copy(
            src_ref=block, dst_ref=block, send_sem=(send_wr if from_left else send_wl).at[k],
            recv_sem=(recv_wr if from_left else recv_wl).at[k], device_id={"tm": 2 * col + 1 - y}, device_id_type=MESH)

    def mine(half, j):
        return v_ref.at[pl.ds(half * share, share), :, j]

    def swap_sent(n):
        return y * frames + n

    def swap_got(n):
        return (1 - y) * frames + n

    def swap_copy(n):
        o = swap_sent(n)
        return pltpu.make_async_remote_copy(
            src_ref=mine(1 - y, lax.rem(o, frames)), dst_ref=x.at[base + o], send_sem=send_y.at[n], recv_sem=recv_y.at[n],
            device_id={"tm": 2 * col + 1 - y}, device_id_type=MESH)

    def left_copy(o, src):
        return pltpu.make_async_remote_copy(
            src_ref=src, dst_ref=x.at[base + wide + o], send_sem=send_l.at[o], recv_sem=recv_r.at[o],
            device_id={"tm": me - 2}, device_id_type=MESH)

    def right_copy(o, src):
        return pltpu.make_async_remote_copy(
            src_ref=src, dst_ref=x.at[base - wide + o], send_sem=send_r.at[o], recv_sem=recv_l.at[o],
            device_id={"tm": me + 2}, device_id_type=MESH)

    def own_src(o):
        return mine(y, o % frames)

    def got_src(o):
        return x.at[base + o]

    def power_copy(i):
        return pltpu.make_async_remote_copy(
            src_ref=given.at[frames + i], dst_ref=out_ref.at[i], send_sem=send_p.at[i], recv_sem=recv_p.at[i],
            device_id={"tm": me + 2}, device_id_type=MESH)

    def power_keep(i):
        return pltpu.make_async_copy(given.at[i], out_ref.at[i], own_p.at[i])

    def own_copy(j):
        return pltpu.make_async_copy(mine(y, j), x.at[base + y * frames + j], local.at[j])

    rows_copy().start()
    swap_copy(0).start()

    @pl.when(to_right & (y == 0))
    def _():
        right_copy(frames - 1, own_src(frames - 1)).start()

    @pl.when(to_right & (y == 1))
    def _():
        for o in range(wide - 1, wide - 3, -1):
            right_copy(o, own_src(o)).start()

    @pl.when(has_left & (y == 0))
    def _():
        for o in range(2):
            left_copy(o, own_src(o)).start()

    @pl.when(has_left & (y == 1))
    def _():
        left_copy(frames, own_src(frames)).start()

    for n in range(1, frames):
        swap_copy(n).start()
    for j in range(frames):
        own_copy(j).start()
    keep = pltpu.make_async_copy(rows_ref, table.at[me], local.at[frames])
    keep.start()

    def clear(n, carry):
        x[n] = jnp.zeros(x.shape[1:], x.dtype)
        return carry
    lax.fori_loop(0, jnp.where(first_col, base, jnp.where(second_col, base - wide, 0)), clear, 0)

    for a in range(taps.shape[1] // 2):
        piece = taps_ref[:, a * LANES:(a + 1) * LANES]
        taps[:, 2 * a, :] = piece
        taps[:, 2 * a + 1, :] = piece

    for j in range(frames):
        own_copy(j).wait()

    plans = schedule(frames)

    def look(j):
        words = []
        for k in range(2):
            kinds = []
            for kind in plans:
                sides = []
                for rows in kind:
                    word = jnp.int32(0)
                    for step, row in enumerate(rows):
                        if row[k]:
                            word = jnp.where(j == step, row[k], word)
                    sides.append(word)
                kinds.append(jnp.where(y == 0, sides[0], sides[1]))
            words.append(jnp.where(first_col, kinds[0], jnp.where(second_col, kinds[1], jnp.where(mid, kinds[2], 0))))
        ops, waits = words
        ops = [lax.rem(ops // 32 ** n, 32) - 1 for n in (3, 2, 1, 0)]
        waits = [lax.rem(waits // 16 ** n, 16) for n in (3, 2, 1, 0)]
        return ops, waits

    def busy(d):
        stays = d < wide
        near = lax.rem(d, frames) < KEPT
        return (first_col & (stays | near)) | (second_col & jnp.logical_not(stays & near)) | (
            mid & jnp.logical_not(second_col | stays))

    def plan(d):
        owner = lax.rem(d // frames, 2)
        bank = d // wide * frames + lax.rem(d, frames)
        return owner, bank

    def spectra_copy(i, h, p, owner, bank):
        return pltpu.make_async_remote_copy(
            src_ref=z.at[i, h, p], dst_ref=r.at[bank, p, :, :, pl.ds(place * share, share), :],
            send_sem=send_z.at[i, h, p], recv_sem=recv_z.at[i, place, p],
            device_id={"tm": 2 * col + owner, "stn": h}, device_id_type=MESH)

    def spectra_keep(i, h, p, bank):
        return pltpu.make_async_copy(
            z.at[i, h, p], r.at[bank, p, :, :, pl.ds(place * share, share), :], own_z.at[i, p])

    def spectra_wait(i, where, p, bank):
        return pltpu.make_async_remote_copy(
            src_ref=z.at[i, 0, p], dst_ref=r.at[bank, p, :, :, pl.ds(where * share, share), :],
            send_sem=send_z.at[i, 0, p], recv_sem=recv_z.at[i, where, p],
            device_id={"tm": 2 * col + 1 - y}, device_id_type=MESH)

    def pick_weights():
        width = groups * 2 * SB
        entries = table[:, :, pl.ds(pl.multiple_of(core * width, width), width)].reshape(-1, width)
        entries = entries.astype(f32).T.astype(bf16)
        ids = lax.broadcasted_iota(jnp.int32, (entries.shape[1], beams), 0)
        stations = index_ref.shape[0] * SB
        for q in range(index_ref.shape[0]):
            onehot = jnp.where(ids == index_ref[q:q + 1, :], mask_ref[q:q + 1, :], 0).astype(f32).astype(bf16)
            picked = jnp.dot(entries, onehot, preferred_element_type=f32)
            for g in range(groups):
                low = 2 * g * SB
                re = picked[low:low + SB]
                im = picked[low + SB:low + 2 * SB]
                weights[g, q * SB:(q + 1) * SB, :beams] = re.astype(bf16)
                weights[g, q * SB:(q + 1) * SB, beams:] = im.astype(bf16)
                weights[g, stations + q * SB:stations + (q + 1) * SB, :beams] = (-im).astype(bf16)
                weights[g, stations + q * SB:stations + (q + 1) * SB, beams:] = re.astype(bf16)

    def pass_rows(j):
        @pl.when(j == 0)
        def _():
            keep.wait()
            rows_copy().wait_recv()

        @pl.when((j > 0) & (col - j >= 0))
        def _():
            rows_got(j - 1, True).wait_recv()

        @pl.when((j > 0) & (col + j < cols))
        def _():
            rows_got(j - 1, False).wait_recv()

        @pl.when((j < cols - 1) & has_left & (col + j < cols))
        def _():
            rows_left(j).start()

        @pl.when((j < cols - 1) & has_right & (col - j >= 0))
        def _():
            rows_right(j).start()

    def forward(n):
        o = swap_got(n)

        @pl.when((n < frames - 2) & has_left & (y == 0))
        def _():
            left_copy(n + 2, mine(y, n + 2)).start()

        @pl.when((n < frames - 2) & to_right & (y == 1))
        def _():
            right_copy(wide - 3 - n, mine(y, frames - 3 - n)).start()

        @pl.when(to_right & (y == 0))
        def _():
            right_copy(o, got_src(o)).start()

        @pl.when(has_left & (y == 1))
        def _():
            left_copy(o, got_src(o)).start()

        @pl.when((n == frames - 1) & has_left & (y == 0))
        def _():
            for o in range(frames, frames + KEPT):
                left_copy(o, got_src(o)).start()

            @pl.when(col > 1)
            def _():
                for o in range(frames + KEPT, wide):
                    left_copy(o, got_src(o)).start()

        @pl.when((n == frames - 1) & has_left & (y == 1))
        def _():
            for o in range(frames + 1, frames + KEPT):
                left_copy(o, own_src(o)).start()

            @pl.when(col > 1)
            def _():
                for o in range(frames + KEPT, wide):
                    left_copy(o, own_src(o)).start()

        @pl.when((n == frames - 1) & to_right & (y == 0))
        def _():
            for o in range(frames - 2, 0, -1):
                right_copy(o, own_src(o)).start()

            @pl.when(first_col)
            def _():
                right_copy(0, own_src(0)).start()

        @pl.when((n == frames - 1) & to_right & (y == 1))
        def _():
            for o in range(frames - 1, 0, -1):
                right_copy(o, got_src(o)).start()

            @pl.when(first_col)
            def _():
                right_copy(0, got_src(0)).start()

    def wait_right(o):
        left_copy(o, got_src(0)).wait_recv()

    def wait_left(o):
        right_copy(o, got_src(0)).wait_recv()

    halves = 2

    def channelize(i):
        slot = base + i

        def filter_rows(n, carry):
            quad = n // halves
            rows = pl.ds(pl.multiple_of(lax.rem(n, halves) * 16, 16), 16)
            sums = [None] * (4 * pols)
            for k in range(depth):
                tap = taps[k, rows, :]
                for m in range(4):
                    for p in range(pols):
                        term = tap * x[slot - k, quad * 4 + m, p, rows, :].astype(f32)
                        j = m * pols + p
                        sums[j] = term if k == 0 else sums[j] + term
            for m in range(4):
                for p in range(pols):
                    row = (lax.rem(quad, 2) * 4 + m) * 32 + lax.rem(n, halves) * 16
                    held[quad // 2, pl.ds(pl.multiple_of(row, 16), 16), p * LANES:(p + 1) * LANES] = (
                        sums[m * pols + p].astype(bf16))
            return carry
        lax.fori_loop(0, share // 4 * halves, filter_rows, 0)

        batches = share // 8
        block = FIRST * 8
        for b in range(batches):
            spread = jnp.dot(one_ref[...], held[b], preferred_element_type=f32)
            for lh in range(2):
                cos, sin = cos_ref[lh], sin_ref[lh]
                for p in range(pols):
                    re = spread[2 * lh * block:(2 * lh + 1) * block, p * LANES:(p + 1) * LANES]
                    im = spread[(2 * lh + 1) * block:(2 * lh + 2) * block, p * LANES:(p + 1) * LANES]
                    tw[p, b * block:(b + 1) * block, lh * LANES:(lh + 1) * LANES] = (re * cos + im * sin).astype(bf16)
                    tw[p, b * block:(b + 1) * block, (2 + lh) * LANES:(3 + lh) * LANES] = (
                        im * cos - re * sin).astype(bf16)
        for p in range(pols):
            for h in range(2):
                spectra = jnp.dot(
                    tw[p], two_ref[:, h * 2 * LANES:(h + 1) * 2 * LANES], preferred_element_type=f32)
                for k1 in range(FIRST):
                    rows = jnp.concatenate(
                        [spectra[b * block + k1 * 8:b * block + (k1 + 1) * 8] for b in range(batches)], axis=0).astype(bf16)
                    for part in range(2):
                        z[i, h, p, k1, part] = rows[:, part * LANES:(part + 1) * LANES]

    def share_out(i):
        owner, bank = plan(i)
        for p in range(pols):
            for h in range(2):
                stay = (owner == y) & (core == h)

                @pl.when(stay)
                def _():
                    spectra_keep(i, h, p, bank).start()

                @pl.when(jnp.logical_not(stay))
                def _():
                    spectra_copy(i, h, p, owner, bank).start()

    def beamform(i):
        _, bank = plan(i)
        for p in range(pols):
            for where in range(4):
                @pl.when(place == where)
                def _():
                    spectra_keep(i, core, p, bank).wait()

                @pl.when(place != where)
                def _():
                    spectra_wait(i, where, p, bank).wait_recv()

        def turn(k1, carry):
            for p in range(pols):
                for part in range(2):
                    tile = r[bank, p, k1, part].T
                    for g in range(groups):
                        turned[p, g, pl.ds(pl.multiple_of(k1 * lows, lows), lows), part * LANES:(part + 1) * LANES] = (
                            tile[g * lows:(g + 1) * lows])
            return carry
        lax.fori_loop(0, FIRST, turn, 0)

        stays = i < wide
        at = lax.rem(bank, frames)

        def group(g, carry):
            power = None
            for p in range(pols):
                beam = jnp.dot(turned[p, g], weights[g], preferred_element_type=f32)
                term = beam[:, :beams] * beam[:, :beams] + beam[:, beams:] * beam[:, beams:]
                power = term if p == 0 else power + term
            given[bank, pl.ds(pl.multiple_of(g * LANES, LANES), LANES), :] = power.astype(bf16)
            return carry
        lax.fori_loop(0, groups, group, 0)

        @pl.when(stays)
        def _():
            power_keep(at).start()

        @pl.when(jnp.logical_not(stays))
        def _():
            power_copy(at).start()

    def round_(j, carry):
        (made, sent, also, late), (right_from, right_to, left_from, left_to) = look(j)

        @pl.when(j < frames)
        def _():
            swap_copy(j).wait_recv()

        @pl.when(j < cols)
        def _():
            pass_rows(j)

        @pl.when(j < frames)
        def _():
            forward(j)

        @pl.when(j == cols - 1)
        def _():
            pick_weights()

        @pl.when(made >= 0)
        def _():
            def from_right(o, carry):
                wait_right(o)
                return carry
            lax.fori_loop(right_from, right_to, from_right, 0)

            def from_left(n, carry):
                wait_left(wide - 1 - n)
                return carry
            lax.fori_loop(left_from, left_to, from_left, 0)
            channelize(made)

        @pl.when(sent >= 0)
        def _():
            share_out(sent)

        @pl.when(also >= 0)
        def _():
            share_out(also)

        @pl.when(late >= 0)
        def _():
            beamform(late)
        return carry
    lax.fori_loop(0, ROUNDS, round_, 0)

    for n in range(frames):
        @pl.when(has_left & ((col > 1) | (n < KEPT)))
        def _():
            power_copy(n).wait_recv()

        @pl.when(first_col | (second_col & (n >= KEPT)))
        def _():
            power_keep(n).wait()

    rows_copy().wait_send()
    for k in range(cols - 1):
        @pl.when(has_left & (col + k < cols))
        def _():
            rows_left(k).wait_send()

        @pl.when(has_right & (col - k >= 0))
        def _():
            rows_right(k).wait_send()
    for n in range(frames):
        swap_copy(n).wait_send()

    @pl.when(has_left)
    def _():
        for o in range(frames + KEPT):
            left_copy(o, got_src(0)).wait_send()

        @pl.when(col > 1)
        def _():
            for o in range(frames + KEPT, wide):
                left_copy(o, got_src(0)).wait_send()

    @pl.when(to_right)
    def _():
        for o in range(1, wide):
            right_copy(o, got_src(0)).wait_send()

        @pl.when(first_col)
        def _():
            right_copy(0, got_src(0)).wait_send()

    for n in range(frames):
        @pl.when(mid | (first_col & (n < KEPT)))
        def _():
            power_copy(n).wait_send()

    def drain(i, carry):
        @pl.when(busy(i))
        def _():
            owner, bank = plan(i)
            for h in range(2):
                @pl.when(jnp.logical_not((owner == y) & (core == h)))
                def _():
                    for p in range(pols):
                        spectra_copy(i, h, p, owner, bank).wait_send()
        return carry
    lax.fori_loop(0, 2 * wide, drain, 0)


def fused(v, weight_rows, index, mask, taps, tables, size):
    stations, pols, frames, rows, _ = v.shape
    share = stations // 2
    groups = G // 2
    beams = index.shape[1]
    depth, channels = taps.shape
    wide = 2 * frames
    bf16 = jnp.bfloat16
    dma = pltpu.SemaphoreType.DMA
    vmem = pl.BlockSpec(memory_space=pltpu.VMEM)
    hbm = pl.BlockSpec(memory_space=pl.ANY)
    return pl.pallas_call(
        functools.partial(kernel, size),
        out_shape=jax.ShapeDtypeStruct((frames, channels // 2, beams), bf16),
        in_specs=[hbm] + [vmem] * 8,
        out_specs=hbm,
        scratch_shapes=[
            pltpu.VMEM((depth - 1 + 2 * wide, share, pols, rows, LANES), bf16),
            pltpu.VMEM((depth, rows, LANES), jnp.float32),
            pltpu.VMEM((share // 8, 8 * rows, pols * LANES), bf16),
            pltpu.VMEM((pols, FIRST * share, 4 * LANES), bf16),
            pltpu.VMEM((2 * wide, 2, pols, FIRST, 2, share, LANES), bf16),
            pltpu.VMEM((wide, pols, FIRST, 2, 4 * share, LANES), bf16),
            pltpu.VMEM((size,) + weight_rows.shape, bf16),
            pltpu.VMEM((groups, 8 * share, 2 * beams), bf16),
            pltpu.VMEM((pols, groups, LANES, 2 * LANES), bf16),
            pltpu.VMEM((wide, channels // 2, beams), bf16),
            dma((frames + 1,)), dma((1,)), dma((1,)), dma((size // 2,)), dma((size // 2,)), dma((size // 2,)), dma((size // 2,)),
            dma((frames,)), dma((frames,)),
            dma((wide,)), dma((wide,)), dma((wide,)), dma((wide,)),
            dma((2 * wide, 2, pols)), dma((2 * wide, 4, pols)), dma((2 * wide, pols)), dma((frames,)), dma((frames,)), dma((frames,)),
        ],
        compiler_params=pltpu.CompilerParams(collective_id=0, has_side_effects=True, vmem_limit_bytes=60 << 20),
        name="fused_beams",
    )(v, weight_rows, index, mask, taps, *tables)


def spread_kernel(power_ref, out_ref):
    frames, rows, beams = power_ref.shape
    lows = LANES // (G // 2)
    pieces = beams // LANES
    pitch = pieces * frames
    for part in range(rows // LANES):
        for k1 in range(FIRST):
            low = part * LANES + k1 * lows
            tiles = [power_ref[f, low:low + lows, :].astype(jnp.float32) for f in range(frames)]
            for half in range(lows // 8):
                block = jnp.stack(
                    [tiles[f][half * 8:(half + 1) * 8, piece * LANES:(piece + 1) * LANES]
                     for piece in range(pieces) for f in range(frames)], axis=0)
                block = jnp.swapaxes(block, 0, 1)
                for m in range(8):
                    row = (part * LANES + (half * 8 + m) * FIRST + k1) * pitch
                    out_ref[row:row + pitch, :] = block[m]


def spread(power):
    frames, rows, beams = power.shape
    step = rows // 2
    high = step * frames * beams // LANES
    return pl.pallas_call(
        spread_kernel,
        grid=(rows // step,),
        out_shape=jax.ShapeDtypeStruct((rows * frames * beams // LANES, LANES), jnp.float32),
        in_specs=[pl.BlockSpec((frames, step, beams), lambda n: (0, n, 0))],
        out_specs=pl.BlockSpec((high, LANES), lambda n: (n, 0)),
        compiler_params=pltpu.CompilerParams(vmem_limit_bytes=32 << 20),
        name="spread_power",
    )(power)


def body(voltages, filter_taps, use_mask, block_index, weight_blocks):
    stations, pols, frames, _, channels = voltages.shape
    size = lax.axis_size("tm")
    v = voltages.reshape(stations, pols, frames, 2, channels // LANES, LANES).swapaxes(-3, -2)
    v = v.reshape(stations, pols, frames, 2 * channels // LANES, LANES)
    beams = block_index.shape[0]
    power = fused(v, weight_blocks, block_index.T, use_mask.T, filter_taps, transform_tables(channels), size)
    power = spread(power).reshape(channels // 2, beams // LANES, frames, LANES)
    return power.swapaxes(1, 2).reshape(channels // 2, frames, beams)


def solution(mesh):
    in_specs = (
        P(("parts", "stn"), None, "tm", None, None),
        P(),
        P("parts", None),
        P("parts", None),
        P("tm", None),
    )
    out_specs = P("stn", "tm", "parts")
    return jax.shard_map(body, mesh=mesh, in_specs=in_specs, out_specs=out_specs, check_vma=False)
```

```python
import functools
import math

import jax
import jax.numpy as jnp
import numpy as np
from jax import lax
from jax.experimental import pallas as pl
from jax.experimental.pallas import tpu as pltpu
from jax.sharding import PartitionSpec as P

SB = 16
G = 16
LANES = 128
FIRST = 8
KEPT = 3
ROUNDS = 17
MESH = pl.DeviceIdType.MESH


def transform_tables(channels):
    second = channels // FIRST
    parts = second // LANES
    a = np.arange(FIRST)
    l = np.arange(second)

    def waves(product, period):
        angle = (product % period).astype(np.float32) * np.float32(2.0 * math.pi / period)
        return np.cos(angle), np.sin(angle)

    cos, sin = waves(a[:, None] * a[None, :], FIRST)
    one = np.zeros((parts, 2, FIRST, 8, 8, FIRST, parts, 2), np.float32)
    for lh in range(parts):
        for s in range(8):
            one[lh, 0, :, s, s, :, lh, 0] = cos
            one[lh, 0, :, s, s, :, lh, 1] = sin
            one[lh, 1, :, s, s, :, lh, 0] = -sin
            one[lh, 1, :, s, s, :, lh, 1] = cos
    one = one.reshape(parts * 2 * FIRST * 8, 8 * FIRST * parts * 2)
    cos, sin = waves(l[:, None] * l[None, :], second)
    two = np.stack([np.stack([cos, -sin], axis=1), np.stack([sin, cos], axis=1)], axis=0)
    two = two.reshape(2, second, 2, 2, LANES).transpose(0, 1, 3, 2, 4).reshape(2 * second, 2 * second)
    cos, sin = waves(a[:, None] * l[None, :], channels)
    norm = np.float32(1.0 / math.sqrt(channels))
    cos, sin = (
        np.repeat((w * norm).reshape(FIRST, parts, LANES).swapaxes(0, 1), 8, axis=1) for w in (cos, sin))
    return jnp.asarray(one, jnp.bfloat16), jnp.asarray(two, jnp.bfloat16), jnp.asarray(cos), jnp.asarray(sin)


def schedule(frames):
    wide = 2 * frames

    def orders(filters, early, beams, right, left):
        rows = []
        had = [0, 0]
        for j in range(ROUNDS):
            here = [d for k, d in filters if k == j]
            need = list(had)
            for d in here:
                need = [max(need[0], right(d)), max(need[1], left(d))]
            sent = [d for k, d in early if k == j]
            done = [d for k, d in beams if k == j]
            word = 0
            for d in (here + [-1])[:1] + (sent + [-1, -1])[:2] + (done + [-1])[:1]:
                word = word * 32 + d + 1
            rows.append((word, ((had[0] * 16 + need[0]) * 16 + had[1]) * 16 + need[1]))
            had = need
        return rows

    def right(d):
        return max(d - wide + 1, 0)

    def left(most):
        return lambda d: min(max(2 * wide - 1 - d, 0), most)

    def placed(first, order):
        return [(first + k, d) for k, d in enumerate(order)]

    upper_head = placed(0, [4, 5, 6, 7, 0, 8, 12, 9, 13, 10, 1, 14, 2, 3])
    lower_head = placed(0, [0, 1, 2, 3, 8, 9, 12, 10, 13, 4, 5, 14, 6, 7])
    upper_sent = [(0, 4), (1, 5)] + placed(4, [0, 8, 12, 9, 13, 10, 1, 14, 2, 3]) + [(11, 6), (12, 7)]
    lower_sent = [(0, 0)] + placed(4, [8, 9, 12, 10, 13, 4, 5, 14, 6, 7]) + placed(8, [1, 2, 3])
    upper_done = [(7, 0), (9, 8), (11, 9), (13, 10), (14, 1), (15, 2), (16, 3)]
    lower_done = [(10, 4), (11, 12), (12, 13), (13, 5), (14, 14), (15, 6), (16, 7)]
    upper_shift = [12, 11, 10, 13, 9, 14, 8, 15]
    lower_shift = [11, 12, 10, 13, 9, 8, 14, 15]
    upper_both, lower_both = placed(4, upper_shift + [7, 3]), placed(4, lower_shift + [3, 7])
    upper_only, lower_only = placed(4, upper_shift), placed(4, lower_shift)
    zero = lambda d: 0
    upper = [(7, 11), (9, 10), (11, 9), (13, 8)]
    lower = [(7, 12), (9, 13), (11, 14), (13, 15)]
    return [
        [orders(upper_head, upper_sent, upper_done, right, zero),
         orders(lower_head, lower_sent, lower_done, right, zero)],
        [orders(upper_both, upper_both, upper + [(14, 3)], right, left(wide)),
         orders(lower_both, lower_both, lower + [(14, 7)], right, left(wide))],
        [orders(upper_only, upper_only, upper, right, left(wide - 1)),
         orders(lower_only, lower_only, lower, right, left(wide - 1))],
    ]


def kernel(size, v_ref, rows_ref, index_ref, mask_ref, *refs):
    far, (out_ref, taps_ref, one_ref, two_ref, cos_ref, sin_ref, tables_sem) = refs[:5], refs[5:12]
    near = (taps_ref, one_ref, two_ref, cos_ref, sin_ref)
    (x, taps, held, tw, z, r, table, weights, turned, given,
           local, send_w, recv_w, send_wl, recv_wl, send_wr, recv_wr, send_y, recv_y, send_l, recv_l, send_r, recv_r, send_z, recv_z, own_z, send_p, recv_p, own_p) = refs[12:]
    me = lax.axis_index("tm")
    core = lax.axis_index("stn")
    col = me // 2
    y = lax.rem(me, 2)
    cols = size // 2
    frames = v_ref.shape[2]
    wide = 2 * frames
    depth = taps_ref.shape[0]
    base = depth - 1
    pols = v_ref.shape[1]
    share = v_ref.shape[0] // 2
    groups, _, beams2 = weights.shape
    beams = beams2 // 2
    lows = LANES // groups
    bf16 = jnp.bfloat16
    f32 = jnp.float32
    place = 2 * core + y

    first_col = col == 0
    second_col = col == 1
    mid = (col > 0) & (col < cols - 1)
    has_left = col > 0
    has_right = col < cols - 1
    to_right = col < cols - 2

    barrier = pltpu.get_barrier_semaphore()

    def greet(**where):
        pl.semaphore_signal(barrier, inc=1, device_id=where, device_id_type=MESH)

    greet(stn=1 - core)
    for side in range(2):
        greet(tm=2 * col + 1 - y, stn=side)

    @pl.when(has_left)
    def _():
        greet(tm=me - 2)

    @pl.when(has_right)
    def _():
        greet(tm=me + 2)
    pl.semaphore_wait(barrier, 3 + has_left.astype(jnp.int32) + has_right.astype(jnp.int32))

    def rows_copy():
        return pltpu.make_async_remote_copy(
            src_ref=rows_ref, dst_ref=table.at[me], send_sem=send_w.at[0], recv_sem=recv_w.at[0],
            device_id={"tm": 2 * col + 1 - y}, device_id_type=MESH)

    def rows_left(k):
        block = table.at[pl.ds(2 * (col + k), 2)]
        return pltpu.make_async_remote_copy(
            src_ref=block, dst_ref=block, send_sem=send_wl.at[k], recv_sem=recv_wl.at[k],
            device_id={"tm": me - 2}, device_id_type=MESH)

    def rows_right(k):
        block = table.at[pl.ds(2 * (col - k), 2)]
        return pltpu.make_async_remote_copy(
            src_ref=block, dst_ref=block, send_sem=send_wr.at[k], recv_sem=recv_wr.at[k],
            device_id={"tm": me + 2}, device_id_type=MESH)

    def rows_got(k, from_left):
        block = table.at[pl.ds(2 * (col - 1 - k if from_left else col + 1 + k), 2)]
        return pltpu.make_async_remote_copy(
            src_ref=block, dst_ref=block, send_sem=(send_wr if from_left else send_wl).at[k],
            recv_sem=(recv_wr if from_left else recv_wl).at[k], device_id={"tm": 2 * col + 1 - y}, device_id_type=MESH)

    def mine(half, j):
        return v_ref.at[pl.ds(half * share, share), :, j]

    def swap_sent(n):
        return y * frames + n

    def swap_got(n):
        return (1 - y) * frames + n

    def swap_copy(n):
        o = swap_sent(n)
        return pltpu.make_async_remote_copy(
            src_ref=mine(1 - y, lax.rem(o, frames)), dst_ref=x.at[base + o], send_sem=send_y.at[n], recv_sem=recv_y.at[n],
            device_id={"tm": 2 * col + 1 - y}, device_id_type=MESH)

    def left_copy(o, src):
        return pltpu.make_async_remote_copy(
            src_ref=src, dst_ref=x.at[base + wide + o], send_sem=send_l.at[o], recv_sem=recv_r.at[o],
            device_id={"tm": me - 2}, device_id_type=MESH)

    def right_copy(o, src):
        return pltpu.make_async_remote_copy(
            src_ref=src, dst_ref=x.at[base - wide + o], send_sem=send_r.at[o], recv_sem=recv_l.at[o],
            device_id={"tm": me + 2}, device_id_type=MESH)

    def own_src(o):
        return mine(y, o % frames)

    def got_src(o):
        return x.at[base + o]

    def power_copy(i):
        return pltpu.make_async_remote_copy(
            src_ref=given.at[frames + i], dst_ref=out_ref.at[i], send_sem=send_p.at[i], recv_sem=recv_p.at[i],
            device_id={"tm": me + 2}, device_id_type=MESH)

    def power_keep(i):
        return pltpu.make_async_copy(given.at[i], out_ref.at[i], own_p.at[i])

    def own_copy(j):
        return pltpu.make_async_copy(mine(y, j), x.at[base + y * frames + j], local.at[j])

    rows_copy().start()
    swap_copy(0).start()

    @pl.when(to_right & (y == 0))
    def _():
        right_copy(frames - 1, own_src(frames - 1)).start()

    @pl.when(to_right & (y == 1))
    def _():
        for o in range(wide - 1, wide - 3, -1):
            right_copy(o, own_src(o)).start()

    @pl.when(has_left & (y == 0))
    def _():
        for o in range(2):
            left_copy(o, own_src(o)).start()

    @pl.when(has_left & (y == 1))
    def _():
        left_copy(frames, own_src(frames)).start()

    for n in range(1, frames):
        swap_copy(n).start()
    for j in range(frames):
        own_copy(j).start()
    keep = pltpu.make_async_copy(rows_ref, table.at[me], local.at[frames])
    keep.start()
    loads = [pltpu.make_async_copy(src, dst, tables_sem.at[n]) for n, (src, dst) in enumerate(zip(far, near))]
    for load in loads:
        load.start()

    def clear(n, carry):
        x[n] = jnp.zeros(x.shape[1:], x.dtype)
        return carry
    lax.fori_loop(0, jnp.where(first_col, base, jnp.where(second_col, base - wide, 0)), clear, 0)

    for load in loads:
        load.wait()
    for a in range(taps.shape[1] // 2):
        piece = taps_ref[:, a * LANES:(a + 1) * LANES]
        taps[:, 2 * a, :] = piece
        taps[:, 2 * a + 1, :] = piece

    for j in range(frames):
        own_copy(j).wait()

    plans = schedule(frames)

    def look(j):
        words = []
        for k in range(2):
            kinds = []
            for kind in plans:
                sides = []
                for rows in kind:
                    word = jnp.int32(0)
                    for step, row in enumerate(rows):
                        if row[k]:
                            word = jnp.where(j == step, row[k], word)
                    sides.append(word)
                kinds.append(jnp.where(y == 0, sides[0], sides[1]))
            words.append(jnp.where(first_col, kinds[0], jnp.where(second_col, kinds[1], jnp.where(mid, kinds[2], 0))))
        ops, waits = words
        ops = [lax.rem(ops // 32 ** n, 32) - 1 for n in (3, 2, 1, 0)]
        waits = [lax.rem(waits // 16 ** n, 16) for n in (3, 2, 1, 0)]
        return ops, waits

    def busy(d):
        stays = d < wide
        near = lax.rem(d, frames) < KEPT
        return (first_col & (stays | near)) | (second_col & jnp.logical_not(stays & near)) | (
            mid & jnp.logical_not(second_col | stays))

    def plan(d):
        owner = lax.rem(d // frames, 2)
        bank = d // wide * frames + lax.rem(d, frames)
        return owner, bank

    def spectra_copy(i, h, p, owner, bank):
        return pltpu.make_async_remote_copy(
            src_ref=z.at[i, h, p], dst_ref=r.at[bank, p, :, :, pl.ds(place * share, share), :],
            send_sem=send_z.at[i, h, p], recv_sem=recv_z.at[i, place, p],
            device_id={"tm": 2 * col + owner, "stn": h}, device_id_type=MESH)

    def spectra_keep(i, h, p, bank):
        return pltpu.make_async_copy(
            z.at[i, h, p], r.at[bank, p, :, :, pl.ds(place * share, share), :], own_z.at[i, p])

    def spectra_wait(i, where, p, bank):
        return pltpu.make_async_remote_copy(
            src_ref=z.at[i, 0, p], dst_ref=r.at[bank, p, :, :, pl.ds(where * share, share), :],
            send_sem=send_z.at[i, 0, p], recv_sem=recv_z.at[i, where, p],
            device_id={"tm": 2 * col + 1 - y}, device_id_type=MESH)

    def pick_weights():
        width = groups * 2 * SB
        entries = table[:, :, pl.ds(pl.multiple_of(core * width, width), width)].reshape(-1, width)
        entries = entries.astype(f32).T.astype(bf16)
        ids = lax.broadcasted_iota(jnp.int32, (entries.shape[1], beams), 0)
        stations = index_ref.shape[0] * SB
        for q in range(index_ref.shape[0]):
            onehot = jnp.where(ids == index_ref[q:q + 1, :], mask_ref[q:q + 1, :], 0).astype(f32).astype(bf16)
            picked = jnp.dot(entries, onehot, preferred_element_type=f32)
            for g in range(groups):
                low = 2 * g * SB
                re = picked[low:low + SB]
                im = picked[low + SB:low + 2 * SB]
                weights[g, q * SB:(q + 1) * SB, :beams] = re.astype(bf16)
                weights[g, q * SB:(q + 1) * SB, beams:] = im.astype(bf16)
                weights[g, stations + q * SB:stations + (q + 1) * SB, :beams] = (-im).astype(bf16)
                weights[g, stations + q * SB:stations + (q + 1) * SB, beams:] = re.astype(bf16)

    def pass_rows(j):
        @pl.when(j == 0)
        def _():
            keep.wait()
            rows_copy().wait_recv()

        @pl.when((j > 0) & (col - j >= 0))
        def _():
            rows_got(j - 1, True).wait_recv()

        @pl.when((j > 0) & (col + j < cols))
        def _():
            rows_got(j - 1, False).wait_recv()

        @pl.when((j < cols - 1) & has_left & (col + j < cols))
        def _():
            rows_left(j).start()

        @pl.when((j < cols - 1) & has_right & (col - j >= 0))
        def _():
            rows_right(j).start()

    def forward(n):
        o = swap_got(n)

        @pl.when((n < frames - 2) & has_left & (y == 0))
        def _():
            left_copy(n + 2, mine(y, n + 2)).start()

        @pl.when((n < frames - 2) & to_right & (y == 1))
        def _():
            right_copy(wide - 3 - n, mine(y, frames - 3 - n)).start()

        @pl.when(to_right & (y == 0))
        def _():
            right_copy(o, got_src(o)).start()

        @pl.when(has_left & (y == 1))
        def _():
            left_copy(o, got_src(o)).start()

        @pl.when((n == frames - 1) & has_left & (y == 0))
        def _():
            for o in range(frames, frames + KEPT):
                left_copy(o, got_src(o)).start()

            @pl.when(col > 1)
            def _():
                for o in range(frames + KEPT, wide):
                    left_copy(o, got_src(o)).start()

        @pl.when((n == frames - 1) & has_left & (y == 1))
        def _():
            for o in range(frames + 1, frames + KEPT):
                left_copy(o, own_src(o)).start()

            @pl.when(col > 1)
            def _():
                for o in range(frames + KEPT, wide):
                    left_copy(o, own_src(o)).start()

        @pl.when((n == frames - 1) & to_right & (y == 0))
        def _():
            for o in range(frames - 2, 0, -1):
                right_copy(o, own_src(o)).start()

            @pl.when(first_col)
            def _():
                right_copy(0, own_src(0)).start()

        @pl.when((n == frames - 1) & to_right & (y == 1))
        def _():
            for o in range(frames - 1, 0, -1):
                right_copy(o, got_src(o)).start()

            @pl.when(first_col)
            def _():
                right_copy(0, got_src(0)).start()

    def wait_right(o):
        left_copy(o, got_src(0)).wait_recv()

    def wait_left(o):
        right_copy(o, got_src(0)).wait_recv()

    halves = 2

    def channelize(i):
        slot = base + i

        def filter_rows(n, carry):
            quad = n // halves
            rows = pl.ds(pl.multiple_of(lax.rem(n, halves) * 16, 16), 16)
            sums = [None] * (4 * pols)
            for k in range(depth):
                tap = taps[k, rows, :]
                for m in range(4):
                    for p in range(pols):
                        term = tap * x[slot - k, quad * 4 + m, p, rows, :].astype(f32)
                        j = m * pols + p
                        sums[j] = term if k == 0 else sums[j] + term
            for m in range(4):
                for p in range(pols):
                    row = (lax.rem(quad, 2) * 4 + m) * 32 + lax.rem(n, halves) * 16
                    held[quad // 2, pl.ds(pl.multiple_of(row, 16), 16), p * LANES:(p + 1) * LANES] = (
                        sums[m * pols + p].astype(bf16))
            return carry
        lax.fori_loop(0, share // 4 * halves, filter_rows, 0)

        batches = share // 8
        block = FIRST * 8
        for b in range(batches):
            spread = jnp.dot(one_ref[...], held[b], preferred_element_type=f32)
            for lh in range(2):
                cos, sin = cos_ref[lh], sin_ref[lh]
                for p in range(pols):
                    re = spread[2 * lh * block:(2 * lh + 1) * block, p * LANES:(p + 1) * LANES]
                    im = spread[(2 * lh + 1) * block:(2 * lh + 2) * block, p * LANES:(p + 1) * LANES]
                    tw[p, b * block:(b + 1) * block, lh * LANES:(lh + 1) * LANES] = (re * cos + im * sin).astype(bf16)
                    tw[p, b * block:(b + 1) * block, (2 + lh) * LANES:(3 + lh) * LANES] = (
                        im * cos - re * sin).astype(bf16)
        for p in range(pols):
            for h in range(2):
                spectra = jnp.dot(
                    tw[p], two_ref[:, h * 2 * LANES:(h + 1) * 2 * LANES], preferred_element_type=f32)
                for k1 in range(FIRST):
                    rows = jnp.concatenate(
                        [spectra[b * block + k1 * 8:b * block + (k1 + 1) * 8] for b in range(batches)], axis=0).astype(bf16)
                    for part in range(2):
                        z[i, h, p, k1, part] = rows[:, part * LANES:(part + 1) * LANES]

    def share_out(i):
        owner, bank = plan(i)
        for p in range(pols):
            for h in range(2):
                stay = (owner == y) & (core == h)

                @pl.when(stay)
                def _():
                    spectra_keep(i, h, p, bank).start()

                @pl.when(jnp.logical_not(stay))
                def _():
                    spectra_copy(i, h, p, owner, bank).start()

    def beamform(i):
        _, bank = plan(i)
        for p in range(pols):
            for where in range(4):
                @pl.when(place == where)
                def _():
                    spectra_keep(i, core, p, bank).wait()

                @pl.when(place != where)
                def _():
                    spectra_wait(i, where, p, bank).wait_recv()

        def turn(k1, carry):
            for p in range(pols):
                for part in range(2):
                    tile = r[bank, p, k1, part].T
                    for g in range(groups):
                        turned[p, g, pl.ds(pl.multiple_of(k1 * lows, lows), lows), part * LANES:(part + 1) * LANES] = (
                            tile[g * lows:(g + 1) * lows])
            return carry
        lax.fori_loop(0, FIRST, turn, 0)

        stays = i < wide
        at = lax.rem(bank, frames)

        def group(g, carry):
            power = None
            for p in range(pols):
                beam = jnp.dot(turned[p, g], weights[g], preferred_element_type=f32)
                term = beam[:, :beams] * beam[:, :beams] + beam[:, beams:] * beam[:, beams:]
                power = term if p == 0 else power + term
            given[bank, pl.ds(pl.multiple_of(g * LANES, LANES), LANES), :] = power.astype(bf16)
            return carry
        lax.fori_loop(0, groups, group, 0)

        @pl.when(stays)
        def _():
            power_keep(at).start()

        @pl.when(jnp.logical_not(stays))
        def _():
            power_copy(at).start()

    def round_(j, carry):
        (made, sent, also, late), (right_from, right_to, left_from, left_to) = look(j)

        @pl.when(j < frames)
        def _():
            swap_copy(j).wait_recv()

            forward(j)

        @pl.when(j < cols)
        def _():
            pass_rows(j)

        @pl.when(j == cols - 1)
        def _():
            pick_weights()

        @pl.when(made >= 0)
        def _():
            def from_right(o, carry):
                wait_right(o)
                return carry
            lax.fori_loop(right_from, right_to, from_right, 0)

            def from_left(n, carry):
                wait_left(wide - 1 - n)
                return carry
            lax.fori_loop(left_from, left_to, from_left, 0)
            channelize(made)

        @pl.when(sent >= 0)
        def _():
            share_out(sent)

        @pl.when(also >= 0)
        def _():
            share_out(also)

        @pl.when(late >= 0)
        def _():
            beamform(late)
        return carry
    lax.fori_loop(0, ROUNDS, round_, 0)

    for n in range(frames):
        @pl.when(has_left & ((col > 1) | (n < KEPT)))
        def _():
            power_copy(n).wait_recv()

        @pl.when(first_col | (second_col & (n >= KEPT)))
        def _():
            power_keep(n).wait()

    rows_copy().wait_send()
    for k in range(cols - 1):
        @pl.when(has_left & (col + k < cols))
        def _():
            rows_left(k).wait_send()

        @pl.when(has_right & (col - k >= 0))
        def _():
            rows_right(k).wait_send()
    for n in range(frames):
        swap_copy(n).wait_send()

    @pl.when(has_left)
    def _():
        for o in range(frames + KEPT):
            left_copy(o, got_src(0)).wait_send()

        @pl.when(col > 1)
        def _():
            for o in range(frames + KEPT, wide):
                left_copy(o, got_src(0)).wait_send()

    @pl.when(to_right)
    def _():
        for o in range(1, wide):
            right_copy(o, got_src(0)).wait_send()

        @pl.when(first_col)
        def _():
            right_copy(0, got_src(0)).wait_send()

    for n in range(frames):
        @pl.when(mid | (first_col & (n < KEPT)))
        def _():
            power_copy(n).wait_send()

    def drain(i, carry):
        @pl.when(busy(i))
        def _():
            owner, bank = plan(i)
            for h in range(2):
                @pl.when(jnp.logical_not((owner == y) & (core == h)))
                def _():
                    for p in range(pols):
                        spectra_copy(i, h, p, owner, bank).wait_send()
        return carry
    lax.fori_loop(0, 2 * wide, drain, 0)


def fused(v, weight_rows, index, mask, taps, tables, size):
    stations, pols, frames, rows, _ = v.shape
    share = stations // 2
    groups = G // 2
    beams = index.shape[1]
    depth, channels = taps.shape
    wide = 2 * frames
    bf16 = jnp.bfloat16
    dma = pltpu.SemaphoreType.DMA
    vmem = pl.BlockSpec(memory_space=pltpu.VMEM)
    hbm = pl.BlockSpec(memory_space=pl.ANY)
    return pl.pallas_call(
        functools.partial(kernel, size),
        out_shape=jax.ShapeDtypeStruct((frames, channels // 2, beams), bf16),
        in_specs=[hbm] + [vmem] * 3 + [hbm] * 5,
        out_specs=hbm,
        scratch_shapes=[pltpu.VMEM(a.shape, a.dtype) for a in (taps, *tables)] + [
            dma((5,)),
            pltpu.VMEM((depth - 1 + 2 * wide, share, pols, rows, LANES), bf16),
            pltpu.VMEM((depth, rows, LANES), jnp.float32),
            pltpu.VMEM((share // 8, 8 * rows, pols * LANES), bf16),
            pltpu.VMEM((pols, FIRST * share, 4 * LANES), bf16),
            pltpu.VMEM((2 * wide, 2, pols, FIRST, 2, share, LANES), bf16),
            pltpu.VMEM((wide, pols, FIRST, 2, 4 * share, LANES), bf16),
            pltpu.VMEM((size,) + weight_rows.shape, bf16),
            pltpu.VMEM((groups, 8 * share, 2 * beams), bf16),
            pltpu.VMEM((pols, groups, LANES, 2 * LANES), bf16),
            pltpu.VMEM((wide, channels // 2, beams), bf16),
            dma((frames + 1,)), dma((1,)), dma((1,)), dma((size // 2,)), dma((size // 2,)), dma((size // 2,)), dma((size // 2,)),
            dma((frames,)), dma((frames,)),
            dma((wide,)), dma((wide,)), dma((wide,)), dma((wide,)),
            dma((2 * wide, 2, pols)), dma((2 * wide, 4, pols)), dma((2 * wide, pols)), dma((frames,)), dma((frames,)), dma((frames,)),
        ],
        compiler_params=pltpu.CompilerParams(collective_id=0, has_side_effects=True, vmem_limit_bytes=60 << 20),
        name="fused_beams",
    )(v, weight_rows, index, mask, taps, *tables)


def spread_kernel(power_ref, out_ref, inside, outside, sem_in, sem_out):
    frames, rows, beams = power_ref.shape
    lows = LANES // (G // 2)
    pieces = beams // LANES
    pitch = pieces * frames

    def fetch(part):
        block = pl.ds(pl.multiple_of(part * LANES, LANES), LANES)
        return pltpu.make_async_copy(power_ref.at[:, block, :], inside.at[:, block, :], sem_in.at[part])

    def store(part):
        block = pl.ds(pl.multiple_of(part * LANES * pitch, LANES * pitch), LANES * pitch)
        return pltpu.make_async_copy(outside.at[block], out_ref.at[block], sem_out.at[part])

    for part in range(rows // LANES):
        fetch(part).start()

    def widen(part, carry):
        fetch(part).wait()
        for k1 in range(FIRST):
            low = pl.ds(pl.multiple_of(part * LANES + k1 * lows, lows), lows)
            tiles = [inside[f, low, :].astype(jnp.float32) for f in range(frames)]
            for half in range(lows // 8):
                block = jnp.stack(
                    [tiles[f][half * 8:(half + 1) * 8, piece * LANES:(piece + 1) * LANES]
                     for piece in range(pieces) for f in range(frames)], axis=0)
                block = jnp.swapaxes(block, 0, 1)
                for m in range(8):
                    row = part * LANES * pitch + ((half * 8 + m) * FIRST + k1) * pitch
                    outside[pl.ds(pl.multiple_of(row, pitch), pitch), :] = block[m]
        store(part).start()
        return carry
    lax.fori_loop(0, rows // LANES, widen, 0)
    for part in range(rows // LANES):
        store(part).wait()


def spread(power):
    frames, rows, beams = power.shape
    high = rows * frames * beams // LANES
    hbm = pl.BlockSpec(memory_space=pl.ANY)
    return pl.pallas_call(
        spread_kernel,
        out_shape=jax.ShapeDtypeStruct((high, LANES), jnp.float32),
        in_specs=[hbm],
        out_specs=hbm,
        scratch_shapes=[
            pltpu.VMEM(power.shape, power.dtype),
            pltpu.VMEM((high, LANES), jnp.float32),
            pltpu.SemaphoreType.DMA((rows // LANES,)),
            pltpu.SemaphoreType.DMA((rows // LANES,)),
        ],
        compiler_params=pltpu.CompilerParams(vmem_limit_bytes=32 << 20),
        name="spread_power",
    )(power)


def body(voltages, filter_taps, use_mask, block_index, weight_blocks):
    stations, pols, frames, _, channels = voltages.shape
    size = lax.axis_size("tm")
    v = voltages.reshape(stations, pols, frames, 2, channels // LANES, LANES).swapaxes(-3, -2)
    v = v.reshape(stations, pols, frames, 2 * channels // LANES, LANES)
    beams = block_index.shape[0]
    power = fused(v, weight_blocks, block_index.T, use_mask.T, filter_taps, transform_tables(channels), size)
    power = spread(power).reshape(channels // 2, beams // LANES, frames, LANES)
    return power.swapaxes(1, 2).reshape(channels // 2, frames, beams)


def solution(mesh):
    in_specs = (
        P(("parts", "stn"), None, "tm", None, None),
        P(),
        P("parts", None),
        P("parts", None),
        P("tm", None),
    )
    out_specs = P("stn", "tm", "parts")
    return jax.shard_map(body, mesh=mesh, in_specs=in_specs, out_specs=out_specs, check_vma=False)
```

```python
import functools
import math

import jax
import jax.numpy as jnp
import numpy as np
from jax import lax
from jax.experimental import pallas as pl
from jax.experimental.pallas import tpu as pltpu
from jax.sharding import PartitionSpec as P

SB = 16
G = 16
LANES = 128
FIRST = 8
KEPT = 3
ROUNDS = 17
MESH = pl.DeviceIdType.MESH


def transform_tables(channels):
    second = channels // FIRST
    parts = second // LANES
    a = np.arange(FIRST)
    l = np.arange(second)

    def waves(product, period):
        angle = (product % period).astype(np.float32) * np.float32(2.0 * math.pi / period)
        return np.cos(angle), np.sin(angle)

    cos, sin = waves(a[:, None] * a[None, :], FIRST)
    one = np.zeros((parts, 2, FIRST, 8, 8, FIRST, parts, 2), np.float32)
    for lh in range(parts):
        for s in range(8):
            one[lh, 0, :, s, s, :, lh, 0] = cos
            one[lh, 0, :, s, s, :, lh, 1] = sin
            one[lh, 1, :, s, s, :, lh, 0] = -sin
            one[lh, 1, :, s, s, :, lh, 1] = cos
    one = one.reshape(parts * 2 * FIRST * 8, 8 * FIRST * parts * 2)
    cos, sin = waves(l[:, None] * l[None, :], second)
    two = np.stack([np.stack([cos, -sin], axis=1), np.stack([sin, cos], axis=1)], axis=0)
    two = two.reshape(2, second, 2, 2, LANES).transpose(0, 1, 3, 2, 4).reshape(2 * second, 2 * second)
    cos, sin = waves(a[:, None] * l[None, :], channels)
    norm = np.float32(1.0 / math.sqrt(channels))
    cos, sin = (
        np.repeat((w * norm).reshape(FIRST, parts, LANES).swapaxes(0, 1), 8, axis=1) for w in (cos, sin))
    return jnp.asarray(one, jnp.bfloat16), jnp.asarray(two, jnp.bfloat16), jnp.asarray(cos), jnp.asarray(sin)


def schedule(frames):
    wide = 2 * frames

    def orders(filters, early, beams, right, left):
        rows = []
        had = [0, 0]
        for j in range(ROUNDS):
            here = [d for k, d in filters if k == j]
            need = list(had)
            for d in here:
                need = [max(need[0], right(d)), max(need[1], left(d))]
            sent = [d for k, d in early if k == j]
            done = [d for k, d in beams if k == j]
            word = 0
            for d in (here + [-1])[:1] + (sent + [-1, -1])[:2] + (done + [-1])[:1]:
                word = word * 32 + d + 1
            rows.append((word, ((had[0] * 16 + need[0]) * 16 + had[1]) * 16 + need[1]))
            had = need
        return rows

    def right(d):
        return max(d - wide + 1, 0)

    def left(most):
        return lambda d: min(max(2 * wide - 1 - d, 0), most)

    def placed(first, order):
        return [(first + k, d) for k, d in enumerate(order)]

    upper_head = placed(0, [4, 5, 6, 7, 0, 8, 12, 9, 13, 10, 1, 14, 2, 3])
    lower_head = placed(0, [0, 1, 2, 3, 8, 9, 12, 10, 13, 4, 5, 14, 6, 7])
    upper_sent = [(0, 4), (1, 5)] + placed(4, [0, 8, 12, 9, 13, 10, 1, 14, 2, 3]) + [(11, 6), (12, 7)]
    lower_sent = [(0, 0)] + placed(4, [8, 9, 12, 10, 13, 4, 5, 14, 6, 7]) + placed(8, [1, 2, 3])
    upper_done = [(7, 0), (9, 8), (11, 9), (13, 10), (14, 1), (15, 2), (16, 3)]
    lower_done = [(10, 4), (11, 12), (12, 13), (13, 5), (14, 14), (15, 6), (16, 7)]
    upper_shift = [12, 11, 10, 13, 9, 14, 8, 15]
    lower_shift = [11, 12, 10, 13, 9, 8, 14, 15]
    upper_both, lower_both = placed(4, upper_shift + [7, 3]), placed(4, lower_shift + [3, 7])
    upper_only, lower_only = placed(4, upper_shift), placed(4, lower_shift)
    zero = lambda d: 0
    upper = [(7, 11), (9, 10), (11, 9), (13, 8)]
    lower = [(7, 12), (9, 13), (11, 14), (13, 15)]
    return [
        [orders(upper_head, upper_sent, upper_done, right, zero),
         orders(lower_head, lower_sent, lower_done, right, zero)],
        [orders(upper_both, upper_both, upper + [(14, 3)], right, left(wide)),
         orders(lower_both, lower_both, lower + [(14, 7)], right, left(wide))],
        [orders(upper_only, upper_only, upper, right, left(wide - 1)),
         orders(lower_only, lower_only, lower, right, left(wide - 1))],
    ]


def kernel(size, v_ref, rows_ref, index_ref, mask_ref, *refs):
    far, (out_ref, taps_ref, one_ref, two_ref, cos_ref, sin_ref, tables_sem) = refs[:5], refs[5:12]
    near = (taps_ref, one_ref, two_ref, cos_ref, sin_ref)
    (x, taps, held, tw, z, r, table, weights, turned, part_power, given,
           local, send_w, recv_w, send_wl, recv_wl, send_wr, recv_wr, send_y, recv_y, send_l, recv_l, send_r, recv_r, send_z, recv_z, own_z, send_p, recv_p, own_p) = refs[12:]
    me = lax.axis_index("tm")
    core = lax.axis_index("stn")
    col = me // 2
    y = lax.rem(me, 2)
    cols = size // 2
    frames = v_ref.shape[2]
    wide = 2 * frames
    depth = taps_ref.shape[0]
    base = depth - 1
    pols = v_ref.shape[1]
    share = v_ref.shape[0] // 2
    few = share // 2
    groups, _, beams2 = weights.shape
    beams = beams2 // 2
    lows = LANES // groups
    bf16 = jnp.bfloat16
    f32 = jnp.float32
    place = 2 * core + y

    first_col = col == 0
    second_col = col == 1
    mid = (col > 0) & (col < cols - 1)
    has_left = col > 0
    has_right = col < cols - 1
    to_right = col < cols - 2

    barrier = pltpu.get_barrier_semaphore()

    def greet(**where):
        pl.semaphore_signal(barrier, inc=1, device_id=where, device_id_type=MESH)

    greet(stn=1 - core)
    for side in range(2):
        greet(tm=2 * col + 1 - y, stn=side)

    @pl.when(has_left)
    def _():
        greet(tm=me - 2)

    @pl.when(has_right)
    def _():
        greet(tm=me + 2)
    pl.semaphore_wait(barrier, 3 + has_left.astype(jnp.int32) + has_right.astype(jnp.int32))

    def rows_copy():
        return pltpu.make_async_remote_copy(
            src_ref=rows_ref, dst_ref=table.at[me], send_sem=send_w.at[0], recv_sem=recv_w.at[0],
            device_id={"tm": 2 * col + 1 - y}, device_id_type=MESH)

    def rows_left(k):
        block = table.at[pl.ds(2 * (col + k), 2)]
        return pltpu.make_async_remote_copy(
            src_ref=block, dst_ref=block, send_sem=send_wl.at[k], recv_sem=recv_wl.at[k],
            device_id={"tm": me - 2}, device_id_type=MESH)

    def rows_right(k):
        block = table.at[pl.ds(2 * (col - k), 2)]
        return pltpu.make_async_remote_copy(
            src_ref=block, dst_ref=block, send_sem=send_wr.at[k], recv_sem=recv_wr.at[k],
            device_id={"tm": me + 2}, device_id_type=MESH)

    def rows_got(k, from_left):
        block = table.at[pl.ds(2 * (col - 1 - k if from_left else col + 1 + k), 2)]
        return pltpu.make_async_remote_copy(
            src_ref=block, dst_ref=block, send_sem=(send_wr if from_left else send_wl).at[k],
            recv_sem=(recv_wr if from_left else recv_wl).at[k], device_id={"tm": 2 * col + 1 - y}, device_id_type=MESH)

    def mine(half, j):
        return v_ref.at[pl.ds(half * share, share), :, j]

    def swap_sent(n):
        return y * frames + n

    def swap_got(n):
        return (1 - y) * frames + n

    def swap_copy(n, part):
        o = swap_sent(n)
        return pltpu.make_async_remote_copy(
            src_ref=v_ref.at[pl.ds((1 - y) * share + part * few, few), :, lax.rem(o, frames)],
            dst_ref=x.at[base + o, pl.ds(part * few, few)], send_sem=send_y.at[n, part], recv_sem=recv_y.at[n, part],
            device_id={"tm": 2 * col + 1 - y}, device_id_type=MESH)

    def left_part(o, part):
        some = pl.ds(part * few, few)
        return pltpu.make_async_remote_copy(
            src_ref=x.at[base + o, some], dst_ref=x.at[base + wide + o, some], send_sem=send_l.at[o],
            recv_sem=recv_r.at[o], device_id={"tm": me - 2}, device_id_type=MESH)

    def right_part(o, part):
        some = pl.ds(part * few, few)
        return pltpu.make_async_remote_copy(
            src_ref=x.at[base + o, some], dst_ref=x.at[base - wide + o, some], send_sem=send_r.at[o],
            recv_sem=recv_l.at[o], device_id={"tm": me + 2}, device_id_type=MESH)

    def left_copy(o, src):
        return pltpu.make_async_remote_copy(
            src_ref=src, dst_ref=x.at[base + wide + o], send_sem=send_l.at[o], recv_sem=recv_r.at[o],
            device_id={"tm": me - 2}, device_id_type=MESH)

    def right_copy(o, src):
        return pltpu.make_async_remote_copy(
            src_ref=src, dst_ref=x.at[base - wide + o], send_sem=send_r.at[o], recv_sem=recv_l.at[o],
            device_id={"tm": me + 2}, device_id_type=MESH)

    def own_src(o):
        return mine(y, o % frames)

    def got_src(o):
        return x.at[base + o]

    def power_copy(i):
        return pltpu.make_async_remote_copy(
            src_ref=given.at[frames + i], dst_ref=out_ref.at[i], send_sem=send_p.at[i], recv_sem=recv_p.at[i],
            device_id={"tm": me + 2}, device_id_type=MESH)

    def power_keep(i):
        return pltpu.make_async_copy(given.at[i], out_ref.at[i], own_p.at[i])

    def own_copy(j):
        return pltpu.make_async_copy(mine(y, j), x.at[base + y * frames + j], local.at[j])

    rows_copy().start()
    for part in range(2):
        swap_copy(0, part).start()

    @pl.when(to_right & (y == 0))
    def _():
        right_copy(frames - 1, own_src(frames - 1)).start()

    @pl.when(to_right & (y == 1))
    def _():
        for o in range(wide - 1, wide - 3, -1):
            right_copy(o, own_src(o)).start()

    @pl.when(has_left & (y == 0))
    def _():
        for o in range(2):
            left_copy(o, own_src(o)).start()

    @pl.when(has_left & (y == 1))
    def _():
        left_copy(frames, own_src(frames)).start()

    for n in range(1, frames):
        for part in range(2):
            swap_copy(n, part).start()
    for j in range(frames):
        own_copy(j).start()
    keep = pltpu.make_async_copy(rows_ref, table.at[me], local.at[frames])
    keep.start()
    loads = [pltpu.make_async_copy(src, dst, tables_sem.at[n]) for n, (src, dst) in enumerate(zip(far, near))]
    for load in loads:
        load.start()

    def clear(n, carry):
        x[n] = jnp.zeros(x.shape[1:], x.dtype)
        return carry
    lax.fori_loop(0, jnp.where(first_col, base, jnp.where(second_col, base - wide, 0)), clear, 0)

    for load in loads:
        load.wait()
    for a in range(taps.shape[1] // 2):
        piece = taps_ref[:, a * LANES:(a + 1) * LANES]
        taps[:, 2 * a, :] = piece
        taps[:, 2 * a + 1, :] = piece

    for j in range(frames):
        own_copy(j).wait()

    plans = schedule(frames)

    def look(j):
        words = []
        for k in range(2):
            kinds = []
            for kind in plans:
                sides = []
                for rows in kind:
                    word = jnp.int32(0)
                    for step, row in enumerate(rows):
                        if row[k]:
                            word = jnp.where(j == step, row[k], word)
                    sides.append(word)
                kinds.append(jnp.where(y == 0, sides[0], sides[1]))
            words.append(jnp.where(first_col, kinds[0], jnp.where(second_col, kinds[1], jnp.where(mid, kinds[2], 0))))
        ops, waits = words
        ops = [lax.rem(ops // 32 ** n, 32) - 1 for n in (3, 2, 1, 0)]
        waits = [lax.rem(waits // 16 ** n, 16) for n in (3, 2, 1, 0)]
        return ops, waits

    def busy(d):
        stays = d < wide
        near = lax.rem(d, frames) < KEPT
        return (first_col & (stays | near)) | (second_col & jnp.logical_not(stays & near)) | (
            mid & jnp.logical_not(second_col | stays))

    def plan(d):
        owner = lax.rem(d // frames, 2)
        bank = d // wide * frames + lax.rem(d, frames)
        return owner, bank

    def spectra_copy(i, h, p, owner, bank):
        return pltpu.make_async_remote_copy(
            src_ref=z.at[i, h, p], dst_ref=r.at[bank, p, :, :, pl.ds(place * share, share), :],
            send_sem=send_z.at[i, h, p], recv_sem=recv_z.at[i, place, p],
            device_id={"tm": 2 * col + owner, "stn": h}, device_id_type=MESH)

    def spectra_keep(i, h, p, bank):
        return pltpu.make_async_copy(
            z.at[i, h, p], r.at[bank, p, :, :, pl.ds(place * share, share), :], own_z.at[i, p])

    def spectra_wait(i, where, p, bank):
        return pltpu.make_async_remote_copy(
            src_ref=z.at[i, 0, p], dst_ref=r.at[bank, p, :, :, pl.ds(where * share, share), :],
            send_sem=send_z.at[i, 0, p], recv_sem=recv_z.at[i, where, p],
            device_id={"tm": 2 * col + 1 - y}, device_id_type=MESH)

    def pick_weights():
        width = groups * 2 * SB
        entries = table[:, :, pl.ds(pl.multiple_of(core * width, width), width)].reshape(-1, width)
        entries = entries.astype(f32).T.astype(bf16)
        ids = lax.broadcasted_iota(jnp.int32, (entries.shape[1], beams), 0)
        stations = index_ref.shape[0] * SB
        for q in range(index_ref.shape[0]):
            onehot = jnp.where(ids == index_ref[q:q + 1, :], mask_ref[q:q + 1, :], 0).astype(f32).astype(bf16)
            picked = jnp.dot(entries, onehot, preferred_element_type=f32)
            for g in range(groups):
                low = 2 * g * SB
                re = picked[low:low + SB]
                im = picked[low + SB:low + 2 * SB]
                weights[g, q * SB:(q + 1) * SB, :beams] = re.astype(bf16)
                weights[g, q * SB:(q + 1) * SB, beams:] = im.astype(bf16)
                weights[g, stations + q * SB:stations + (q + 1) * SB, :beams] = (-im).astype(bf16)
                weights[g, stations + q * SB:stations + (q + 1) * SB, beams:] = re.astype(bf16)

    def pass_rows(j):
        @pl.when(j == 0)
        def _():
            keep.wait()
            rows_copy().wait_recv()

        @pl.when((j > 0) & (col - j >= 0))
        def _():
            rows_got(j - 1, True).wait_recv()

        @pl.when((j > 0) & (col + j < cols))
        def _():
            rows_got(j - 1, False).wait_recv()

        @pl.when((j < cols - 1) & has_left & (col + j < cols))
        def _():
            rows_left(j).start()

        @pl.when((j < cols - 1) & has_right & (col - j >= 0))
        def _():
            rows_right(j).start()

    def relay(n, part):
        swap_copy(n, part).wait_recv()
        o = swap_got(n)

        @pl.when(to_right & (y == 0))
        def _():
            right_part(o, part).start()

        @pl.when(has_left & (y == 1))
        def _():
            left_part(o, part).start()

    def forward(n):
        @pl.when((n < frames - 2) & has_left & (y == 0))
        def _():
            left_copy(n + 2, mine(y, n + 2)).start()

        @pl.when((n < frames - 2) & to_right & (y == 1))
        def _():
            right_copy(wide - 3 - n, mine(y, frames - 3 - n)).start()


        @pl.when((n == frames - 1) & has_left & (y == 0))
        def _():
            for o in range(frames, frames + KEPT):
                left_copy(o, got_src(o)).start()

            @pl.when(col > 1)
            def _():
                for o in range(frames + KEPT, wide):
                    left_copy(o, got_src(o)).start()

        @pl.when((n == frames - 1) & has_left & (y == 1))
        def _():
            for o in range(frames + 1, frames + KEPT):
                left_copy(o, own_src(o)).start()

            @pl.when(col > 1)
            def _():
                for o in range(frames + KEPT, wide):
                    left_copy(o, own_src(o)).start()

        @pl.when((n == frames - 1) & to_right & (y == 0))
        def _():
            for o in range(frames - 2, 0, -1):
                right_copy(o, own_src(o)).start()

            @pl.when(first_col)
            def _():
                right_copy(0, own_src(0)).start()

        @pl.when((n == frames - 1) & to_right & (y == 1))
        def _():
            for o in range(frames - 1, 0, -1):
                right_copy(o, got_src(o)).start()

            @pl.when(first_col)
            def _():
                right_copy(0, got_src(0)).start()

    def wait_right(o):
        left_copy(o, got_src(0)).wait_recv()

    def wait_left(o):
        right_copy(o, got_src(0)).wait_recv()

    halves = 2

    def channelize(i):
        slot = base + i

        def filter_rows(n, carry):
            quad = n // halves
            rows = pl.ds(pl.multiple_of(lax.rem(n, halves) * 16, 16), 16)
            sums = [None] * (4 * pols)
            for k in range(depth):
                tap = taps[k, rows, :]
                for m in range(4):
                    for p in range(pols):
                        term = tap * x[slot - k, quad * 4 + m, p, rows, :].astype(f32)
                        j = m * pols + p
                        sums[j] = term if k == 0 else sums[j] + term
            for m in range(4):
                for p in range(pols):
                    row = (lax.rem(quad, 2) * 4 + m) * 32 + lax.rem(n, halves) * 16
                    held[quad // 2, pl.ds(pl.multiple_of(row, 16), 16), p * LANES:(p + 1) * LANES] = (
                        sums[m * pols + p].astype(bf16))
            return carry
        lax.fori_loop(0, share // 4 * halves, filter_rows, 0)

        batches = share // 8
        block = FIRST * 8
        for b in range(batches):
            spread = jnp.dot(one_ref[...], held[b], preferred_element_type=f32)
            for lh in range(2):
                cos, sin = cos_ref[lh], sin_ref[lh]
                for p in range(pols):
                    re = spread[2 * lh * block:(2 * lh + 1) * block, p * LANES:(p + 1) * LANES]
                    im = spread[(2 * lh + 1) * block:(2 * lh + 2) * block, p * LANES:(p + 1) * LANES]
                    tw[p, b * block:(b + 1) * block, lh * LANES:(lh + 1) * LANES] = (re * cos + im * sin).astype(bf16)
                    tw[p, b * block:(b + 1) * block, (2 + lh) * LANES:(3 + lh) * LANES] = (
                        im * cos - re * sin).astype(bf16)
        for p in range(pols):
            for h in range(2):
                spectra = jnp.dot(
                    tw[p], two_ref[:, h * 2 * LANES:(h + 1) * 2 * LANES], preferred_element_type=f32)
                for k1 in range(FIRST):
                    rows = jnp.concatenate(
                        [spectra[b * block + k1 * 8:b * block + (k1 + 1) * 8] for b in range(batches)], axis=0).astype(bf16)
                    for part in range(2):
                        z[i, h, p, k1, part] = rows[:, part * LANES:(part + 1) * LANES]

    def share_out(i):
        owner, bank = plan(i)
        for p in range(pols):
            for h in range(2):
                stay = (owner == y) & (core == h)

                @pl.when(stay)
                def _():
                    spectra_keep(i, h, p, bank).start()

                @pl.when(jnp.logical_not(stay))
                def _():
                    spectra_copy(i, h, p, owner, bank).start()

    def beamform(i):
        _, bank = plan(i)
        stays = i < wide
        at = lax.rem(bank, frames)
        for p in range(pols):
            for where in range(4):
                @pl.when(place == where)
                def _():
                    spectra_keep(i, core, p, bank).wait()

                @pl.when(place != where)
                def _():
                    spectra_wait(i, where, p, bank).wait_recv()

            def turn(k1, carry):
                for part in range(2):
                    tile = r[bank, p, k1, part].T
                    for g in range(groups):
                        turned[p, g, pl.ds(pl.multiple_of(k1 * lows, lows), lows), part * LANES:(part + 1) * LANES] = (
                            tile[g * lows:(g + 1) * lows])
                return carry
            lax.fori_loop(0, FIRST, turn, 0, unroll=2)

            def group(g, carry):
                rows = pl.ds(pl.multiple_of(g * LANES, LANES), LANES)
                beam = jnp.dot(turned[p, g], weights[g], preferred_element_type=f32)
                power = beam[:, :beams] * beam[:, :beams] + beam[:, beams:] * beam[:, beams:]
                if p:
                    power = part_power[rows, :] + power
                if p < pols - 1:
                    part_power[rows, :] = power
                else:
                    given[bank, rows, :] = power.astype(bf16)
                return carry
            lax.fori_loop(0, groups, group, 0, unroll=2)

        @pl.when(stays)
        def _():
            power_keep(at).start()

        @pl.when(jnp.logical_not(stays))
        def _():
            power_copy(at).start()

    def round_(j, carry):
        (made, sent, also, late), (right_from, right_to, left_from, left_to) = look(j)

        @pl.when(j < frames)
        def _():
            for part in range(2):
                relay(j, part)


        @pl.when(j < cols)
        def _():
            pass_rows(j)

        @pl.when(j < frames)
        def _():
            forward(j)

        @pl.when(j == cols - 1)
        def _():
            pick_weights()

        @pl.when(made >= 0)
        def _():
            def from_right(o, carry):
                wait_right(o)
                return carry
            lax.fori_loop(right_from, right_to, from_right, 0)

            def from_left(n, carry):
                wait_left(wide - 1 - n)
                return carry
            lax.fori_loop(left_from, left_to, from_left, 0)
            channelize(made)

        @pl.when(sent >= 0)
        def _():
            share_out(sent)

        @pl.when(also >= 0)
        def _():
            share_out(also)

        @pl.when(late >= 0)
        def _():
            beamform(late)
        return carry
    lax.fori_loop(0, ROUNDS, round_, 0)

    for n in range(frames):
        @pl.when(has_left & ((col > 1) | (n < KEPT)))
        def _():
            power_copy(n).wait_recv()

        @pl.when(first_col | (second_col & (n >= KEPT)))
        def _():
            power_keep(n).wait()

    rows_copy().wait_send()
    for k in range(cols - 1):
        @pl.when(has_left & (col + k < cols))
        def _():
            rows_left(k).wait_send()

        @pl.when(has_right & (col - k >= 0))
        def _():
            rows_right(k).wait_send()
    for n in range(frames):
        for part in range(2):
            swap_copy(n, part).wait_send()

    @pl.when(has_left)
    def _():
        for o in range(frames + KEPT):
            left_copy(o, got_src(0)).wait_send()

        @pl.when(col > 1)
        def _():
            for o in range(frames + KEPT, wide):
                left_copy(o, got_src(0)).wait_send()

    @pl.when(to_right)
    def _():
        for o in range(1, wide):
            right_copy(o, got_src(0)).wait_send()

        @pl.when(first_col)
        def _():
            right_copy(0, got_src(0)).wait_send()

    for n in range(frames):
        @pl.when(mid | (first_col & (n < KEPT)))
        def _():
            power_copy(n).wait_send()

    def drain(i, carry):
        @pl.when(busy(i))
        def _():
            owner, bank = plan(i)
            for h in range(2):
                @pl.when(jnp.logical_not((owner == y) & (core == h)))
                def _():
                    for p in range(pols):
                        spectra_copy(i, h, p, owner, bank).wait_send()
        return carry
    lax.fori_loop(0, 2 * wide, drain, 0)


def fused(v, weight_rows, index, mask, taps, tables, size):
    stations, pols, frames, rows, _ = v.shape
    share = stations // 2
    groups = G // 2
    beams = index.shape[1]
    depth, channels = taps.shape
    wide = 2 * frames
    bf16 = jnp.bfloat16
    dma = pltpu.SemaphoreType.DMA
    vmem = pl.BlockSpec(memory_space=pltpu.VMEM)
    hbm = pl.BlockSpec(memory_space=pl.ANY)
    return pl.pallas_call(
        functools.partial(kernel, size),
        out_shape=jax.ShapeDtypeStruct((frames, channels // 2, beams), bf16),
        in_specs=[hbm] + [vmem] * 3 + [hbm] * 5,
        out_specs=hbm,
        scratch_shapes=[pltpu.VMEM(a.shape, a.dtype) for a in (taps, *tables)] + [
            dma((5,)),
            pltpu.VMEM((depth - 1 + 2 * wide, share, pols, rows, LANES), bf16),
            pltpu.VMEM((depth, rows, LANES), jnp.float32),
            pltpu.VMEM((share // 8, 8 * rows, pols * LANES), bf16),
            pltpu.VMEM((pols, FIRST * share, 4 * LANES), bf16),
            pltpu.VMEM((2 * wide, 2, pols, FIRST, 2, share, LANES), bf16),
            pltpu.VMEM((wide, pols, FIRST, 2, 4 * share, LANES), bf16),
            pltpu.VMEM((size,) + weight_rows.shape, bf16),
            pltpu.VMEM((groups, 8 * share, 2 * beams), bf16),
            pltpu.VMEM((pols, groups, LANES, 2 * LANES), bf16),
            pltpu.VMEM((channels // 2, beams), jnp.float32),
            pltpu.VMEM((wide, channels // 2, beams), bf16),
            dma((frames + 1,)), dma((1,)), dma((1,)), dma((size // 2,)), dma((size // 2,)), dma((size // 2,)), dma((size // 2,)),
            dma((frames, 2)), dma((frames, 2)),
            dma((wide,)), dma((wide,)), dma((wide,)), dma((wide,)),
            dma((2 * wide, 2, pols)), dma((2 * wide, 4, pols)), dma((2 * wide, pols)), dma((frames,)), dma((frames,)), dma((frames,)),
        ],
        compiler_params=pltpu.CompilerParams(collective_id=0, has_side_effects=True, vmem_limit_bytes=60 << 20),
        name="fused_beams",
    )(v, weight_rows, index, mask, taps, *tables)


def spread_kernel(power_ref, out_ref):
    frames, rows, beams = power_ref.shape
    lows = LANES // (G // 2)
    pieces = beams // LANES
    pitch = pieces * frames
    for part in range(rows // LANES):
        for k1 in range(FIRST):
            low = part * LANES + k1 * lows
            tiles = [power_ref[f, low:low + lows, :].astype(jnp.float32) for f in range(frames)]
            for half in range(lows // 8):
                block = jnp.stack(
                    [tiles[f][half * 8:(half + 1) * 8, piece * LANES:(piece + 1) * LANES]
                     for piece in range(pieces) for f in range(frames)], axis=0)
                block = jnp.swapaxes(block, 0, 1)
                for m in range(8):
                    row = (part * LANES + (half * 8 + m) * FIRST + k1) * pitch
                    out_ref[row:row + pitch, :] = block[m]


def spread(power):
    frames, rows, beams = power.shape
    step = rows // 2
    high = step * frames * beams // LANES
    return pl.pallas_call(
        spread_kernel,
        grid=(rows // step,),
        out_shape=jax.ShapeDtypeStruct((rows * frames * beams // LANES, LANES), jnp.float32),
        in_specs=[pl.BlockSpec((frames, step, beams), lambda n: (0, n, 0))],
        out_specs=pl.BlockSpec((high, LANES), lambda n: (n, 0)),
        compiler_params=pltpu.CompilerParams(vmem_limit_bytes=32 << 20),
        name="spread_power",
    )(power)


def body(voltages, filter_taps, use_mask, block_index, weight_blocks):
    stations, pols, frames, _, channels = voltages.shape
    size = lax.axis_size("tm")
    v = voltages.reshape(stations, pols, frames, 2, channels // LANES, LANES).swapaxes(-3, -2)
    v = v.reshape(stations, pols, frames, 2 * channels // LANES, LANES)
    beams = block_index.shape[0]
    power = fused(v, weight_blocks, block_index.T, use_mask.T, filter_taps, transform_tables(channels), size)
    power = spread(power).reshape(channels // 2, beams // LANES, frames, LANES)
    return power.swapaxes(1, 2).reshape(channels // 2, frames, beams)


def solution(mesh):
    in_specs = (
        P(("parts", "stn"), None, "tm", None, None),
        P(),
        P("parts", None),
        P("parts", None),
        P("tm", None),
    )
    out_specs = P("stn", "tm", "parts")
    return jax.shard_map(body, mesh=mesh, in_specs=in_specs, out_specs=out_specs, check_vma=False)
```

```python
import functools
import math

import jax
import jax.numpy as jnp
import numpy as np
from jax import lax
from jax.experimental import pallas as pl
from jax.experimental.pallas import tpu as pltpu
from jax.sharding import PartitionSpec as P

SB = 16
G = 16
LANES = 128
FIRST = 8
KEPT = 3
ROUNDS = 17
MESH = pl.DeviceIdType.MESH


def transform_tables(channels):
    second = channels // FIRST
    parts = second // LANES
    a = np.arange(FIRST)
    l = np.arange(second)

    def waves(product, period):
        angle = (product % period).astype(np.float32) * np.float32(2.0 * math.pi / period)
        return np.cos(angle), np.sin(angle)

    cos, sin = waves(a[:, None] * a[None, :], FIRST)
    one = np.zeros((parts, 2, FIRST, 8, 8, FIRST, parts, 2), np.float32)
    for lh in range(parts):
        for s in range(8):
            one[lh, 0, :, s, s, :, lh, 0] = cos
            one[lh, 0, :, s, s, :, lh, 1] = sin
            one[lh, 1, :, s, s, :, lh, 0] = -sin
            one[lh, 1, :, s, s, :, lh, 1] = cos
    one = one.reshape(parts * 2 * FIRST * 8, 8 * FIRST * parts * 2)
    cos, sin = waves(l[:, None] * l[None, :], second)
    two = np.stack([np.stack([cos, -sin], axis=1), np.stack([sin, cos], axis=1)], axis=0)
    two = two.reshape(2, second, 2, 2, LANES).transpose(0, 1, 3, 2, 4).reshape(2 * second, 2 * second)
    cos, sin = waves(a[:, None] * l[None, :], channels)
    norm = np.float32(1.0 / math.sqrt(channels))
    cos, sin = (
        np.repeat((w * norm).reshape(FIRST, parts, LANES).swapaxes(0, 1), 8, axis=1) for w in (cos, sin))
    return jnp.asarray(one, jnp.bfloat16), jnp.asarray(two, jnp.bfloat16), jnp.asarray(cos), jnp.asarray(sin)


def schedule(frames):
    wide = 2 * frames

    def orders(filters, early, beams, right, left):
        rows = []
        had = [0, 0]
        for j in range(ROUNDS):
            here = [d for k, d in filters if k == j]
            need = list(had)
            for d in here:
                need = [max(need[0], right(d)), max(need[1], left(d))]
            sent = [d for k, d in early if k == j]
            done = [d for k, d in beams if k == j]
            word = 0
            for d in (here + [-1])[:1] + (sent + [-1, -1])[:2] + (done + [-1])[:1]:
                word = word * 32 + d + 1
            rows.append((word, ((had[0] * 16 + need[0]) * 16 + had[1]) * 16 + need[1]))
            had = need
        return rows

    def right(d):
        return max(d - wide + 1, 0)

    def left(most):
        return lambda d: min(max(2 * wide - 1 - d, 0), most)

    def placed(first, order):
        return [(first + k, d) for k, d in enumerate(order)]

    upper_head = placed(0, [4, 5, 6, 7, 0, 8, 12, 9, 13, 10, 1, 14, 2, 3])
    lower_head = placed(0, [0, 1, 2, 3, 8, 9, 12, 10, 13, 4, 5, 14, 6, 7])
    upper_sent = [(0, 4), (1, 5)] + placed(4, [0, 8, 12, 9, 13, 10, 1, 14, 2, 3]) + [(11, 6), (12, 7)]
    lower_sent = [(0, 0)] + placed(4, [8, 9, 12, 10, 13, 4, 5, 14, 6, 7]) + placed(8, [1, 2, 3])
    upper_done = [(7, 0), (9, 8), (11, 9), (13, 10), (14, 1), (15, 2), (16, 3)]
    lower_done = [(10, 4), (11, 12), (12, 13), (13, 5), (14, 14), (15, 6), (16, 7)]
    upper_shift = [12, 11, 10, 13, 9, 14, 8, 15]
    lower_shift = [11, 12, 10, 13, 9, 8, 14, 15]
    upper_both, lower_both = placed(4, upper_shift + [7, 3]), placed(4, lower_shift + [3, 7])
    upper_only, lower_only = placed(4, upper_shift), placed(4, lower_shift)
    zero = lambda d: 0
    upper = [(7, 11), (9, 10), (11, 9), (13, 8)]
    lower = [(7, 12), (9, 13), (11, 14), (13, 15)]
    return [
        [orders(upper_head, upper_sent, upper_done, right, zero),
         orders(lower_head, lower_sent, lower_done, right, zero)],
        [orders(upper_both, upper_both, upper + [(14, 3)], right, left(wide)),
         orders(lower_both, lower_both, lower + [(14, 7)], right, left(wide))],
        [orders(upper_only, upper_only, upper, right, left(wide - 1)),
         orders(lower_only, lower_only, lower, right, left(wide - 1))],
    ]


def kernel(size, v_ref, rows_ref, index_ref, mask_ref, *refs):
    far, (out_ref, taps_ref, one_ref, two_ref, cos_ref, sin_ref, tables_sem) = refs[:5], refs[5:12]
    near = (taps_ref, one_ref, two_ref, cos_ref, sin_ref)
    (x, taps, held, tw, z, r, table, weights, turned, part_power, given,
           local, send_w, recv_w, send_wl, recv_wl, send_wr, recv_wr, send_y, recv_y, send_l, recv_l, send_r, recv_r, send_z, recv_z, own_z, send_p, recv_p, own_p) = refs[12:]
    me = lax.axis_index("tm")
    core = lax.axis_index("stn")
    col = me // 2
    y = lax.rem(me, 2)
    cols = size // 2
    frames = v_ref.shape[2]
    wide = 2 * frames
    depth = taps_ref.shape[0]
    base = depth - 1
    pols = v_ref.shape[1]
    share = v_ref.shape[0] // 2
    few = share // 2
    groups, _, beams2 = weights.shape
    beams = beams2 // 2
    lows = LANES // groups
    bf16 = jnp.bfloat16
    f32 = jnp.float32
    place = 2 * core + y

    first_col = col == 0
    second_col = col == 1
    mid = (col > 0) & (col < cols - 1)
    has_left = col > 0
    has_right = col < cols - 1
    to_right = col < cols - 2

    barrier = pltpu.get_barrier_semaphore()

    def greet(**where):
        pl.semaphore_signal(barrier, inc=1, device_id=where, device_id_type=MESH)

    greet(stn=1 - core)
    for side in range(2):
        greet(tm=2 * col + 1 - y, stn=side)

    @pl.when(has_left)
    def _():
        greet(tm=me - 2)

    @pl.when(has_right)
    def _():
        greet(tm=me + 2)
    pl.semaphore_wait(barrier, 3 + has_left.astype(jnp.int32) + has_right.astype(jnp.int32))

    def rows_copy():
        return pltpu.make_async_remote_copy(
            src_ref=rows_ref, dst_ref=table.at[me], send_sem=send_w.at[0], recv_sem=recv_w.at[0],
            device_id={"tm": 2 * col + 1 - y}, device_id_type=MESH)

    def rows_left(k):
        block = table.at[pl.ds(2 * (col + k), 2)]
        return pltpu.make_async_remote_copy(
            src_ref=block, dst_ref=block, send_sem=send_wl.at[k], recv_sem=recv_wl.at[k],
            device_id={"tm": lax.rem(me + size - 2, size)}, device_id_type=MESH)

    def rows_right(k):
        block = table.at[pl.ds(2 * (col - k), 2)]
        return pltpu.make_async_remote_copy(
            src_ref=block, dst_ref=block, send_sem=send_wr.at[k], recv_sem=recv_wr.at[k],
            device_id={"tm": lax.rem(me + 2, size)}, device_id_type=MESH)

    def rows_got(k, from_left):
        block = table.at[pl.ds(2 * (col - 1 - k if from_left else col + 1 + k), 2)]
        return pltpu.make_async_remote_copy(
            src_ref=block, dst_ref=block, send_sem=(send_wr if from_left else send_wl).at[k],
            recv_sem=(recv_wr if from_left else recv_wl).at[k], device_id={"tm": 2 * col + 1 - y}, device_id_type=MESH)

    def mine(half, j):
        return v_ref.at[pl.ds(half * share, share), :, j]

    def swap_sent(n):
        return y * frames + n

    def swap_got(n):
        return (1 - y) * frames + n

    def swap_copy(n, part):
        o = swap_sent(n)
        return pltpu.make_async_remote_copy(
            src_ref=v_ref.at[pl.ds((1 - y) * share + part * few, few), :, lax.rem(o, frames)],
            dst_ref=x.at[base + o, pl.ds(part * few, few)], send_sem=send_y.at[n, part], recv_sem=recv_y.at[n, part],
            device_id={"tm": 2 * col + 1 - y}, device_id_type=MESH)

    def left_part(o, part):
        some = pl.ds(part * few, few)
        return pltpu.make_async_remote_copy(
            src_ref=x.at[base + o, some], dst_ref=x.at[base + wide + o, some], send_sem=send_l.at[o],
            recv_sem=recv_r.at[o], device_id={"tm": lax.rem(me + size - 2, size)}, device_id_type=MESH)

    def right_part(o, part):
        some = pl.ds(part * few, few)
        return pltpu.make_async_remote_copy(
            src_ref=x.at[base + o, some], dst_ref=x.at[base - wide + o, some], send_sem=send_r.at[o],
            recv_sem=recv_l.at[o], device_id={"tm": lax.rem(me + 2, size)}, device_id_type=MESH)

    def left_copy(o, src):
        return pltpu.make_async_remote_copy(
            src_ref=src, dst_ref=x.at[base + wide + o], send_sem=send_l.at[o], recv_sem=recv_r.at[o],
            device_id={"tm": lax.rem(me + size - 2, size)}, device_id_type=MESH)

    def right_copy(o, src):
        return pltpu.make_async_remote_copy(
            src_ref=src, dst_ref=x.at[base - wide + o], send_sem=send_r.at[o], recv_sem=recv_l.at[o],
            device_id={"tm": lax.rem(me + 2, size)}, device_id_type=MESH)

    def own_src(o):
        return mine(y, o % frames)

    def got_src(o):
        return x.at[base + o]

    def power_copy(i):
        return pltpu.make_async_remote_copy(
            src_ref=given.at[frames + i], dst_ref=out_ref.at[i], send_sem=send_p.at[i], recv_sem=recv_p.at[i],
            device_id={"tm": lax.rem(me + 2, size)}, device_id_type=MESH)

    def power_keep(i):
        return pltpu.make_async_copy(given.at[i], out_ref.at[i], own_p.at[i])

    def own_copy(j):
        return pltpu.make_async_copy(mine(y, j), x.at[base + y * frames + j], local.at[j])

    rows_copy().start()
    for part in range(2):
        swap_copy(0, part).start()

    @pl.when(to_right & (y == 0))
    def _():
        right_copy(frames - 1, own_src(frames - 1)).start()

    @pl.when(to_right & (y == 1))
    def _():
        for o in range(wide - 1, wide - 3, -1):
            right_copy(o, own_src(o)).start()

    @pl.when(has_left & (y == 0))
    def _():
        for o in range(2):
            left_copy(o, own_src(o)).start()

    @pl.when(has_left & (y == 1))
    def _():
        left_copy(frames, own_src(frames)).start()

    for n in range(1, frames):
        for part in range(2):
            swap_copy(n, part).start()
    for j in range(frames):
        own_copy(j).start()
    keep = pltpu.make_async_copy(rows_ref, table.at[me], local.at[frames])
    keep.start()
    loads = [pltpu.make_async_copy(src, dst, tables_sem.at[n]) for n, (src, dst) in enumerate(zip(far, near))]
    for load in loads:
        load.start()

    def clear(n, carry):
        x[n] = jnp.zeros(x.shape[1:], x.dtype)
        return carry
    lax.fori_loop(0, jnp.where(first_col, base, jnp.where(second_col, base - wide, 0)), clear, 0)

    for load in loads:
        load.wait()
    for a in range(taps.shape[1] // 2):
        piece = taps_ref[:, a * LANES:(a + 1) * LANES]
        taps[:, 2 * a, :] = piece
        taps[:, 2 * a + 1, :] = piece

    for j in range(frames):
        own_copy(j).wait()

    plans = schedule(frames)

    def look(j):
        words = []
        for k in range(2):
            kinds = []
            for kind in plans:
                sides = []
                for rows in kind:
                    word = jnp.int32(0)
                    for step, row in enumerate(rows):
                        if row[k]:
                            word = jnp.where(j == step, row[k], word)
                    sides.append(word)
                kinds.append(jnp.where(y == 0, sides[0], sides[1]))
            words.append(jnp.where(first_col, kinds[0], jnp.where(second_col, kinds[1], jnp.where(mid, kinds[2], 0))))
        ops, waits = words
        ops = [lax.rem(ops // 32 ** n, 32) - 1 for n in (3, 2, 1, 0)]
        waits = [lax.rem(waits // 16 ** n, 16) for n in (3, 2, 1, 0)]
        return ops, waits

    def busy(d):
        stays = d < wide
        near = lax.rem(d, frames) < KEPT
        return (first_col & (stays | near)) | (second_col & jnp.logical_not(stays & near)) | (
            mid & jnp.logical_not(second_col | stays))

    def plan(d):
        owner = lax.rem(d // frames, 2)
        bank = d // wide * frames + lax.rem(d, frames)
        return owner, bank

    def spectra_copy(i, h, p, owner, bank):
        return pltpu.make_async_remote_copy(
            src_ref=z.at[i, h, p], dst_ref=r.at[bank, p, :, :, pl.ds(place * share, share), :],
            send_sem=send_z.at[i, h, p], recv_sem=recv_z.at[i, place, p],
            device_id={"tm": 2 * col + owner, "stn": h}, device_id_type=MESH)

    def spectra_keep(i, h, p, bank):
        return pltpu.make_async_copy(
            z.at[i, h, p], r.at[bank, p, :, :, pl.ds(place * share, share), :], own_z.at[i, p])

    def spectra_wait(i, where, p, bank):
        return pltpu.make_async_remote_copy(
            src_ref=z.at[i, 0, p], dst_ref=r.at[bank, p, :, :, pl.ds(where * share, share), :],
            send_sem=send_z.at[i, 0, p], recv_sem=recv_z.at[i, where, p],
            device_id={"tm": 2 * col + 1 - y}, device_id_type=MESH)

    def pick_weights():
        width = groups * 2 * SB
        entries = table[:, :, pl.ds(pl.multiple_of(core * width, width), width)].reshape(-1, width)
        entries = entries.astype(f32).T.astype(bf16)
        ids = lax.broadcasted_iota(jnp.int32, (entries.shape[1], beams), 0)
        stations = index_ref.shape[0] * SB
        for q in range(index_ref.shape[0]):
            onehot = jnp.where(ids == index_ref[q:q + 1, :], mask_ref[q:q + 1, :], 0).astype(f32).astype(bf16)
            picked = jnp.dot(entries, onehot, preferred_element_type=f32)
            for g in range(groups):
                low = 2 * g * SB
                re = picked[low:low + SB]
                im = picked[low + SB:low + 2 * SB]
                weights[g, q * SB:(q + 1) * SB, :beams] = re.astype(bf16)
                weights[g, q * SB:(q + 1) * SB, beams:] = im.astype(bf16)
                weights[g, stations + q * SB:stations + (q + 1) * SB, :beams] = (-im).astype(bf16)
                weights[g, stations + q * SB:stations + (q + 1) * SB, beams:] = re.astype(bf16)

    def pass_rows(j):
        @pl.when(j == 0)
        def _():
            keep.wait()
            rows_copy().wait_recv()

        @pl.when((j > 0) & (col - j >= 0))
        def _():
            rows_got(j - 1, True).wait_recv()

        @pl.when((j > 0) & (col + j < cols))
        def _():
            rows_got(j - 1, False).wait_recv()

        @pl.when((j < cols - 1) & has_left & (col + j < cols))
        def _():
            rows_left(j).start()

        @pl.when((j < cols - 1) & has_right & (col - j >= 0))
        def _():
            rows_right(j).start()

    def relay(n, part):
        swap_copy(n, part).wait_recv()
        o = swap_got(n)

        @pl.when(to_right & (y == 0))
        def _():
            right_part(o, part).start()

        @pl.when(has_left & (y == 1))
        def _():
            left_part(o, part).start()

    def forward(n):
        @pl.when((n < frames - 2) & has_left & (y == 0))
        def _():
            left_copy(n + 2, mine(y, n + 2)).start()

        @pl.when((n < frames - 2) & to_right & (y == 1))
        def _():
            right_copy(wide - 3 - n, mine(y, frames - 3 - n)).start()


        @pl.when((n == frames - 1) & has_left & (y == 0))
        def _():
            for o in range(frames, frames + KEPT):
                left_copy(o, got_src(o)).start()

            @pl.when(col > 1)
            def _():
                for o in range(frames + KEPT, wide):
                    left_copy(o, got_src(o)).start()

        @pl.when((n == frames - 1) & has_left & (y == 1))
        def _():
            for o in range(frames + 1, frames + KEPT):
                left_copy(o, own_src(o)).start()

            @pl.when(col > 1)
            def _():
                for o in range(frames + KEPT, wide):
                    left_copy(o, own_src(o)).start()

        @pl.when((n == frames - 1) & to_right & (y == 0))
        def _():
            for o in range(frames - 2, 0, -1):
                right_copy(o, own_src(o)).start()

            @pl.when(first_col)
            def _():
                right_copy(0, own_src(0)).start()

        @pl.when((n == frames - 1) & to_right & (y == 1))
        def _():
            for o in range(frames - 1, 0, -1):
                right_copy(o, got_src(o)).start()

            @pl.when(first_col)
            def _():
                right_copy(0, got_src(0)).start()

    def wait_right(o):
        left_copy(o, got_src(0)).wait_recv()

    def wait_left(o):
        right_copy(o, got_src(0)).wait_recv()

    halves = 2

    def channelize(i):
        slot = base + i

        def filter_rows(n, carry):
            quad = n // halves
            rows = pl.ds(pl.multiple_of(lax.rem(n, halves) * 16, 16), 16)
            sums = [None] * (4 * pols)
            for k in range(depth):
                tap = taps[k, rows, :]
                for m in range(4):
                    for p in range(pols):
                        term = tap * x[slot - k, quad * 4 + m, p, rows, :].astype(f32)
                        j = m * pols + p
                        sums[j] = term if k == 0 else sums[j] + term
            for m in range(4):
                for p in range(pols):
                    row = (lax.rem(quad, 2) * 4 + m) * 32 + lax.rem(n, halves) * 16
                    held[quad // 2, pl.ds(pl.multiple_of(row, 16), 16), p * LANES:(p + 1) * LANES] = (
                        sums[m * pols + p].astype(bf16))
            return carry
        lax.fori_loop(0, share // 4 * halves, filter_rows, 0)

        batches = share // 8
        block = FIRST * 8
        whole = batches * block
        for b in range(batches):
            spread = jnp.dot(one_ref[...], held[b], preferred_element_type=f32)
            for lh in range(2):
                cos, sin = cos_ref[lh], sin_ref[lh]
                for p in range(pols):
                    re = spread[2 * lh * block:(2 * lh + 1) * block, p * LANES:(p + 1) * LANES]
                    im = spread[(2 * lh + 1) * block:(2 * lh + 2) * block, p * LANES:(p + 1) * LANES]
                    tw[p * whole + b * block:p * whole + (b + 1) * block, lh * LANES:(lh + 1) * LANES] = (re * cos + im * sin).astype(bf16)
                    tw[p * whole + b * block:p * whole + (b + 1) * block, (2 + lh) * LANES:(3 + lh) * LANES] = (
                        im * cos - re * sin).astype(bf16)
        for h in range(2):
            spectra = jnp.dot(
                tw[...], two_ref[:, h * 2 * LANES:(h + 1) * 2 * LANES], preferred_element_type=f32)
            for p in range(pols):
                for k1 in range(FIRST):
                    low = p * whole + k1 * 8
                    rows = jnp.concatenate(
                        [spectra[low + b * block:low + b * block + 8] for b in range(batches)], axis=0).astype(bf16)
                    for part in range(2):
                        z[i, h, p, k1, part] = rows[:, part * LANES:(part + 1) * LANES]

    def share_out(i):
        owner, bank = plan(i)
        for p in range(pols):
            for h in range(2):
                stay = (owner == y) & (core == h)

                @pl.when(stay)
                def _():
                    spectra_keep(i, h, p, bank).start()

                @pl.when(jnp.logical_not(stay))
                def _():
                    spectra_copy(i, h, p, owner, bank).start()

    def beamform(i):
        _, bank = plan(i)
        stays = i < wide
        at = lax.rem(bank, frames)
        for p in range(pols):
            for where in range(4):
                @pl.when(place == where)
                def _():
                    spectra_keep(i, core, p, bank).wait()

                @pl.when(place != where)
                def _():
                    spectra_wait(i, where, p, bank).wait_recv()

            def turn(k1, carry):
                for part in range(2):
                    tile = r[bank, p, k1, part].T
                    for g in range(groups):
                        turned[p, g, pl.ds(pl.multiple_of(k1 * lows, lows), lows), part * LANES:(part + 1) * LANES] = (
                            tile[g * lows:(g + 1) * lows])
                return carry
            lax.fori_loop(0, FIRST, turn, 0, unroll=2)

            def group(g, carry):
                rows = pl.ds(pl.multiple_of(g * LANES, LANES), LANES)
                beam = jnp.dot(turned[p, g], weights[g], preferred_element_type=f32)
                power = beam[:, :beams] * beam[:, :beams] + beam[:, beams:] * beam[:, beams:]
                if p:
                    power = part_power[rows, :] + power
                if p < pols - 1:
                    part_power[rows, :] = power
                else:
                    given[bank, rows, :] = power.astype(bf16)
                return carry
            lax.fori_loop(0, groups, group, 0, unroll=2)

        @pl.when(stays)
        def _():
            power_keep(at).start()

        @pl.when(jnp.logical_not(stays))
        def _():
            power_copy(at).start()

    def round_(j, carry):
        (made, sent, also, late), (right_from, right_to, left_from, left_to) = look(j)

        @pl.when(j < frames)
        def _():
            for part in range(2):
                relay(j, part)


        @pl.when(j < cols)
        def _():
            pass_rows(j)

        @pl.when(j < frames)
        def _():
            forward(j)

        @pl.when(j == cols - 1)
        def _():
            pick_weights()

        @pl.when(made >= 0)
        def _():
            def from_right(o, carry):
                wait_right(o)
                return carry
            lax.fori_loop(right_from, right_to, from_right, 0)

            def from_left(n, carry):
                wait_left(wide - 1 - n)
                return carry
            lax.fori_loop(left_from, left_to, from_left, 0)
            channelize(made)

        @pl.when(sent >= 0)
        def _():
            share_out(sent)

        @pl.when(also >= 0)
        def _():
            share_out(also)

        @pl.when(late >= 0)
        def _():
            beamform(late)
        return carry
    lax.fori_loop(0, ROUNDS, round_, 0)

    for n in range(frames):
        @pl.when(has_left & ((col > 1) | (n < KEPT)))
        def _():
            power_copy(n).wait_recv()

        @pl.when(first_col | (second_col & (n >= KEPT)))
        def _():
            power_keep(n).wait()

    rows_copy().wait_send()
    for k in range(cols - 1):
        @pl.when(has_left & (col + k < cols))
        def _():
            rows_left(k).wait_send()

        @pl.when(has_right & (col - k >= 0))
        def _():
            rows_right(k).wait_send()
    for n in range(frames):
        for part in range(2):
            swap_copy(n, part).wait_send()

    @pl.when(has_left)
    def _():
        for o in range(frames + KEPT):
            left_copy(o, got_src(0)).wait_send()

        @pl.when(col > 1)
        def _():
            for o in range(frames + KEPT, wide):
                left_copy(o, got_src(0)).wait_send()

    @pl.when(to_right)
    def _():
        for o in range(1, wide):
            right_copy(o, got_src(0)).wait_send()

        @pl.when(first_col)
        def _():
            right_copy(0, got_src(0)).wait_send()

    for n in range(frames):
        @pl.when(mid | (first_col & (n < KEPT)))
        def _():
            power_copy(n).wait_send()

    def drain(i, carry):
        @pl.when(busy(i))
        def _():
            owner, bank = plan(i)
            for h in range(2):
                @pl.when(jnp.logical_not((owner == y) & (core == h)))
                def _():
                    for p in range(pols):
                        spectra_copy(i, h, p, owner, bank).wait_send()
        return carry
    lax.fori_loop(0, 2 * wide, drain, 0)


def fused(v, weight_rows, index, mask, taps, tables, size):
    stations, pols, frames, rows, _ = v.shape
    share = stations // 2
    groups = G // 2
    beams = index.shape[1]
    depth, channels = taps.shape
    wide = 2 * frames
    bf16 = jnp.bfloat16
    dma = pltpu.SemaphoreType.DMA
    vmem = pl.BlockSpec(memory_space=pltpu.VMEM)
    hbm = pl.BlockSpec(memory_space=pl.ANY)
    return pl.pallas_call(
        functools.partial(kernel, size),
        out_shape=jax.ShapeDtypeStruct((frames, channels // 2, beams), bf16),
        in_specs=[hbm] + [vmem] * 3 + [hbm] * 5,
        out_specs=hbm,
        scratch_shapes=[pltpu.VMEM(a.shape, a.dtype) for a in (taps, *tables)] + [
            dma((5,)),
            pltpu.VMEM((depth - 1 + 2 * wide, share, pols, rows, LANES), bf16),
            pltpu.VMEM((depth, rows, LANES), jnp.float32),
            pltpu.VMEM((share // 8, 8 * rows, pols * LANES), bf16),
            pltpu.VMEM((pols * FIRST * share, 4 * LANES), bf16),
            pltpu.VMEM((2 * wide, 2, pols, FIRST, 2, share, LANES), bf16),
            pltpu.VMEM((wide, pols, FIRST, 2, 4 * share, LANES), bf16),
            pltpu.VMEM((size,) + weight_rows.shape, bf16),
            pltpu.VMEM((groups, 8 * share, 2 * beams), bf16),
            pltpu.VMEM((pols, groups, LANES, 2 * LANES), bf16),
            pltpu.VMEM((channels // 2, beams), jnp.float32),
            pltpu.VMEM((wide, channels // 2, beams), bf16),
            dma((frames + 1,)), dma((1,)), dma((1,)), dma((size // 2,)), dma((size // 2,)), dma((size // 2,)), dma((size // 2,)),
            dma((frames, 2)), dma((frames, 2)),
            dma((wide,)), dma((wide,)), dma((wide,)), dma((wide,)),
            dma((2 * wide, 2, pols)), dma((2 * wide, 4, pols)), dma((2 * wide, pols)), dma((frames,)), dma((frames,)), dma((frames,)),
        ],
        compiler_params=pltpu.CompilerParams(collective_id=0, has_side_effects=True, vmem_limit_bytes=60 << 20),
        name="fused_beams",
    )(v, weight_rows, index, mask, taps, *tables)


def spread_kernel(power_ref, out_ref):
    frames, rows, beams = power_ref.shape
    lows = LANES // (G // 2)
    pieces = beams // LANES
    pitch = pieces * frames
    for part in range(rows // LANES):
        for k1 in range(FIRST):
            low = part * LANES + k1 * lows
            tiles = [power_ref[f, low:low + lows, :].astype(jnp.float32) for f in range(frames)]
            for half in range(lows // 8):
                block = jnp.stack(
                    [tiles[f][half * 8:(half + 1) * 8, piece * LANES:(piece + 1) * LANES]
                     for piece in range(pieces) for f in range(frames)], axis=0)
                block = jnp.swapaxes(block, 0, 1)
                for m in range(8):
                    row = (part * LANES + (half * 8 + m) * FIRST + k1) * pitch
                    out_ref[row:row + pitch, :] = block[m]


def spread(power):
    frames, rows, beams = power.shape
    step = rows // 2
    high = step * frames * beams // LANES
    return pl.pallas_call(
        spread_kernel,
        grid=(rows // step,),
        out_shape=jax.ShapeDtypeStruct((rows * frames * beams // LANES, LANES), jnp.float32),
        in_specs=[pl.BlockSpec((frames, step, beams), lambda n: (0, n, 0))],
        out_specs=pl.BlockSpec((high, LANES), lambda n: (n, 0)),
        compiler_params=pltpu.CompilerParams(vmem_limit_bytes=32 << 20),
        name="spread_power",
    )(power)


def body(voltages, filter_taps, use_mask, block_index, weight_blocks):
    stations, pols, frames, _, channels = voltages.shape
    size = lax.axis_size("tm")
    v = voltages.reshape(stations, pols, frames, 2, channels // LANES, LANES).swapaxes(-3, -2)
    v = v.reshape(stations, pols, frames, 2 * channels // LANES, LANES)
    beams = block_index.shape[0]
    power = fused(v, weight_blocks, block_index.T, use_mask.T, filter_taps, transform_tables(channels), size)
    power = spread(power).reshape(channels // 2, beams // LANES, frames, LANES)
    return power.swapaxes(1, 2).reshape(channels // 2, frames, beams)


def solution(mesh):
    in_specs = (
        P(("parts", "stn"), None, "tm", None, None),
        P(),
        P("parts", None),
        P("parts", None),
        P("tm", None),
    )
    out_specs = P("stn", "tm", "parts")
    return jax.shard_map(body, mesh=mesh, in_specs=in_specs, out_specs=out_specs, check_vma=False)
```

```python
import functools
import math

import jax
import jax.numpy as jnp
import numpy as np
from jax import lax
from jax.experimental import pallas as pl
from jax.experimental.pallas import tpu as pltpu
from jax.sharding import PartitionSpec as P

SB = 16
G = 16
LANES = 128
FIRST = 8
KEPT = 3
ROUNDS = 17
MESH = pl.DeviceIdType.MESH


def transform_tables(channels):
    second = channels // FIRST
    parts = second // LANES
    a = np.arange(FIRST)
    l = np.arange(second)

    def waves(product, period):
        angle = (product % period).astype(np.float32) * np.float32(2.0 * math.pi / period)
        return np.cos(angle), np.sin(angle)

    cos, sin = waves(a[:, None] * a[None, :], FIRST)
    one = np.zeros((parts, 2, FIRST, 8, 8, FIRST, parts, 2), np.float32)
    for lh in range(parts):
        for s in range(8):
            one[lh, 0, :, s, s, :, lh, 0] = cos
            one[lh, 0, :, s, s, :, lh, 1] = sin
            one[lh, 1, :, s, s, :, lh, 0] = -sin
            one[lh, 1, :, s, s, :, lh, 1] = cos
    one = one.reshape(parts * 2 * FIRST * 8, 8 * FIRST * parts * 2)
    cos, sin = waves(l[:, None] * l[None, :], second)
    two = np.stack([np.stack([cos, -sin], axis=1), np.stack([sin, cos], axis=1)], axis=0)
    two = two.reshape(2, second, 2, 2, LANES).transpose(0, 1, 3, 2, 4).reshape(2 * second, 2 * second)
    cos, sin = waves(a[:, None] * l[None, :], channels)
    norm = np.float32(1.0 / math.sqrt(channels))
    cos, sin = (
        np.repeat((w * norm).reshape(FIRST, parts, LANES).swapaxes(0, 1), 8, axis=1) for w in (cos, sin))
    return jnp.asarray(one, jnp.bfloat16), jnp.asarray(two, jnp.bfloat16), jnp.asarray(cos), jnp.asarray(sin)


def schedule(frames):
    wide = 2 * frames

    def orders(filters, early, beams, right, left):
        rows = []
        had = [0, 0]
        for j in range(ROUNDS):
            here = [d for k, d in filters if k == j]
            need = list(had)
            for d in here:
                need = [max(need[0], right(d)), max(need[1], left(d))]
            sent = [d for k, d in early if k == j]
            done = [d for k, d in beams if k == j]
            word = 0
            for d in (here + [-1])[:1] + (sent + [-1, -1])[:2] + (done + [-1])[:1]:
                word = word * 32 + d + 1
            rows.append((word, ((had[0] * 16 + need[0]) * 16 + had[1]) * 16 + need[1]))
            had = need
        return rows

    def right(d):
        return max(d - wide + 1, 0)

    def left(most):
        return lambda d: min(max(2 * wide - 1 - d, 0), most)

    def placed(first, order):
        return [(first + k, d) for k, d in enumerate(order)]

    upper_head = placed(0, [4, 5, 6, 7, 0, 8, 12, 9, 13, 10, 1, 14, 2, 3])
    lower_head = placed(0, [0, 1, 2, 3, 8, 9, 12, 10, 13, 4, 5, 14, 6, 7])
    upper_sent = [(0, 4), (1, 5)] + placed(4, [0, 8, 12, 9, 13, 10, 1, 14, 2, 3]) + [(11, 6), (12, 7)]
    lower_sent = [(0, 0)] + placed(4, [8, 9, 12, 10, 13, 4, 5, 14, 6, 7]) + placed(8, [1, 2, 3])
    upper_done = [(7, 0), (9, 8), (11, 9), (13, 10), (14, 1), (15, 2), (16, 3)]
    lower_done = [(10, 4), (11, 12), (12, 13), (13, 5), (14, 14), (15, 6), (16, 7)]
    upper_shift = [12, 11, 10, 13, 9, 14, 8, 15]
    lower_shift = [11, 12, 10, 13, 9, 8, 14, 15]
    upper_both, lower_both = placed(4, upper_shift + [7, 3]), placed(4, lower_shift + [3, 7])
    upper_only, lower_only = placed(4, upper_shift), placed(4, lower_shift)
    zero = lambda d: 0
    upper = [(7, 11), (9, 10), (11, 9), (13, 8)]
    lower = [(7, 12), (9, 13), (11, 14), (13, 15)]
    return [
        [orders(upper_head, upper_sent, upper_done, right, zero),
         orders(lower_head, lower_sent, lower_done, right, zero)],
        [orders(upper_both, upper_both, upper + [(14, 3)], right, left(wide)),
         orders(lower_both, lower_both, lower + [(14, 7)], right, left(wide))],
        [orders(upper_only, upper_only, upper, right, left(wide - 1)),
         orders(lower_only, lower_only, lower, right, left(wide - 1))],
    ]


def kernel(size, v_ref, rows_ref, index_ref, mask_ref, *refs):
    far, (out_ref, taps_ref, one_ref, two_ref, cos_ref, sin_ref, tables_sem) = refs[:5], refs[5:12]
    near = (taps_ref, one_ref, two_ref, cos_ref, sin_ref)
    (x, taps, held, tw, z, r, table, weights, turned, part_power, given,
           local, send_w, recv_w, send_wl, recv_wl, send_wr, recv_wr, send_y, recv_y, send_l, recv_l, send_r, recv_r, send_z, recv_z, own_z, send_p, recv_p, own_p) = refs[12:]
    me = lax.axis_index("tm")
    core = lax.axis_index("stn")
    col = me // 2
    y = lax.rem(me, 2)
    cols = size // 2
    frames = v_ref.shape[2]
    wide = 2 * frames
    depth = taps_ref.shape[0]
    base = depth - 1
    pols = v_ref.shape[1]
    share = v_ref.shape[0] // 2
    few = share // 2
    groups, _, beams2 = weights.shape
    beams = beams2 // 2
    lows = LANES // groups
    bf16 = jnp.bfloat16
    f32 = jnp.float32
    place = 2 * core + y

    first_col = col == 0
    second_col = col == 1
    mid = (col > 0) & (col < cols - 1)
    has_left = col > 0
    has_right = col < cols - 1
    to_right = col < cols - 2

    barrier = pltpu.get_barrier_semaphore()

    def greet(**where):
        pl.semaphore_signal(barrier, inc=1, device_id=where, device_id_type=MESH)

    greet(stn=1 - core)
    for side in range(2):
        greet(tm=2 * col + 1 - y, stn=side)

    @pl.when(has_left)
    def _():
        greet(tm=me - 2)

    @pl.when(has_right)
    def _():
        greet(tm=me + 2)
    pl.semaphore_wait(barrier, 3 + has_left.astype(jnp.int32) + has_right.astype(jnp.int32))

    width = groups * 2 * SB
    own_rows = rows_ref.at[:, pl.ds(pl.multiple_of(core * width, width), width)]

    def rows_copy():
        return pltpu.make_async_remote_copy(
            src_ref=own_rows, dst_ref=table.at[me], send_sem=send_w.at[0], recv_sem=recv_w.at[0],
            device_id={"tm": 2 * col + 1 - y}, device_id_type=MESH)

    def rows_left(k):
        block = table.at[pl.ds(2 * (col + k), 2)]
        return pltpu.make_async_remote_copy(
            src_ref=block, dst_ref=block, send_sem=send_wl.at[k], recv_sem=recv_wl.at[k],
            device_id={"tm": lax.rem(me + size - 2, size)}, device_id_type=MESH)

    def rows_right(k):
        block = table.at[pl.ds(2 * (col - k), 2)]
        return pltpu.make_async_remote_copy(
            src_ref=block, dst_ref=block, send_sem=send_wr.at[k], recv_sem=recv_wr.at[k],
            device_id={"tm": lax.rem(me + 2, size)}, device_id_type=MESH)

    def rows_got(k, from_left):
        block = table.at[pl.ds(2 * (col - 1 - k if from_left else col + 1 + k), 2)]
        return pltpu.make_async_remote_copy(
            src_ref=block, dst_ref=block, send_sem=(send_wr if from_left else send_wl).at[k],
            recv_sem=(recv_wr if from_left else recv_wl).at[k], device_id={"tm": 2 * col + 1 - y}, device_id_type=MESH)

    def mine(half, j):
        return v_ref.at[pl.ds(half * share, share), :, j]

    def swap_sent(n):
        return y * frames + n

    def swap_got(n):
        return (1 - y) * frames + n

    def swap_copy(n, part):
        o = swap_sent(n)
        return pltpu.make_async_remote_copy(
            src_ref=v_ref.at[pl.ds((1 - y) * share + part * few, few), :, lax.rem(o, frames)],
            dst_ref=x.at[base + o, pl.ds(part * few, few)], send_sem=send_y.at[n, part], recv_sem=recv_y.at[n, part],
            device_id={"tm": 2 * col + 1 - y}, device_id_type=MESH)

    def left_part(o, part):
        some = pl.ds(part * few, few)
        return pltpu.make_async_remote_copy(
            src_ref=x.at[base + o, some], dst_ref=x.at[base + wide + o, some], send_sem=send_l.at[o],
            recv_sem=recv_r.at[o], device_id={"tm": lax.rem(me + size - 2, size)}, device_id_type=MESH)

    def right_part(o, part):
        some = pl.ds(part * few, few)
        return pltpu.make_async_remote_copy(
            src_ref=x.at[base + o, some], dst_ref=x.at[base - wide + o, some], send_sem=send_r.at[o],
            recv_sem=recv_l.at[o], device_id={"tm": lax.rem(me + 2, size)}, device_id_type=MESH)

    def left_copy(o, src):
        return pltpu.make_async_remote_copy(
            src_ref=src, dst_ref=x.at[base + wide + o], send_sem=send_l.at[o], recv_sem=recv_r.at[o],
            device_id={"tm": lax.rem(me + size - 2, size)}, device_id_type=MESH)

    def right_copy(o, src):
        return pltpu.make_async_remote_copy(
            src_ref=src, dst_ref=x.at[base - wide + o], send_sem=send_r.at[o], recv_sem=recv_l.at[o],
            device_id={"tm": lax.rem(me + 2, size)}, device_id_type=MESH)

    def own_src(o):
        return mine(y, o % frames)

    def got_src(o):
        return x.at[base + o]

    def power_copy(i):
        return pltpu.make_async_remote_copy(
            src_ref=given.at[frames + i], dst_ref=out_ref.at[i], send_sem=send_p.at[i], recv_sem=recv_p.at[i],
            device_id={"tm": lax.rem(me + 2, size)}, device_id_type=MESH)

    def power_keep(i):
        return pltpu.make_async_copy(given.at[i], out_ref.at[i], own_p.at[i])

    def own_copy(j):
        return pltpu.make_async_copy(mine(y, j), x.at[base + y * frames + j], local.at[j])

    rows_copy().start()
    for part in range(2):
        swap_copy(0, part).start()

    @pl.when(to_right & (y == 0))
    def _():
        right_copy(frames - 1, own_src(frames - 1)).start()

    @pl.when(to_right & (y == 1))
    def _():
        for o in range(wide - 1, wide - 3, -1):
            right_copy(o, own_src(o)).start()

    @pl.when(has_left & (y == 0))
    def _():
        for o in range(2):
            left_copy(o, own_src(o)).start()

    @pl.when(has_left & (y == 1))
    def _():
        left_copy(frames, own_src(frames)).start()

    for n in range(1, frames):
        for part in range(2):
            swap_copy(n, part).start()
    for j in range(frames):
        own_copy(j).start()
    keep = pltpu.make_async_copy(own_rows, table.at[me], local.at[frames])
    keep.start()
    loads = [pltpu.make_async_copy(src, dst, tables_sem.at[n]) for n, (src, dst) in enumerate(zip(far, near))]
    for load in loads:
        load.start()

    def clear(n, carry):
        x[n] = jnp.zeros(x.shape[1:], x.dtype)
        return carry
    lax.fori_loop(0, jnp.where(first_col, base, jnp.where(second_col, base - wide, 0)), clear, 0)

    for load in loads:
        load.wait()
    for a in range(taps.shape[1] // 2):
        piece = taps_ref[:, a * LANES:(a + 1) * LANES]
        taps[:, 2 * a, :] = piece
        taps[:, 2 * a + 1, :] = piece

    for j in range(frames):
        own_copy(j).wait()

    plans = schedule(frames)

    def look(j):
        words = []
        for k in range(2):
            kinds = []
            for kind in plans:
                sides = []
                for rows in kind:
                    word = jnp.int32(0)
                    for step, row in enumerate(rows):
                        if row[k]:
                            word = jnp.where(j == step, row[k], word)
                    sides.append(word)
                kinds.append(jnp.where(y == 0, sides[0], sides[1]))
            words.append(jnp.where(first_col, kinds[0], jnp.where(second_col, kinds[1], jnp.where(mid, kinds[2], 0))))
        ops, waits = words
        ops = [lax.rem(ops // 32 ** n, 32) - 1 for n in (3, 2, 1, 0)]
        waits = [lax.rem(waits // 16 ** n, 16) for n in (3, 2, 1, 0)]
        return ops, waits

    def busy(d):
        stays = d < wide
        near = lax.rem(d, frames) < KEPT
        return (first_col & (stays | near)) | (second_col & jnp.logical_not(stays & near)) | (
            mid & jnp.logical_not(second_col | stays))

    def plan(d):
        owner = lax.rem(d // frames, 2)
        bank = d // wide * frames + lax.rem(d, frames)
        return owner, bank

    def spectra_copy(i, h, p, owner, bank):
        return pltpu.make_async_remote_copy(
            src_ref=z.at[i, h, p], dst_ref=r.at[bank, p, :, :, pl.ds(place * share, share), :],
            send_sem=send_z.at[i, h, p], recv_sem=recv_z.at[i, place, p],
            device_id={"tm": 2 * col + owner, "stn": h}, device_id_type=MESH)

    def spectra_keep(i, h, p, bank):
        return pltpu.make_async_copy(
            z.at[i, h, p], r.at[bank, p, :, :, pl.ds(place * share, share), :], own_z.at[i, p])

    def spectra_wait(i, where, p, bank):
        return pltpu.make_async_remote_copy(
            src_ref=z.at[i, 0, p], dst_ref=r.at[bank, p, :, :, pl.ds(where * share, share), :],
            send_sem=send_z.at[i, 0, p], recv_sem=recv_z.at[i, where, p],
            device_id={"tm": 2 * col + 1 - y}, device_id_type=MESH)

    def pick_weights():
        entries = table[...].reshape(-1, width)
        entries = entries.astype(f32).T.astype(bf16)
        ids = lax.broadcasted_iota(jnp.int32, (entries.shape[1], beams), 0)
        stations = index_ref.shape[0] * SB
        for q in range(index_ref.shape[0]):
            onehot = jnp.where(ids == index_ref[q:q + 1, :], mask_ref[q:q + 1, :], 0).astype(f32).astype(bf16)
            picked = jnp.dot(entries, onehot, preferred_element_type=f32)
            for g in range(groups):
                low = 2 * g * SB
                re = picked[low:low + SB]
                im = picked[low + SB:low + 2 * SB]
                weights[g, q * SB:(q + 1) * SB, :beams] = re.astype(bf16)
                weights[g, q * SB:(q + 1) * SB, beams:] = im.astype(bf16)
                weights[g, stations + q * SB:stations + (q + 1) * SB, :beams] = (-im).astype(bf16)
                weights[g, stations + q * SB:stations + (q + 1) * SB, beams:] = re.astype(bf16)

    def pass_rows(j):
        @pl.when(j == 0)
        def _():
            keep.wait()
            rows_copy().wait_recv()

        @pl.when((j > 0) & (col - j >= 0))
        def _():
            rows_got(j - 1, True).wait_recv()

        @pl.when((j > 0) & (col + j < cols))
        def _():
            rows_got(j - 1, False).wait_recv()

        @pl.when((j < cols - 1) & has_left & (col + j < cols))
        def _():
            rows_left(j).start()

        @pl.when((j < cols - 1) & has_right & (col - j >= 0))
        def _():
            rows_right(j).start()

    def relay(n, part):
        swap_copy(n, part).wait_recv()
        o = swap_got(n)

        @pl.when(to_right & (y == 0))
        def _():
            right_part(o, part).start()

        @pl.when(has_left & (y == 1))
        def _():
            left_part(o, part).start()

    def forward(n):
        @pl.when((n < frames - 2) & has_left & (y == 0))
        def _():
            left_copy(n + 2, mine(y, n + 2)).start()

        @pl.when((n < frames - 2) & to_right & (y == 1))
        def _():
            right_copy(wide - 3 - n, mine(y, frames - 3 - n)).start()


        @pl.when((n == frames - 1) & has_left & (y == 0))
        def _():
            for o in range(frames, frames + KEPT):
                left_copy(o, got_src(o)).start()

            @pl.when(col > 1)
            def _():
                for o in range(frames + KEPT, wide):
                    left_copy(o, got_src(o)).start()

        @pl.when((n == frames - 1) & has_left & (y == 1))
        def _():
            for o in range(frames + 1, frames + KEPT):
                left_copy(o, own_src(o)).start()

            @pl.when(col > 1)
            def _():
                for o in range(frames + KEPT, wide):
                    left_copy(o, own_src(o)).start()

        @pl.when((n == frames - 1) & to_right & (y == 0))
        def _():
            for o in range(frames - 2, 0, -1):
                right_copy(o, own_src(o)).start()

            @pl.when(first_col)
            def _():
                right_copy(0, own_src(0)).start()

        @pl.when((n == frames - 1) & to_right & (y == 1))
        def _():
            for o in range(frames - 1, 0, -1):
                right_copy(o, got_src(o)).start()

            @pl.when(first_col)
            def _():
                right_copy(0, got_src(0)).start()

    def wait_right(o):
        left_copy(o, got_src(0)).wait_recv()

    def wait_left(o):
        right_copy(o, got_src(0)).wait_recv()

    halves = 2

    def channelize(i):
        slot = base + i

        def filter_rows(n, carry):
            quad = n // halves
            rows = pl.ds(pl.multiple_of(lax.rem(n, halves) * 16, 16), 16)
            sums = [None] * (4 * pols)
            for k in range(depth):
                tap = taps[k, rows, :]
                for m in range(4):
                    for p in range(pols):
                        term = tap * x[slot - k, quad * 4 + m, p, rows, :].astype(f32)
                        j = m * pols + p
                        sums[j] = term if k == 0 else sums[j] + term
            for m in range(4):
                for p in range(pols):
                    row = (lax.rem(quad, 2) * 4 + m) * 32 + lax.rem(n, halves) * 16
                    held[quad // 2, pl.ds(pl.multiple_of(row, 16), 16), p * LANES:(p + 1) * LANES] = (
                        sums[m * pols + p].astype(bf16))
            return carry
        lax.fori_loop(0, share // 4 * halves, filter_rows, 0)

        batches = share // 8
        block = FIRST * 8
        whole = batches * block
        for b in range(batches):
            spread = jnp.dot(one_ref[...], held[b], preferred_element_type=f32)
            for lh in range(2):
                cos, sin = cos_ref[lh], sin_ref[lh]
                for p in range(pols):
                    re = spread[2 * lh * block:(2 * lh + 1) * block, p * LANES:(p + 1) * LANES]
                    im = spread[(2 * lh + 1) * block:(2 * lh + 2) * block, p * LANES:(p + 1) * LANES]
                    tw[p * whole + b * block:p * whole + (b + 1) * block, lh * LANES:(lh + 1) * LANES] = (re * cos + im * sin).astype(bf16)
                    tw[p * whole + b * block:p * whole + (b + 1) * block, (2 + lh) * LANES:(3 + lh) * LANES] = (
                        im * cos - re * sin).astype(bf16)
        for h in range(2):
            spectra = jnp.dot(
                tw[...], two_ref[:, h * 2 * LANES:(h + 1) * 2 * LANES], preferred_element_type=f32)
            for p in range(pols):
                for k1 in range(FIRST):
                    low = p * whole + k1 * 8
                    rows = jnp.concatenate(
                        [spectra[low + b * block:low + b * block + 8] for b in range(batches)], axis=0).astype(bf16)
                    for part in range(2):
                        z[i, h, p, k1, part] = rows[:, part * LANES:(part + 1) * LANES]

    def share_out(i):
        owner, bank = plan(i)
        for p in range(pols):
            for h in range(2):
                stay = (owner == y) & (core == h)

                @pl.when(stay)
                def _():
                    spectra_keep(i, h, p, bank).start()

                @pl.when(jnp.logical_not(stay))
                def _():
                    spectra_copy(i, h, p, owner, bank).start()

    def beamform(i):
        _, bank = plan(i)
        stays = i < wide
        at = lax.rem(bank, frames)
        for p in range(pols):
            for where in range(4):
                @pl.when(place == where)
                def _():
                    spectra_keep(i, core, p, bank).wait()

                @pl.when(place != where)
                def _():
                    spectra_wait(i, where, p, bank).wait_recv()

            def turn(k1, carry):
                for part in range(2):
                    tile = r[bank, p, k1, part].T
                    for g in range(groups):
                        turned[p, g, pl.ds(pl.multiple_of(k1 * lows, lows), lows), part * LANES:(part + 1) * LANES] = (
                            tile[g * lows:(g + 1) * lows])
                return carry
            lax.fori_loop(0, FIRST, turn, 0, unroll=2)

            def group(g, carry):
                rows = pl.ds(pl.multiple_of(g * LANES, LANES), LANES)
                beam = jnp.dot(turned[p, g], weights[g], preferred_element_type=f32)
                power = beam[:, :beams] * beam[:, :beams] + beam[:, beams:] * beam[:, beams:]
                if p:
                    power = part_power[rows, :] + power
                if p < pols - 1:
                    part_power[rows, :] = power
                else:
                    given[bank, rows, :] = power.astype(bf16)
                return carry
            lax.fori_loop(0, groups, group, 0, unroll=2)

        @pl.when(stays)
        def _():
            power_keep(at).start()

        @pl.when(jnp.logical_not(stays))
        def _():
            power_copy(at).start()

    def round_(j, carry):
        (made, sent, also, late), (right_from, right_to, left_from, left_to) = look(j)

        @pl.when(j < frames)
        def _():
            for part in range(2):
                relay(j, part)


        @pl.when(j < cols)
        def _():
            pass_rows(j)

        @pl.when(j < frames)
        def _():
            forward(j)

        @pl.when(j == cols - 1)
        def _():
            pick_weights()

        @pl.when(made >= 0)
        def _():
            def from_right(o, carry):
                wait_right(o)
                return carry
            lax.fori_loop(right_from, right_to, from_right, 0)

            def from_left(n, carry):
                wait_left(wide - 1 - n)
                return carry
            lax.fori_loop(left_from, left_to, from_left, 0)
            channelize(made)

        @pl.when(sent >= 0)
        def _():
            share_out(sent)

        @pl.when(also >= 0)
        def _():
            share_out(also)

        @pl.when(late >= 0)
        def _():
            beamform(late)
        return carry
    lax.fori_loop(0, ROUNDS, round_, 0)

    for n in range(frames):
        @pl.when(has_left & ((col > 1) | (n < KEPT)))
        def _():
            power_copy(n).wait_recv()

        @pl.when(first_col | (second_col & (n >= KEPT)))
        def _():
            power_keep(n).wait()

    rows_copy().wait_send()
    for k in range(cols - 1):
        @pl.when(has_left & (col + k < cols))
        def _():
            rows_left(k).wait_send()

        @pl.when(has_right & (col - k >= 0))
        def _():
            rows_right(k).wait_send()
    for n in range(frames):
        for part in range(2):
            swap_copy(n, part).wait_send()

    @pl.when(has_left)
    def _():
        for o in range(frames + KEPT):
            left_copy(o, got_src(0)).wait_send()

        @pl.when(col > 1)
        def _():
            for o in range(frames + KEPT, wide):
                left_copy(o, got_src(0)).wait_send()

    @pl.when(to_right)
    def _():
        for o in range(1, wide):
            right_copy(o, got_src(0)).wait_send()

        @pl.when(first_col)
        def _():
            right_copy(0, got_src(0)).wait_send()

    for n in range(frames):
        @pl.when(mid | (first_col & (n < KEPT)))
        def _():
            power_copy(n).wait_send()

    def drain(i, carry):
        @pl.when(busy(i))
        def _():
            owner, bank = plan(i)
            for h in range(2):
                @pl.when(jnp.logical_not((owner == y) & (core == h)))
                def _():
                    for p in range(pols):
                        spectra_copy(i, h, p, owner, bank).wait_send()
        return carry
    lax.fori_loop(0, 2 * wide, drain, 0)


def fused(v, weight_rows, index, mask, taps, tables, size):
    stations, pols, frames, rows, _ = v.shape
    share = stations // 2
    groups = G // 2
    beams = index.shape[1]
    depth, channels = taps.shape
    wide = 2 * frames
    bf16 = jnp.bfloat16
    dma = pltpu.SemaphoreType.DMA
    vmem = pl.BlockSpec(memory_space=pltpu.VMEM)
    hbm = pl.BlockSpec(memory_space=pl.ANY)
    return pl.pallas_call(
        functools.partial(kernel, size),
        out_shape=jax.ShapeDtypeStruct((frames, channels // 2, beams), bf16),
        in_specs=[hbm] + [vmem] * 3 + [hbm] * 5,
        out_specs=hbm,
        scratch_shapes=[pltpu.VMEM(a.shape, a.dtype) for a in (taps, *tables)] + [
            dma((5,)),
            pltpu.VMEM((depth - 1 + 2 * wide, share, pols, rows, LANES), bf16),
            pltpu.VMEM((depth, rows, LANES), jnp.float32),
            pltpu.VMEM((share // 8, 8 * rows, pols * LANES), bf16),
            pltpu.VMEM((pols * FIRST * share, 4 * LANES), bf16),
            pltpu.VMEM((2 * wide, 2, pols, FIRST, 2, share, LANES), bf16),
            pltpu.VMEM((wide, pols, FIRST, 2, 4 * share, LANES), bf16),
            pltpu.VMEM((size, weight_rows.shape[0], weight_rows.shape[1] // 2), bf16),
            pltpu.VMEM((groups, 8 * share, 2 * beams), bf16),
            pltpu.VMEM((pols, groups, LANES, 2 * LANES), bf16),
            pltpu.VMEM((channels // 2, beams), jnp.float32),
            pltpu.VMEM((wide, channels // 2, beams), bf16),
            dma((frames + 1,)), dma((1,)), dma((1,)), dma((size // 2,)), dma((size // 2,)), dma((size // 2,)), dma((size // 2,)),
            dma((frames, 2)), dma((frames, 2)),
            dma((wide,)), dma((wide,)), dma((wide,)), dma((wide,)),
            dma((2 * wide, 2, pols)), dma((2 * wide, 4, pols)), dma((2 * wide, pols)), dma((frames,)), dma((frames,)), dma((frames,)),
        ],
        compiler_params=pltpu.CompilerParams(collective_id=0, has_side_effects=True, vmem_limit_bytes=60 << 20),
        name="fused_beams",
    )(v, weight_rows, index, mask, taps, *tables)


def spread_kernel(power_ref, out_ref):
    frames, rows, beams = power_ref.shape
    lows = LANES // (G // 2)
    pieces = beams // LANES
    pitch = pieces * frames
    for part in range(rows // LANES):
        for k1 in range(FIRST):
            low = part * LANES + k1 * lows
            tiles = [power_ref[f, low:low + lows, :].astype(jnp.float32) for f in range(frames)]
            for half in range(lows // 8):
                block = jnp.stack(
                    [tiles[f][half * 8:(half + 1) * 8, piece * LANES:(piece + 1) * LANES]
                     for piece in range(pieces) for f in range(frames)], axis=0)
                block = jnp.swapaxes(block, 0, 1)
                for m in range(8):
                    row = (part * LANES + (half * 8 + m) * FIRST + k1) * pitch
                    out_ref[row:row + pitch, :] = block[m]


def spread(power):
    frames, rows, beams = power.shape
    step = rows // 2
    high = step * frames * beams // LANES
    return pl.pallas_call(
        spread_kernel,
        grid=(rows // step,),
        out_shape=jax.ShapeDtypeStruct((rows * frames * beams // LANES, LANES), jnp.float32),
        in_specs=[pl.BlockSpec((frames, step, beams), lambda n: (0, n, 0))],
        out_specs=pl.BlockSpec((high, LANES), lambda n: (n, 0)),
        compiler_params=pltpu.CompilerParams(vmem_limit_bytes=32 << 20),
        name="spread_power",
    )(power)


def body(voltages, filter_taps, use_mask, block_index, weight_blocks):
    stations, pols, frames, _, channels = voltages.shape
    size = lax.axis_size("tm")
    v = voltages.reshape(stations, pols, frames, 2, channels // LANES, LANES).swapaxes(-3, -2)
    v = v.reshape(stations, pols, frames, 2 * channels // LANES, LANES)
    beams = block_index.shape[0]
    power = fused(v, weight_blocks, block_index.T, use_mask.T, filter_taps, transform_tables(channels), size)
    power = spread(power).reshape(channels // 2, beams // LANES, frames, LANES)
    return power.swapaxes(1, 2).reshape(channels // 2, frames, beams)


def solution(mesh):
    in_specs = (
        P(("parts", "stn"), None, "tm", None, None),
        P(),
        P("parts", None),
        P("parts", None),
        P("tm", None),
    )
    out_specs = P("stn", "tm", "parts")
    return jax.shard_map(body, mesh=mesh, in_specs=in_specs, out_specs=out_specs, check_vma=False)
```

```python
import functools
import math

import jax
import jax.numpy as jnp
import numpy as np
from jax import lax
from jax.experimental import pallas as pl
from jax.experimental.pallas import tpu as pltpu
from jax.sharding import PartitionSpec as P

SB = 16
G = 16
LANES = 128
FIRST = 8
KEPT = 3
ROUNDS = 17
MESH = pl.DeviceIdType.MESH


def transform_tables(channels):
    second = channels // FIRST
    parts = second // LANES
    a = np.arange(FIRST)
    l = np.arange(second)

    def waves(product, period):
        angle = (product % period).astype(np.float32) * np.float32(2.0 * math.pi / period)
        return np.cos(angle), np.sin(angle)

    cos, sin = waves(a[:, None] * a[None, :], FIRST)
    one = np.zeros((parts, 2, FIRST, 8, 8, FIRST, parts, 2), np.float32)
    for lh in range(parts):
        for s in range(8):
            one[lh, 0, :, s, s, :, lh, 0] = cos
            one[lh, 0, :, s, s, :, lh, 1] = sin
            one[lh, 1, :, s, s, :, lh, 0] = -sin
            one[lh, 1, :, s, s, :, lh, 1] = cos
    one = one.reshape(parts * 2 * FIRST * 8, 8 * FIRST * parts * 2)
    cos, sin = waves(l[:, None] * l[None, :], second)
    two = np.stack([np.stack([cos, -sin], axis=1), np.stack([sin, cos], axis=1)], axis=0)
    two = two.reshape(2, second, 2, 2, LANES).transpose(0, 1, 3, 2, 4).reshape(2 * second, 2 * second)
    cos, sin = waves(a[:, None] * l[None, :], channels)
    norm = np.float32(1.0 / math.sqrt(channels))
    cos, sin = (
        np.repeat((w * norm).reshape(FIRST, parts, LANES).swapaxes(0, 1), 8, axis=1) for w in (cos, sin))
    return jnp.asarray(one, jnp.bfloat16), jnp.asarray(two, jnp.bfloat16), jnp.asarray(cos), jnp.asarray(sin)


def schedule(frames):
    wide = 2 * frames

    def orders(filters, early, beams, right, left):
        rows = []
        had = [0, 0]
        for j in range(ROUNDS):
            here = [d for k, d in filters if k == j]
            need = list(had)
            for d in here:
                need = [max(need[0], right(d)), max(need[1], left(d))]
            sent = [d for k, d in early if k == j]
            done = [d for k, d in beams if k == j]
            word = 0
            for d in (here + [-1])[:1] + (sent + [-1, -1])[:2] + (done + [-1])[:1]:
                word = word * 32 + d + 1
            rows.append((word, ((had[0] * 16 + need[0]) * 16 + had[1]) * 16 + need[1]))
            had = need
        return rows

    def right(d):
        return max(d - wide + 1, 0)

    def left(most):
        return lambda d: min(max(2 * wide - 1 - d, 0), most)

    def placed(first, order):
        return [(first + k, d) for k, d in enumerate(order)]

    upper_head = placed(0, [4, 5, 6, 7, 0, 8, 12, 9, 13, 10, 1, 14, 2, 3])
    lower_head = placed(0, [0, 1, 2, 3, 8, 9, 12, 10, 13, 4, 5, 14, 6, 7])
    upper_sent = [(0, 4), (1, 5)] + placed(4, [0, 8, 12, 9, 13, 10, 1, 14, 2, 3]) + [(11, 6), (12, 7)]
    lower_sent = [(0, 0)] + placed(4, [8, 9, 12, 10, 13, 4, 5, 14, 6, 7]) + placed(8, [1, 2, 3])
    upper_done = [(7, 0), (9, 8), (11, 9), (13, 10), (14, 1), (15, 2), (16, 3)]
    lower_done = [(10, 4), (11, 12), (12, 13), (13, 5), (14, 14), (15, 6), (16, 7)]
    upper_shift = [12, 11, 10, 13, 9, 14, 8, 15]
    lower_shift = [11, 12, 10, 13, 9, 8, 14, 15]
    upper_both, lower_both = placed(4, upper_shift + [7, 3]), placed(4, lower_shift + [3, 7])
    upper_only, lower_only = placed(4, upper_shift), placed(4, lower_shift)
    zero = lambda d: 0
    upper = [(7, 11), (9, 10), (11, 9), (13, 8)]
    lower = [(7, 12), (9, 13), (11, 14), (13, 15)]
    return [
        [orders(upper_head, upper_sent, upper_done, right, zero),
         orders(lower_head, lower_sent, lower_done, right, zero)],
        [orders(upper_both, upper_both, upper + [(14, 3)], right, left(wide)),
         orders(lower_both, lower_both, lower + [(14, 7)], right, left(wide))],
        [orders(upper_only, upper_only, upper, right, left(wide - 1)),
         orders(lower_only, lower_only, lower, right, left(wide - 1))],
    ]


def kernel(size, v_ref, rows_ref, index_ref, mask_ref, *refs):
    far, (out_ref, taps_ref, one_ref, two_ref, cos_ref, sin_ref, tables_sem) = refs[:5], refs[5:12]
    near = (taps_ref, one_ref, two_ref, cos_ref, sin_ref)
    (x, taps, held, tw, z, r, table, weights, turned, part_power, given,
           local, send_w, recv_w, send_wl, recv_wl, send_wr, recv_wr, send_y, recv_y, send_l, recv_l, send_r, recv_r, send_z, recv_z, own_z, send_p, recv_p, own_p) = refs[12:]
    me = lax.axis_index("tm")
    core = lax.axis_index("stn")
    col = me // 2
    y = lax.rem(me, 2)
    cols = size // 2
    frames = v_ref.shape[2]
    wide = 2 * frames
    depth = taps_ref.shape[0]
    base = depth - 1
    pols = v_ref.shape[1]
    share = v_ref.shape[0] // 2
    few = share // 2
    groups, _, beams2 = weights.shape
    beams = beams2 // 2
    lows = LANES // groups
    bf16 = jnp.bfloat16
    f32 = jnp.float32
    place = 2 * core + y

    first_col = col == 0
    second_col = col == 1
    mid = (col > 0) & (col < cols - 1)
    has_left = col > 0
    has_right = col < cols - 1
    to_right = col < cols - 2

    barrier = pltpu.get_barrier_semaphore()

    def greet(**where):
        pl.semaphore_signal(barrier, inc=1, device_id=where, device_id_type=MESH)

    greet(stn=1 - core)
    for side in range(2):
        greet(tm=2 * col + 1 - y, stn=side)

    @pl.when(has_left)
    def _():
        greet(tm=me - 2)

    @pl.when(has_right)
    def _():
        greet(tm=me + 2)
    pl.semaphore_wait(barrier, 3 + has_left.astype(jnp.int32) + has_right.astype(jnp.int32))

    width = groups * 2 * SB
    own_rows = rows_ref.at[:, pl.ds(pl.multiple_of(core * width, width), width)]

    def rows_copy():
        return pltpu.make_async_remote_copy(
            src_ref=own_rows, dst_ref=table.at[me], send_sem=send_w.at[0], recv_sem=recv_w.at[0],
            device_id={"tm": 2 * col + 1 - y}, device_id_type=MESH)

    def rows_left(k):
        block = table.at[pl.ds(2 * (col + k), 2)]
        return pltpu.make_async_remote_copy(
            src_ref=block, dst_ref=block, send_sem=send_wl.at[k], recv_sem=recv_wl.at[k],
            device_id={"tm": lax.rem(me + size - 2, size)}, device_id_type=MESH)

    def rows_right(k):
        block = table.at[pl.ds(2 * (col - k), 2)]
        return pltpu.make_async_remote_copy(
            src_ref=block, dst_ref=block, send_sem=send_wr.at[k], recv_sem=recv_wr.at[k],
            device_id={"tm": lax.rem(me + 2, size)}, device_id_type=MESH)

    def rows_got(k, from_left):
        block = table.at[pl.ds(2 * (col - 1 - k if from_left else col + 1 + k), 2)]
        return pltpu.make_async_remote_copy(
            src_ref=block, dst_ref=block, send_sem=(send_wr if from_left else send_wl).at[k],
            recv_sem=(recv_wr if from_left else recv_wl).at[k], device_id={"tm": 2 * col + 1 - y}, device_id_type=MESH)

    def mine(half, j):
        return v_ref.at[pl.ds(half * share, share), :, j]

    def swap_sent(n):
        return y * frames + n

    def swap_got(n):
        return (1 - y) * frames + n

    def swap_copy(n, part):
        o = swap_sent(n)
        return pltpu.make_async_remote_copy(
            src_ref=v_ref.at[pl.ds((1 - y) * share + part * few, few), :, lax.rem(o, frames)],
            dst_ref=x.at[base + o, pl.ds(part * few, few)], send_sem=send_y.at[n, part], recv_sem=recv_y.at[n, part],
            device_id={"tm": 2 * col + 1 - y}, device_id_type=MESH)

    def left_part(o, part):
        some = pl.ds(part * few, few)
        return pltpu.make_async_remote_copy(
            src_ref=x.at[base + o, some], dst_ref=x.at[base + wide + o, some], send_sem=send_l.at[o],
            recv_sem=recv_r.at[o], device_id={"tm": lax.rem(me + size - 2, size)}, device_id_type=MESH)

    def right_part(o, part):
        some = pl.ds(part * few, few)
        return pltpu.make_async_remote_copy(
            src_ref=x.at[base + o, some], dst_ref=x.at[base - wide + o, some], send_sem=send_r.at[o],
            recv_sem=recv_l.at[o], device_id={"tm": lax.rem(me + 2, size)}, device_id_type=MESH)

    def left_copy(o, src):
        return pltpu.make_async_remote_copy(
            src_ref=src, dst_ref=x.at[base + wide + o], send_sem=send_l.at[o], recv_sem=recv_r.at[o],
            device_id={"tm": lax.rem(me + size - 2, size)}, device_id_type=MESH)

    def right_copy(o, src):
        return pltpu.make_async_remote_copy(
            src_ref=src, dst_ref=x.at[base - wide + o], send_sem=send_r.at[o], recv_sem=recv_l.at[o],
            device_id={"tm": lax.rem(me + 2, size)}, device_id_type=MESH)

    def own_src(o):
        return mine(y, o % frames)

    def got_src(o):
        return x.at[base + o]

    def power_copy(i):
        return pltpu.make_async_remote_copy(
            src_ref=given.at[frames + i], dst_ref=out_ref.at[i], send_sem=send_p.at[i], recv_sem=recv_p.at[i],
            device_id={"tm": lax.rem(me + 2, size)}, device_id_type=MESH)

    def power_keep(i):
        return pltpu.make_async_copy(given.at[i], out_ref.at[i], own_p.at[i])

    def own_copy(j):
        return pltpu.make_async_copy(mine(y, j), x.at[base + y * frames + j], local.at[j])

    rows_copy().start()
    for part in range(2):
        swap_copy(0, part).start()

    @pl.when(to_right & (y == 0))
    def _():
        right_copy(frames - 1, own_src(frames - 1)).start()

    @pl.when(to_right & (y == 1))
    def _():
        for o in range(wide - 1, wide - 3, -1):
            right_copy(o, own_src(o)).start()

    @pl.when(has_left & (y == 0))
    def _():
        for o in range(2):
            left_copy(o, own_src(o)).start()

    @pl.when(has_left & (y == 1))
    def _():
        left_copy(frames, own_src(frames)).start()

    for n in range(1, frames):
        for part in range(2):
            swap_copy(n, part).start()
    for j in range(frames):
        own_copy(j).start()
    keep = pltpu.make_async_copy(own_rows, table.at[me], local.at[frames])
    keep.start()
    loads = [pltpu.make_async_copy(src, dst, tables_sem.at[n]) for n, (src, dst) in enumerate(zip(far, near))]
    for load in loads:
        load.start()

    def clear(n, carry):
        x[n] = jnp.zeros(x.shape[1:], x.dtype)
        return carry
    lax.fori_loop(0, jnp.where(first_col, base, jnp.where(second_col, base - wide, 0)), clear, 0)

    for load in loads:
        load.wait()
    for a in range(taps.shape[1] // 2):
        piece = taps_ref[:, a * LANES:(a + 1) * LANES]
        taps[:, 2 * a, :] = piece
        taps[:, 2 * a + 1, :] = piece

    for j in range(frames):
        own_copy(j).wait()

    plans = schedule(frames)

    def look(j):
        words = []
        for k in range(2):
            kinds = []
            for kind in plans:
                sides = []
                for rows in kind:
                    word = jnp.int32(0)
                    for step, row in enumerate(rows):
                        if row[k]:
                            word = jnp.where(j == step, row[k], word)
                    sides.append(word)
                kinds.append(jnp.where(y == 0, sides[0], sides[1]))
            words.append(jnp.where(first_col, kinds[0], jnp.where(second_col, kinds[1], jnp.where(mid, kinds[2], 0))))
        ops, waits = words
        ops = [lax.rem(ops // 32 ** n, 32) - 1 for n in (3, 2, 1, 0)]
        waits = [lax.rem(waits // 16 ** n, 16) for n in (3, 2, 1, 0)]
        return ops, waits

    def busy(d):
        stays = d < wide
        near = lax.rem(d, frames) < KEPT
        return (first_col & (stays | near)) | (second_col & jnp.logical_not(stays & near)) | (
            mid & jnp.logical_not(second_col | stays))

    def plan(d):
        owner = lax.rem(d // frames, 2)
        bank = d // wide * frames + lax.rem(d, frames)
        return owner, bank

    def spectra_copy(i, h, p, owner, bank):
        return pltpu.make_async_remote_copy(
            src_ref=z.at[i, h, p], dst_ref=r.at[bank, p, :, :, pl.ds(place * share, share), :],
            send_sem=send_z.at[i, h, p], recv_sem=recv_z.at[i, place, p],
            device_id={"tm": 2 * col + owner, "stn": h}, device_id_type=MESH)

    def spectra_keep(i, h, p, bank):
        return pltpu.make_async_copy(
            z.at[i, h, p], r.at[bank, p, :, :, pl.ds(place * share, share), :], own_z.at[i, p])

    def spectra_wait(i, where, p, bank):
        return pltpu.make_async_remote_copy(
            src_ref=z.at[i, 0, p], dst_ref=r.at[bank, p, :, :, pl.ds(where * share, share), :],
            send_sem=send_z.at[i, 0, p], recv_sem=recv_z.at[i, where, p],
            device_id={"tm": 2 * col + 1 - y}, device_id_type=MESH)

    def pick_weights():
        entries = table[...].reshape(-1, width)
        entries = entries.astype(f32).T.astype(bf16)
        ids = lax.broadcasted_iota(jnp.int32, (entries.shape[1], beams), 0)
        stations = index_ref.shape[0] * SB
        for q in range(index_ref.shape[0]):
            onehot = jnp.where(ids == index_ref[q:q + 1, :], mask_ref[q:q + 1, :], 0).astype(f32).astype(bf16)
            picked = jnp.dot(entries, onehot, preferred_element_type=f32)
            for g in range(groups):
                low = 2 * g * SB
                re = picked[low:low + SB]
                im = picked[low + SB:low + 2 * SB]
                weights[g, q * SB:(q + 1) * SB, :beams] = re.astype(bf16)
                weights[g, q * SB:(q + 1) * SB, beams:] = im.astype(bf16)
                weights[g, stations + q * SB:stations + (q + 1) * SB, :beams] = (-im).astype(bf16)
                weights[g, stations + q * SB:stations + (q + 1) * SB, beams:] = re.astype(bf16)

    def pass_rows(j):
        @pl.when(j == 0)
        def _():
            keep.wait()
            rows_copy().wait_recv()

        @pl.when((j > 0) & (col - j >= 0))
        def _():
            rows_got(j - 1, True).wait_recv()

        @pl.when((j > 0) & (col + j < cols))
        def _():
            rows_got(j - 1, False).wait_recv()

        @pl.when((j < cols - 1) & has_left & (col + j < cols))
        def _():
            rows_left(j).start()

        @pl.when((j < cols - 1) & has_right & (col - j >= 0))
        def _():
            rows_right(j).start()

    def relay(n, part):
        swap_copy(n, part).wait_recv()
        o = swap_got(n)

        @pl.when(to_right & (y == 0))
        def _():
            right_part(o, part).start()

        @pl.when(has_left & (y == 1))
        def _():
            left_part(o, part).start()

    def forward(n):
        @pl.when((n < frames - 2) & has_left & (y == 0))
        def _():
            left_copy(n + 2, mine(y, n + 2)).start()

        @pl.when((n < frames - 2) & to_right & (y == 1))
        def _():
            right_copy(wide - 3 - n, mine(y, frames - 3 - n)).start()


        @pl.when((n == frames - 1) & has_left & (y == 0))
        def _():
            for o in range(frames, frames + KEPT):
                left_copy(o, got_src(o)).start()

            @pl.when(col > 1)
            def _():
                for o in range(frames + KEPT, wide):
                    left_copy(o, got_src(o)).start()

        @pl.when((n == frames - 1) & has_left & (y == 1))
        def _():
            for o in range(frames + 1, frames + KEPT):
                left_copy(o, own_src(o)).start()

            @pl.when(col > 1)
            def _():
                for o in range(frames + KEPT, wide):
                    left_copy(o, own_src(o)).start()

        @pl.when((n == frames - 1) & to_right & (y == 0))
        def _():
            for o in range(frames - 2, 0, -1):
                right_copy(o, own_src(o)).start()

            @pl.when(first_col)
            def _():
                right_copy(0, own_src(0)).start()

        @pl.when((n == frames - 1) & to_right & (y == 1))
        def _():
            for o in range(frames - 1, 0, -1):
                right_copy(o, got_src(o)).start()

            @pl.when(first_col)
            def _():
                right_copy(0, got_src(0)).start()

    def wait_right(o):
        left_copy(o, got_src(0)).wait_recv()

    def wait_left(o):
        right_copy(o, got_src(0)).wait_recv()

    halves = 2

    def channelize(i):
        slot = base + i

        def filter_rows(n, carry):
            quad = n // halves
            rows = pl.ds(pl.multiple_of(lax.rem(n, halves) * 16, 16), 16)
            sums = [None] * (4 * pols)
            for k in range(depth):
                tap = taps[k, rows, :]
                for m in range(4):
                    for p in range(pols):
                        term = tap * x[slot - k, quad * 4 + m, p, rows, :].astype(f32)
                        j = m * pols + p
                        sums[j] = term if k == 0 else sums[j] + term
            for m in range(4):
                for p in range(pols):
                    row = (lax.rem(quad, 2) * 4 + m) * 32 + lax.rem(n, halves) * 16
                    held[quad // 2, pl.ds(pl.multiple_of(row, 16), 16), p * LANES:(p + 1) * LANES] = (
                        sums[m * pols + p].astype(bf16))
            return carry
        lax.fori_loop(0, share // 4 * halves, filter_rows, 0)

        batches = share // 8
        block = FIRST * 8
        whole = batches * block
        for b in range(batches):
            spread = jnp.dot(one_ref[...], held[b], preferred_element_type=f32)
            for lh in range(2):
                cos, sin = cos_ref[lh], sin_ref[lh]
                for p in range(pols):
                    re = spread[2 * lh * block:(2 * lh + 1) * block, p * LANES:(p + 1) * LANES]
                    im = spread[(2 * lh + 1) * block:(2 * lh + 2) * block, p * LANES:(p + 1) * LANES]
                    tw[p * whole + b * block:p * whole + (b + 1) * block, lh * LANES:(lh + 1) * LANES] = (re * cos + im * sin).astype(bf16)
                    tw[p * whole + b * block:p * whole + (b + 1) * block, (2 + lh) * LANES:(3 + lh) * LANES] = (
                        im * cos - re * sin).astype(bf16)
        for h in range(2):
            spectra = jnp.dot(
                tw[...], two_ref[:, h * 2 * LANES:(h + 1) * 2 * LANES], preferred_element_type=f32)
            for p in range(pols):
                for k1 in range(FIRST):
                    low = p * whole + k1 * 8
                    rows = jnp.concatenate(
                        [spectra[low + b * block:low + b * block + 8] for b in range(batches)], axis=0).astype(bf16)
                    for part in range(2):
                        z[i, h, p, k1, part] = rows[:, part * LANES:(part + 1) * LANES]

    def share_out(i):
        owner, bank = plan(i)
        for p in range(pols):
            for h in range(2):
                stay = (owner == y) & (core == h)

                @pl.when(stay)
                def _():
                    spectra_keep(i, h, p, bank).start()

                @pl.when(jnp.logical_not(stay))
                def _():
                    spectra_copy(i, h, p, owner, bank).start()

    def beamform(i):
        _, bank = plan(i)
        stays = i < wide
        at = lax.rem(bank, frames)
        for p in range(pols):
            for where in range(4):
                @pl.when(place == where)
                def _():
                    spectra_keep(i, core, p, bank).wait()

                @pl.when(place != where)
                def _():
                    spectra_wait(i, where, p, bank).wait_recv()

            def turn(k1, carry):
                for part in range(2):
                    tile = r[bank, p, k1, part].T
                    for g in range(groups):
                        turned[p, g, pl.ds(pl.multiple_of(k1 * lows, lows), lows), part * LANES:(part + 1) * LANES] = (
                            tile[g * lows:(g + 1) * lows])
                return carry
            lax.fori_loop(0, FIRST, turn, 0, unroll=4)

            def group(g, carry):
                rows = pl.ds(pl.multiple_of(g * LANES, LANES), LANES)
                beam = jnp.dot(turned[p, g], weights[g], preferred_element_type=f32)
                power = beam[:, :beams] * beam[:, :beams] + beam[:, beams:] * beam[:, beams:]
                if p:
                    power = part_power[rows, :] + power
                if p < pols - 1:
                    part_power[rows, :] = power
                else:
                    given[bank, rows, :] = power.astype(bf16)
                return carry
            lax.fori_loop(0, groups, group, 0, unroll=4)

        @pl.when(stays)
        def _():
            power_keep(at).start()

        @pl.when(jnp.logical_not(stays))
        def _():
            power_copy(at).start()

    def round_(j, carry):
        (made, sent, also, late), (right_from, right_to, left_from, left_to) = look(j)

        @pl.when(j < frames)
        def _():
            for part in range(2):
                relay(j, part)


        @pl.when(j < cols)
        def _():
            pass_rows(j)

        @pl.when(j < frames)
        def _():
            forward(j)

        @pl.when(j == cols - 1)
        def _():
            pick_weights()

        @pl.when(made >= 0)
        def _():
            def from_right(o, carry):
                wait_right(o)
                return carry
            lax.fori_loop(right_from, right_to, from_right, 0)

            def from_left(n, carry):
                wait_left(wide - 1 - n)
                return carry
            lax.fori_loop(left_from, left_to, from_left, 0)
            channelize(made)

        @pl.when(sent >= 0)
        def _():
            share_out(sent)

        @pl.when(also >= 0)
        def _():
            share_out(also)

        @pl.when(late >= 0)
        def _():
            beamform(late)
        return carry
    lax.fori_loop(0, ROUNDS, round_, 0)

    for n in range(frames):
        @pl.when(has_left & ((col > 1) | (n < KEPT)))
        def _():
            power_copy(n).wait_recv()

        @pl.when(first_col | (second_col & (n >= KEPT)))
        def _():
            power_keep(n).wait()

    rows_copy().wait_send()
    for k in range(cols - 1):
        @pl.when(has_left & (col + k < cols))
        def _():
            rows_left(k).wait_send()

        @pl.when(has_right & (col - k >= 0))
        def _():
            rows_right(k).wait_send()
    for n in range(frames):
        for part in range(2):
            swap_copy(n, part).wait_send()

    @pl.when(has_left)
    def _():
        for o in range(frames + KEPT):
            left_copy(o, got_src(0)).wait_send()

        @pl.when(col > 1)
        def _():
            for o in range(frames + KEPT, wide):
                left_copy(o, got_src(0)).wait_send()

    @pl.when(to_right)
    def _():
        for o in range(1, wide):
            right_copy(o, got_src(0)).wait_send()

        @pl.when(first_col)
        def _():
            right_copy(0, got_src(0)).wait_send()

    for n in range(frames):
        @pl.when(mid | (first_col & (n < KEPT)))
        def _():
            power_copy(n).wait_send()

    def drain(i, carry):
        @pl.when(busy(i))
        def _():
            owner, bank = plan(i)
            for h in range(2):
                @pl.when(jnp.logical_not((owner == y) & (core == h)))
                def _():
                    for p in range(pols):
                        spectra_copy(i, h, p, owner, bank).wait_send()
        return carry
    lax.fori_loop(0, 2 * wide, drain, 0)


def fused(v, weight_rows, index, mask, taps, tables, size):
    stations, pols, frames, rows, _ = v.shape
    share = stations // 2
    groups = G // 2
    beams = index.shape[1]
    depth, channels = taps.shape
    wide = 2 * frames
    bf16 = jnp.bfloat16
    dma = pltpu.SemaphoreType.DMA
    vmem = pl.BlockSpec(memory_space=pltpu.VMEM)
    hbm = pl.BlockSpec(memory_space=pl.ANY)
    return pl.pallas_call(
        functools.partial(kernel, size),
        out_shape=jax.ShapeDtypeStruct((frames, channels // 2, beams), bf16),
        in_specs=[hbm] + [vmem] * 3 + [hbm] * 5,
        out_specs=hbm,
        scratch_shapes=[pltpu.VMEM(a.shape, a.dtype) for a in (taps, *tables)] + [
            dma((5,)),
            pltpu.VMEM((depth - 1 + 2 * wide, share, pols, rows, LANES), bf16),
            pltpu.VMEM((depth, rows, LANES), jnp.float32),
            pltpu.VMEM((share // 8, 8 * rows, pols * LANES), bf16),
            pltpu.VMEM((pols * FIRST * share, 4 * LANES), bf16),
            pltpu.VMEM((2 * wide, 2, pols, FIRST, 2, share, LANES), bf16),
            pltpu.VMEM((wide, pols, FIRST, 2, 4 * share, LANES), bf16),
            pltpu.VMEM((size, weight_rows.shape[0], weight_rows.shape[1] // 2), bf16),
            pltpu.VMEM((groups, 8 * share, 2 * beams), bf16),
            pltpu.VMEM((pols, groups, LANES, 2 * LANES), bf16),
            pltpu.VMEM((channels // 2, beams), jnp.float32),
            pltpu.VMEM((wide, channels // 2, beams), bf16),
            dma((frames + 1,)), dma((1,)), dma((1,)), dma((size // 2,)), dma((size // 2,)), dma((size // 2,)), dma((size // 2,)),
            dma((frames, 2)), dma((frames, 2)),
            dma((wide,)), dma((wide,)), dma((wide,)), dma((wide,)),
            dma((2 * wide, 2, pols)), dma((2 * wide, 4, pols)), dma((2 * wide, pols)), dma((frames,)), dma((frames,)), dma((frames,)),
        ],
        compiler_params=pltpu.CompilerParams(collective_id=0, has_side_effects=True, vmem_limit_bytes=60 << 20),
        name="fused_beams",
    )(v, weight_rows, index, mask, taps, *tables)


def spread_kernel(power_ref, out_ref):
    frames, rows, beams = power_ref.shape
    lows = LANES // (G // 2)
    pieces = beams // LANES
    pitch = pieces * frames
    for part in range(rows // LANES):
        for k1 in range(FIRST):
            low = part * LANES + k1 * lows
            tiles = [power_ref[f, low:low + lows, :].astype(jnp.float32) for f in range(frames)]
            for half in range(lows // 8):
                block = jnp.stack(
                    [tiles[f][half * 8:(half + 1) * 8, piece * LANES:(piece + 1) * LANES]
                     for piece in range(pieces) for f in range(frames)], axis=0)
                block = jnp.swapaxes(block, 0, 1)
                for m in range(8):
                    row = (part * LANES + (half * 8 + m) * FIRST + k1) * pitch
                    out_ref[row:row + pitch, :] = block[m]


def spread(power):
    frames, rows, beams = power.shape
    step = rows // 2
    high = step * frames * beams // LANES
    return pl.pallas_call(
        spread_kernel,
        grid=(rows // step,),
        out_shape=jax.ShapeDtypeStruct((rows * frames * beams // LANES, LANES), jnp.float32),
        in_specs=[pl.BlockSpec((frames, step, beams), lambda n: (0, n, 0))],
        out_specs=pl.BlockSpec((high, LANES), lambda n: (n, 0)),
        compiler_params=pltpu.CompilerParams(vmem_limit_bytes=32 << 20),
        name="spread_power",
    )(power)


def body(voltages, filter_taps, use_mask, block_index, weight_blocks):
    stations, pols, frames, _, channels = voltages.shape
    size = lax.axis_size("tm")
    v = voltages.reshape(stations, pols, frames, 2, channels // LANES, LANES).swapaxes(-3, -2)
    v = v.reshape(stations, pols, frames, 2 * channels // LANES, LANES)
    beams = block_index.shape[0]
    power = fused(v, weight_blocks, block_index.T, use_mask.T, filter_taps, transform_tables(channels), size)
    power = spread(power).reshape(channels // 2, beams // LANES, frames, LANES)
    return power.swapaxes(1, 2).reshape(channels // 2, frames, beams)


def solution(mesh):
    in_specs = (
        P(("parts", "stn"), None, "tm", None, None),
        P(),
        P("parts", None),
        P("parts", None),
        P("tm", None),
    )
    out_specs = P("stn", "tm", "parts")
    return jax.shard_map(body, mesh=mesh, in_specs=in_specs, out_specs=out_specs, check_vma=False)
```
